512 devices in a mesh: ctx: 32 (over z, y_lo), exp: 8 (over x, core), dp: 2 (over y_hi).
Axes of the slice: x: 4, y: 4 (y_hi: 2, y_lo: 2; y = y_hi * 2 + y_lo), z: 16, core: 2. Of those that a mesh axis runs over, the one named last changes fastest.
Arguments:
- hidden_in: bfloat16 [2, 32768, 1024], P('dp', ('ctx', 'exp')), may hold values from -6 to 6
- queries: bfloat16 [2, 32768, 1024], P('dp', ('ctx', 'exp')), may hold values from -6 to 6
- keys: bfloat16 [2, 32768, 1024], P('dp', ('ctx', 'exp')), may hold values from -6 to 6
- values: bfloat16 [2, 32768, 1024], P('dp', ('ctx', 'exp')), may hold values from -6 to 6
- log_decay: float32 [2, 32768, 8], P('dp', ('ctx', 'exp')), may hold values from -1 to 0
- retention_gain: float32 [1024], replicated, may hold values from 0.25 to 1.75
- norm_gain: float32 [1024], replicated, may hold values from 0.25 to 1.75
- routes: int32 [2, 32768, 2], P('dp', ('ctx', 'exp')), may hold values from 0 to 63, all different within a row; in each aligned block of 128 rows (0 to 127, 128 to 255, ..., all dimensions but the last counted through in order) at most 5 rows name the same one
- route_weights: float32 [2, 32768, 2], P('dp', ('ctx', 'exp')), may hold values from 0.1 to 1
- w_gate: bfloat16 [64, 1024, 1408], P(('ctx', 'dp'), 'exp'), may hold values from -0.1875 to 0.1875
- w_up: bfloat16 [64, 1024, 1408], P(('ctx', 'dp'), 'exp'), may hold values from -0.1875 to 0.1875
- w_down: bfloat16 [64, 1024, 1408], P(('ctx', 'dp'), 'exp'), may hold values from -0.15625 to 0.15625
Outputs:
- output: bfloat16 [2, 32768, 1024], P('dp', ('ctx', 'exp'))
The draws below stay inside these ranges and needn't reach their ends.
Inputs may be any that keep to these rules, and one draw needn't show every extreme that they name: `routes`: in each aligned block of 128 positions (the positions of one device) no expert is named more than 5 times, and a position's 2 experts differ.
All inputs are finite; a program needn't handle non-finite values.
Results may differ from the reference program's by a relative error of at most 0.007.
Values may be sent and summed in bfloat16 or wider, within the bound.
No kernel may reach another device: no remote copies, remote signals or barrier semaphores. Data moves between devices by JAX's collectives and lax.ppermute only.
A program may use at most 128 MiB of HBM per device.

```python
import math
import jax
import jax.numpy as jnp
import numpy as np
from jax import lax

D = 1024
RETENTION_HEADS = 8
HK = 128
FF = 1408
TOP = 2
TOK_DEV = 128
EXPERTS = 64
CAP = 5
SEQUENCE_LENGTH = 32768
SEQUENCE_COUNT = 2


def draw_log_decay(key, part):
    random_subkeys = jax.random.split(key, 7)
    head_order = jax.random.permutation(random_subkeys[0], RETENTION_HEADS)
    quick_heads = jnp.broadcast_to((head_order < RETENTION_HEADS // 2)[None, None, :], (SEQUENCE_COUNT, 1, RETENTION_HEADS))
    slow_rate = jnp.exp(jax.random.uniform(random_subkeys[1], (SEQUENCE_COUNT, 1, RETENTION_HEADS), minval=math.log(0.05), maxval=math.log(0.3))) / SEQUENCE_LENGTH
    fast_rate = jnp.exp(jax.random.uniform(random_subkeys[2], (SEQUENCE_COUNT, 1, RETENTION_HEADS), minval=math.log(0.02), maxval=math.log(0.034)))
    decay_factor = jnp.where(quick_heads, fast_rate, slow_rate)
    block_decay_scale = jnp.exp(jax.random.uniform(random_subkeys[3], (SEQUENCE_COUNT, SEQUENCE_LENGTH // TOK_DEV, 1, RETENTION_HEADS), minval=math.log(0.5), maxval=math.log(2.0)))
    block_decay_scale = jnp.broadcast_to(block_decay_scale, (SEQUENCE_COUNT, SEQUENCE_LENGTH // TOK_DEV, TOK_DEV, RETENTION_HEADS)).reshape(SEQUENCE_COUNT, SEQUENCE_LENGTH, RETENTION_HEADS)
    step_decay_scale = jax.random.uniform(random_subkeys[4], (SEQUENCE_COUNT, SEQUENCE_LENGTH, RETENTION_HEADS), minval=0.5, maxval=1.5)
    spike_locations = jax.random.randint(random_subkeys[5], (SEQUENCE_COUNT, 2), 0, SEQUENCE_LENGTH)
    spike_penalty = jax.random.uniform(random_subkeys[6], (SEQUENCE_COUNT, 2, RETENTION_HEADS), minval=0.5, maxval=0.8)
    token_position = jnp.arange(SEQUENCE_LENGTH, dtype=jnp.int32)
    spike_events = jnp.zeros((SEQUENCE_COUNT, SEQUENCE_LENGTH, RETENTION_HEADS), jnp.float32)
    for spike_index in range(2):
        spike_mask = (spike_locations[:, spike_index][:, None] == token_position[None, :])[:, :, None]
        spike_events = spike_events + jnp.where(spike_mask, jnp.log(spike_penalty[:, spike_index, :])[:, None, :], 0.0)
    return (-decay_factor * block_decay_scale * step_decay_scale + spike_events).astype(jnp.float32)


def shard_levels(own_key, shape, pieces, smallest, top_value):
    factor_of = 1.0
    for dim, shards_of in pieces:
        steps = jax.random.uniform(jax.random.fold_in(jax.random.fold_in(own_key, 6), dim), (shards_of,), jnp.float32, smallest / len(pieces), top_value / len(pieces))
        factor_of = factor_of * jnp.repeat(jnp.exp(steps), shape[dim] // shards_of).reshape((-1,) + (1,) * (len(shape) - 1 - dim))
    return factor_of


def deal_out(rng, own, number, rows, count, top, limit, skew):
    order = jax.random.permutation(rng, count)
    packed, ordinary = portions_of(count, rows * top, limit, skew, True), portions_of(count, rows * top, limit, skew, False)
    places = jnp.arange(count)

    def named(lengths, turn):
        used = int((lengths > 0).sum())
        fixed = max(1, used // 4)
        shifted = fixed + (places - fixed + turn * (used - fixed)) % max(1, count - fixed)
        return jnp.zeros((count,), jnp.int32).at[order[jnp.where(places < fixed, places, shifted)]].set(jnp.asarray(lengths, jnp.int32))

    lengths = jnp.where(number % 4 == 0, named(packed, number // 4), named(ordinary, number - number // 4 - 1))
    mixed = jax.random.permutation(jax.random.fold_in(own, 3), count)
    source_of, sink = mixed[0:count // 2 * 2:2], mixed[1:count // 2 * 2:2]
    margin = jnp.minimum(lengths[source_of] - 1, limit - lengths[sink]) // 2
    margin = jnp.where((source_of == order[0]) | (sink == order[0]) | (lengths[sink] == 0), 0, jnp.maximum(margin, 0))
    shifted = jax.random.randint(jax.random.fold_in(own, 4), (count // 2,), 0, 1 << 20) % (margin + 1)
    lengths = lengths.at[source_of].add(-shifted).at[sink].add(shifted)
    items = jnp.searchsorted(jnp.cumsum(lengths), jnp.arange(rows * top), side="right").astype(jnp.int32)
    grid = items.reshape(top, rows).T
    grid = grid[jax.random.permutation(jax.random.fold_in(own, 1), rows)]
    turn = jax.random.randint(jax.random.fold_in(own, 2), (rows, 1), 0, top)
    return jnp.take_along_axis(grid, (jnp.arange(top)[None, :] + turn) % top, axis=1)


def portions_of(number_of, total, bound, lean, full):
    loads = [(1 << 20) // math.isqrt(standing ** lean) + 1 for standing in range(1, number_of + 1)]
    largest = bound if full else min(bound, max(-(-total // number_of), total * loads[0] // sum(loads)))
    least = 1 if total - largest >= number_of - 1 else 0
    counts, surplus = [largest] + [least] * (number_of - 1), total - largest - least * (number_of - 1)
    while surplus > 0:
        candidates = [i for i in range(1, number_of) if counts[i] < largest] or [i for i in range(1, number_of) if counts[i] < bound]
        mass, left = sum([loads[i] for i in candidates]), surplus
        for i in candidates:
            more = min(bound - counts[i], max(1, left * loads[i] // mass), surplus)
            counts[i] = counts[i] + more
            surplus = surplus - more
    return np.array(counts)


def normal_values(stream_key, dims, scale, reach, cuts=(), held_as=jnp.bfloat16):
    values = jax.random.normal(stream_key, dims, jnp.float32) * scale
    if len(cuts) > 0:
        values = shard_levels(stream_key, dims, cuts, -0.22, 0.18) * values
    return jnp.clip(values, min=-reach, max=reach).astype(held_as)


def setup_inputs(seed: int = 0) -> dict:
    splits = jax.random.split(jax.random.key(seed), 13)
    hidden_in = normal_values(splits[0], (SEQUENCE_COUNT, SEQUENCE_LENGTH, D), 1.0, 6.0, ((0, 2), (1, 256)))
    queries = normal_values(splits[1], (SEQUENCE_COUNT, SEQUENCE_LENGTH, D), 1.0, 6.0, ((0, 2), (1, 256)))
    keys = normal_values(splits[2], (SEQUENCE_COUNT, SEQUENCE_LENGTH, D), 1.0, 6.0, ((0, 2), (1, 256)))
    values = normal_values(splits[3], (SEQUENCE_COUNT, SEQUENCE_LENGTH, D), 1.0, 6.0, ((0, 2), (1, 256)))
    log_decay = draw_log_decay(jax.random.fold_in(splits[12], 71), 0)
    retention_gain = jnp.clip(1.0 + 0.15 * jax.random.normal(splits[5], (D,), jnp.float32), 0.25, 1.75)
    norm_gain = jnp.clip(1.0 + 0.15 * jax.random.normal(splits[6], (D,), jnp.float32), 0.25, 1.75)
    routes_keys = jax.random.split(jax.random.fold_in(splits[7], 1), SEQUENCE_COUNT * SEQUENCE_LENGTH // TOK_DEV)
    routes_turns = jax.random.permutation(jax.random.fold_in(splits[7], 3), SEQUENCE_COUNT * SEQUENCE_LENGTH // TOK_DEV)
    routes = jax.vmap(lambda own, number: deal_out(jax.random.fold_in(splits[7], 2), own, number, TOK_DEV, EXPERTS, TOP, CAP, 2))(routes_keys, routes_turns).reshape((SEQUENCE_COUNT, SEQUENCE_LENGTH, TOP))
    route_weights = jnp.clip(0.1 + 0.9 * jax.random.uniform(splits[8], (SEQUENCE_COUNT, SEQUENCE_LENGTH, TOP), jnp.float32) ** shard_levels(splits[8], (SEQUENCE_COUNT, SEQUENCE_LENGTH, TOP), ((0, 2), (1, 256)), -0.2, 0.2), 0.1, 1.0)
    w_gate = normal_values(splits[9], (EXPERTS, D, FF), D ** -0.5, 0.1875, ((0, 64), (1, 8)))
    w_up = normal_values(splits[10], (EXPERTS, D, FF), D ** -0.5, 0.1875, ((0, 64), (1, 8)))
    w_down = normal_values(splits[11], (EXPERTS, D, FF), FF ** -0.5, 0.15625, ((0, 64), (1, 8)))
    return {"hidden_in": hidden_in, "queries": queries, "keys": keys, "values": values, "log_decay": log_decay, "retention_gain": retention_gain, "norm_gain": norm_gain, "routes": routes, "route_weights": route_weights, "w_gate": w_gate, "w_up": w_up, "w_down": w_down}


def rotate(vectors, token_position):
    half_dim = vectors.shape[-1] // 2
    inverse = 10000.0 ** (-jnp.arange(half_dim, dtype=jnp.float32) / half_dim)
    angles = token_position.astype(jnp.float32)[:, None] * inverse[None, :]
    cosine = jnp.cos(angles)[:, None, :]
    sine_part = jnp.sin(angles)[:, None, :]
    leading = vectors[..., :half_dim]
    trailing = vectors[..., half_dim:]
    return jnp.concatenate([leading * cosine - trailing * sine_part, trailing * cosine + leading * sine_part], axis=-1)

def retain_block(carried_state, members):
    query_blk, key_blk, value_blk, decay_blk, token_position = members
    tok_count = query_blk.shape[0]
    per_head_queries = (rotate(query_blk.astype(jnp.float32).reshape(tok_count, RETENTION_HEADS, HK), token_position) * HK ** (-0.5)).astype(jnp.bfloat16)
    per_head_keys = rotate(key_blk.astype(jnp.float32).reshape(tok_count, RETENTION_HEADS, HK), token_position).astype(jnp.bfloat16)
    per_head_values = value_blk.reshape(tok_count, RETENTION_HEADS, HK)
    running_total = jnp.cumsum(decay_blk, axis=0)
    scores = jnp.einsum('thd,shd->hts', per_head_queries.astype(jnp.float32), per_head_keys.astype(jnp.float32))
    causal = jnp.arange(tok_count)[:, None] >= jnp.arange(tok_count)[None, :]
    spread = running_total.T[:, :, None] - running_total.T[:, None, :]
    weights = jnp.where(causal[None], scores * jnp.exp(jnp.where(causal[None], spread, 0.0)), 0.0).astype(jnp.bfloat16)
    inside = jnp.einsum('hts,shd->thd', weights.astype(jnp.float32), per_head_values.astype(jnp.float32))
    external_part = jnp.exp(running_total)[:, :, None] * jnp.einsum('wjc,jco->wjo', per_head_queries.astype(jnp.float32), carried_state, precision=lax.Precision.HIGHEST)
    trailing_decay = jnp.exp(running_total[-1][None, :] - running_total)
    block_summary = jnp.einsum('qpf,qpy->pfy', per_head_keys.astype(jnp.float32) * trailing_decay[:, :, None], per_head_values.astype(jnp.float32), precision=lax.Precision.HIGHEST)
    carried_next = jnp.exp(running_total[-1])[:, None, None] * carried_state + block_summary
    return (carried_next, (inside + external_part).reshape(tok_count, RETENTION_HEADS * HK))

def retain_sequence(members):
    query_seq, key_seq, value_seq, decay_seq = members
    blocks = SEQUENCE_LENGTH // TOK_DEV
    token_position = jnp.arange(SEQUENCE_LENGTH, dtype=jnp.int32).reshape(blocks, TOK_DEV)

    def shaped(tensor):
        return tensor.reshape((blocks, TOK_DEV) + tensor.shape[1:])
    start_state = jnp.zeros((RETENTION_HEADS, HK, HK), jnp.float32)
    final_state, retrieved = lax.scan(retain_block, start_state, (shaped(query_seq), shaped(key_seq), shaped(value_seq), shaped(decay_seq), token_position))
    return retrieved.reshape(SEQUENCE_LENGTH, RETENTION_HEADS * HK)

def reference(hidden_in, queries, keys, values, log_decay, retention_gain, norm_gain, routes, route_weights, w_gate, w_up, w_down):
    retrieved = lax.map(retain_sequence, (queries, keys, values, log_decay))
    heads_view = retrieved.reshape(SEQUENCE_COUNT, SEQUENCE_LENGTH, RETENTION_HEADS, HK)
    centre = lax.optimization_barrier(jnp.mean(heads_view, axis=-1, keepdims=True))
    deviation = heads_view - centre
    variance = lax.optimization_barrier(jnp.mean(deviation * deviation, axis=-1, keepdims=True))
    normalized = (deviation * lax.rsqrt(variance + 1e-05)).reshape(SEQUENCE_COUNT, SEQUENCE_LENGTH, D)
    residual = hidden_in.astype(jnp.float32) + retention_gain * normalized
    square_mean = lax.optimization_barrier(jnp.mean(residual * residual, axis=-1, keepdims=True))
    normed = (residual * lax.rsqrt(square_mean + 1e-06) * norm_gain).astype(jnp.bfloat16)
    total_rows = SEQUENCE_COUNT * SEQUENCE_LENGTH
    block_total = total_rows // TOK_DEV
    flat_norm = normed.reshape(total_rows, D)
    route_blocks = routes.reshape(block_total, TOK_DEV * TOP)
    weight_blocks = route_weights.reshape(block_total, TOK_DEV * TOP)
    expert_ids = jnp.arange(EXPERTS, dtype=jnp.int32)
    expert_hits = (route_blocks[:, :, None] == expert_ids[None, None, :]).astype(jnp.int32)
    earlier = jnp.cumsum(expert_hits, axis=1) - expert_hits
    slot_rank = lax.optimization_barrier(jnp.sum(earlier * expert_hits, axis=2)).astype(jnp.int32)
    slot_lanes = jnp.arange(block_total, dtype=jnp.int32)[:, None] * CAP + slot_rank
    owners = jnp.arange(block_total, dtype=jnp.int32)[:, None] * TOK_DEV + jnp.arange(TOK_DEV * TOP, dtype=jnp.int32)[None, :] // TOP
    token_table = jnp.full((EXPERTS, block_total * CAP), -1, jnp.int32).at[route_blocks, slot_lanes].set(owners)
    weight_table = jnp.zeros((EXPERTS, block_total * CAP), jnp.float32).at[route_blocks, slot_lanes].set(weight_blocks)

    def apply_expert(accumulated, members):
        token_ids, token_weights, gate_weight, up_weight, down_weight = members
        present = token_ids >= 0
        safe_ids = jnp.maximum(token_ids, 0)
        picked = flat_norm[safe_ids]
        gate_val = jnp.dot(picked, gate_weight, preferred_element_type=jnp.float32)
        up_val = jnp.dot(picked, up_weight, preferred_element_type=jnp.float32)
        hidden = (jax.nn.silu(gate_val) * up_val).astype(jnp.bfloat16)
        expert_out = jnp.dot(hidden, down_weight.T, preferred_element_type=jnp.float32).astype(jnp.bfloat16)
        contribution = jnp.where(present[:, None], expert_out.astype(jnp.float32) * token_weights[:, None], 0.0)
        return (accumulated.at[safe_ids].add(contribution), None)
    start_sum = jnp.zeros((total_rows, D), jnp.float32)
    accumulated, unused = lax.scan(apply_expert, start_sum, (token_table, weight_table, w_gate, w_up, w_down))
    output = residual.reshape(total_rows, D) + accumulated
    return output.astype(jnp.bfloat16).reshape(SEQUENCE_COUNT, SEQUENCE_LENGTH, D)
```

```python
import jax
import jax.numpy as jnp
from jax import lax
from jax.sharding import Mesh, PartitionSpec as P

CTX = ("z", "ylo")
EXP = ("x", "core")
OWNERS = ("z", "ylo", "yhi")


def exchange(blocks, axes):
    return lax.all_to_all(blocks, axes, split_axis=0, concat_axis=0, tiled=True)


def rotate(vectors, token_position):
    half_dim = vectors.shape[-1] // 2
    inverse = 10000.0 ** (-jnp.arange(half_dim, dtype=jnp.float32) / half_dim)
    angles = token_position.astype(jnp.float32)[:, None] * inverse[None, :]
    cosine = jnp.cos(angles)[:, None, :]
    sine_part = jnp.sin(angles)[:, None, :]
    leading = vectors[..., :half_dim]
    trailing = vectors[..., half_dim:]
    return jnp.concatenate(
        [leading * cosine - trailing * sine_part, trailing * cosine + leading * sine_part], axis=-1
    )


def entering_state(block_summary, block_log):
    member_count = lax.axis_size(EXP)
    ctx_count = lax.axis_size(CTX)
    own_head = lax.axis_index(EXP)
    own_ctx = lax.axis_index(CTX)
    all_logs = lax.all_gather(block_log, CTX + EXP, axis=0).reshape(ctx_count, member_count, -1)
    head_logs = lax.dynamic_index_in_dim(all_logs, own_head, 2, keepdims=False)
    group_logs = jnp.sum(head_logs, axis=1)
    own_logs = lax.dynamic_index_in_dim(head_logs, own_ctx, 0, keepdims=False)
    members = jnp.arange(member_count)
    ctxs = jnp.arange(ctx_count)

    summaries = exchange(block_summary.astype(jnp.bfloat16), EXP).astype(jnp.float32)
    after = jnp.exp(jnp.sum(jnp.where(members[None, :] > members[:, None], own_logs[None, :], 0.0), 1))
    group_sum = jnp.sum(after[:, None, None] * summaries, axis=0)
    group_sums = lax.all_gather(group_sum.astype(jnp.bfloat16), CTX, axis=0).astype(jnp.float32)
    between = (ctxs[None, :] > ctxs[:, None]) & (ctxs[None, :] < own_ctx)
    reach = jnp.exp(jnp.sum(jnp.where(between, group_logs[None, :], 0.0), 1))
    reach = jnp.where(ctxs < own_ctx, reach, 0.0)
    leading = jnp.sum(reach[:, None, None] * group_sums, axis=0)

    to_block = jnp.exp(jnp.sum(jnp.where(members[None, :] < members[:, None], own_logs[None, :], 0.0), 1))
    inner = (members[None, None, :] > members[None, :, None]) & (
        members[None, None, :] < members[:, None, None]
    )
    inner = jnp.exp(jnp.sum(jnp.where(inner, own_logs[None, None, :], 0.0), 2))
    inner = jnp.where(members[None, :] < members[:, None], inner, 0.0)
    entering = to_block[:, None, None] * leading[None] + jnp.sum(
        inner[:, :, None, None] * summaries[None], axis=1
    )
    return exchange(entering.astype(jnp.bfloat16), EXP)


def body(
    hidden_in,
    queries,
    keys,
    values,
    log_decay,
    retention_gain,
    norm_gain,
    routes,
    route_weights,
    w_gate,
    w_up,
    w_down,
):
    tok_rows = hidden_in.shape[1]
    model_width = hidden_in.shape[2]
    head_count = log_decay.shape[2]
    head_dim = model_width // head_count
    block_index = lax.axis_index(CTX) * lax.axis_size(EXP) + lax.axis_index(EXP)
    token_position = block_index * tok_rows + jnp.arange(tok_rows, dtype=jnp.int32)
    per_head_keys = rotate(
        keys[0].astype(jnp.float32).reshape(tok_rows, head_count, head_dim), token_position
    ).astype(jnp.bfloat16)
    per_head_values = values[0].reshape(tok_rows, head_count, head_dim)
    running_total = jnp.cumsum(log_decay[0], axis=0)
    trailing_decay = jnp.exp(running_total[-1][None, :] - running_total)
    block_summary = jnp.einsum(
        "qpf,qpy->pfy",
        (per_head_keys.astype(jnp.float32) * trailing_decay[:, :, None]),
        per_head_values.astype(jnp.float32),
        precision=lax.Precision.HIGHEST,
    )
    state_in = entering_state(block_summary, running_total[-1])

    per_head_queries = (
        rotate(
            queries[0].astype(jnp.float32).reshape(tok_rows, head_count, head_dim), token_position
        )
        * head_dim ** (-0.5)
    ).astype(jnp.bfloat16)
    scores = jnp.einsum(
        "thd,shd->hts", per_head_queries, per_head_keys, preferred_element_type=jnp.float32
    )
    causal = jnp.arange(tok_rows)[:, None] >= jnp.arange(tok_rows)[None, :]
    spread = running_total.T[:, :, None] - running_total.T[:, None, :]
    weights = jnp.where(
        causal[None], scores * jnp.exp(jnp.where(causal[None], spread, 0.0)), 0.0
    ).astype(jnp.bfloat16)
    inside = jnp.einsum(
        "hts,shd->thd", weights, per_head_values, preferred_element_type=jnp.float32
    )
    external_part = jnp.exp(running_total)[:, :, None] * jnp.einsum(
        "wjc,jco->wjo", per_head_queries, state_in, preferred_element_type=jnp.float32
    )
    retrieved = inside + external_part
    centre = jnp.mean(retrieved, axis=-1, keepdims=True)
    deviation = retrieved - centre
    variance = jnp.mean(deviation * deviation, axis=-1, keepdims=True)
    normalized = (deviation * lax.rsqrt(variance + 1e-05)).reshape(tok_rows, model_width)
    residual = hidden_in[0].astype(jnp.float32) + retention_gain * normalized
    square_mean = jnp.mean(residual * residual, axis=-1, keepdims=True)
    normed = (residual * lax.rsqrt(square_mean + 1e-06) * norm_gain).astype(jnp.bfloat16)

    expert_count = lax.axis_size(OWNERS)
    top_count = routes.shape[2]
    capacity = (tok_rows * top_count * 5 + 4 * expert_count - 1) // (4 * expert_count)
    slot_count = expert_count * capacity
    route_rows = routes[0]
    expert_hits = (
        route_rows.reshape(tok_rows * top_count)[:, None]
        == jnp.arange(expert_count, dtype=jnp.int32)[None, :]
    ).astype(jnp.int32)
    earlier = jnp.cumsum(expert_hits, axis=0) - expert_hits
    slot_rank = jnp.sum(earlier * expert_hits, axis=1).reshape(tok_rows, top_count)
    destination = route_rows * capacity + slot_rank
    slot_lanes = jnp.arange(slot_count, dtype=jnp.int32)
    placing = jnp.any(destination[None, :, :] == slot_lanes[:, None, None], axis=2).astype(
        jnp.bfloat16
    )
    outgoing = jnp.dot(placing, normed, preferred_element_type=jnp.float32).astype(jnp.bfloat16)
    lanes = 128
    packed = (expert_count, capacity * model_width // lanes, lanes)
    arrived = exchange(outgoing.reshape(packed), OWNERS).reshape(slot_count, model_width)
    gate_full = lax.all_gather(w_gate[0], EXP, axis=0, tiled=True)
    up_full = lax.all_gather(w_up[0], EXP, axis=0, tiled=True)
    down_full = lax.all_gather(w_down[0], EXP, axis=0, tiled=True)
    gate_next = jnp.dot(arrived, gate_full, preferred_element_type=jnp.float32)
    up_next = jnp.dot(arrived, up_full, preferred_element_type=jnp.float32)
    hidden = (jax.nn.silu(gate_next) * up_next).astype(jnp.bfloat16)
    expert_out = lax.dot_general(
        hidden, down_full, (((1,), (1,)), ((), ())), preferred_element_type=jnp.float32
    ).astype(jnp.bfloat16)
    returned = exchange(expert_out.reshape(packed), OWNERS).reshape(slot_count, model_width)
    output = residual
    for route_index in range(top_count):
        picking = (destination[:, route_index][:, None] == slot_lanes[None, :]).astype(jnp.bfloat16)
        routed = jnp.dot(picking, returned, preferred_element_type=jnp.float32)
        output = output + route_weights[0][:, route_index][:, None] * routed
    return output.astype(jnp.bfloat16)[None]


def solution(mesh):
    ctx, exp, dp = mesh.shape["ctx"], mesh.shape["exp"], mesh.shape["dp"]
    split = Mesh(
        mesh.devices.reshape(ctx // 2, 2, exp // 2, 2, dp), ("z", "ylo", "x", "core", "yhi")
    )
    tokens = P("yhi", CTX + EXP, None)
    experts = P(OWNERS, EXP, None)
    in_specs = (tokens,) * 5 + (P(), P()) + (tokens,) * 2 + (experts,) * 3
    return jax.shard_map(body, mesh=split, in_specs=in_specs, out_specs=tokens, check_vma=False)
```

```python
import jax
import jax.numpy as jnp
from jax import lax
from jax.sharding import Mesh, PartitionSpec as P

CTX = ("z", "ylo")
EXP = ("x", "core")
PLANE = ("ylo", "x", "core")
OWNERS = ("z", "ylo", "yhi")


def exchange(blocks, axes):
    return lax.all_to_all(blocks, axes, split_axis=0, concat_axis=0, tiled=True)


def rotate(vectors, token_position):
    half_dim = vectors.shape[-1] // 2
    inverse = 10000.0 ** (-jnp.arange(half_dim, dtype=jnp.float32) / half_dim)
    angles = token_position.astype(jnp.float32)[:, None] * inverse[None, :]
    cosine = jnp.cos(angles)[:, None, :]
    sine_part = jnp.sin(angles)[:, None, :]
    leading = vectors[..., :half_dim]
    trailing = vectors[..., half_dim:]
    return jnp.concatenate(
        [leading * cosine - trailing * sine_part, trailing * cosine + leading * sine_part], axis=-1
    )


def split_log(value):
    high = lax.reduce_precision(value, 8, 7)
    rest = value - high
    middle = lax.reduce_precision(rest, 8, 7)
    low = rest - middle
    return jnp.stack([high, middle, low] + [jnp.zeros_like(value)] * 5).astype(jnp.bfloat16)


def join_log(rows):
    return jnp.sum(rows[:, :3].astype(jnp.float32), axis=1)


def later_sums(logs):
    place = jnp.arange(logs.shape[0])
    return jnp.sum(jnp.where(place[None, :] > place[:, None], logs[None, :], 0.0), 1)


def before_sums(logs, upto):
    place = jnp.arange(logs.shape[0])
    between = (place[None, None, :] > place[None, :, None]) & (
        place[None, None, :] < upto[:, None, None]
    )
    reach = jnp.exp(jnp.sum(jnp.where(between, logs[None, None, :], 0.0), 2))
    return jnp.where(place[None, :] < upto[:, None], reach, 0.0)


def plane_summaries(block_summary, block_log):
    plane = lax.axis_size(PLANE)
    heads, head_dim, _ = block_summary.shape
    rows = heads * head_dim // plane
    parts = plane // heads
    message = block_summary.astype(jnp.bfloat16).reshape(plane, rows, head_dim)
    logs = jnp.repeat(split_log(block_log).T, parts, axis=0)
    logs = jnp.broadcast_to(logs[:, :, None], (plane, 8, head_dim))
    arrived = exchange(jnp.concatenate([message, logs], axis=1), PLANE)
    return arrived[:, :rows], join_log(arrived[:, rows:])[:, 0]


def leading_state(summaries, logs):
    depth = lax.axis_size("z")
    rows, head_dim = summaries.shape[1:]
    after = jnp.exp(later_sums(logs))
    plane_sum = jnp.sum(after[:, None, None] * summaries.astype(jnp.float32), axis=0)
    plane_log = jnp.broadcast_to(split_log(jnp.sum(logs))[:, None], (8, head_dim))
    message = jnp.concatenate([plane_sum.astype(jnp.bfloat16), plane_log], axis=0)
    arrived = exchange(jnp.broadcast_to(message[None], (depth,) + message.shape), "z")
    plane_logs = join_log(arrived[:, rows:])[:, 0]
    reach = before_sums(plane_logs, lax.axis_index("z")[None])[0]
    return jnp.sum(reach[:, None, None] * arrived[:, :rows].astype(jnp.float32), axis=0)


def entering_state(summaries, logs, leading, heads):
    plane = lax.axis_size(PLANE)
    place = jnp.arange(plane)
    head_dim = summaries.shape[2]
    to_block = jnp.exp(jnp.sum(jnp.where(place[None, :] < place[:, None], logs[None, :], 0.0), 1))
    inner = before_sums(logs, place)
    entering = to_block[:, None, None] * leading[None] + jnp.sum(
        inner[:, :, None, None] * summaries.astype(jnp.float32)[None], axis=1
    )
    return exchange(entering.astype(jnp.bfloat16), PLANE).reshape(heads, head_dim, head_dim)


def gather_weights(stacked):
    size = lax.axis_size("x")
    near = [stacked] + [
        lax.ppermute(stacked, "x", [(i, (i - k) % size) for i in range(size)])
        for k in range(1, size)
    ]
    far = [lax.ppermute(piece, "core", [(0, 1), (1, 0)]) for piece in near]
    return [
        jnp.concatenate([part[index] for pair in zip(near, far) for part in pair], axis=0)
        for index in range(stacked.shape[0])
    ]


def own_order(rows, back=False):
    chips, cores = lax.axis_size("x"), lax.axis_size("core")
    count, width = rows.shape
    view = rows.reshape(count, chips, cores, width // (chips * cores))
    view = jnp.where(lax.axis_index("core") == 1, view[:, :, ::-1], view)
    own = lax.axis_index("x")
    start = (chips - own) % chips if back else own
    twice = jnp.concatenate([view, view], axis=1)
    return lax.dynamic_slice_in_dim(twice, start, chips, axis=1).reshape(count, width)


def body(
    hidden_in,
    queries,
    keys,
    values,
    log_decay,
    retention_gain,
    norm_gain,
    routes,
    route_weights,
    w_gate,
    w_up,
    w_down,
):
    tok_rows = hidden_in.shape[1]
    model_width = hidden_in.shape[2]
    head_count = log_decay.shape[2]
    head_dim = model_width // head_count
    block_index = lax.axis_index(CTX) * lax.axis_size(EXP) + lax.axis_index(EXP)
    token_position = block_index * tok_rows + jnp.arange(tok_rows, dtype=jnp.int32)
    per_head_keys = rotate(
        keys[0].astype(jnp.float32).reshape(tok_rows, head_count, head_dim), token_position
    ).astype(jnp.bfloat16)
    per_head_values = values[0].reshape(tok_rows, head_count, head_dim)
    running_total = jnp.cumsum(log_decay[0], axis=0)
    trailing_decay = jnp.exp(running_total[-1][None, :] - running_total)
    block_summary = jnp.einsum(
        "qpf,qpy->pfy",
        (per_head_keys.astype(jnp.float32) * trailing_decay[:, :, None]),
        per_head_values.astype(jnp.float32),
        precision=lax.Precision.HIGHEST,
    )
    summaries, logs = plane_summaries(block_summary, running_total[-1])
    stacked = jnp.stack([w_gate[0], w_up[0], w_down[0]])
    stacked, summaries = lax.optimization_barrier((stacked, summaries))
    gate_full, up_full, down_full = gather_weights(stacked)
    leading = leading_state(summaries, logs)
    state_in = entering_state(summaries, logs, leading, head_count)

    per_head_queries = (
        rotate(
            queries[0].astype(jnp.float32).reshape(tok_rows, head_count, head_dim), token_position
        )
        * head_dim ** (-0.5)
    ).astype(jnp.bfloat16)
    scores = jnp.einsum(
        "thd,shd->hts", per_head_queries, per_head_keys, preferred_element_type=jnp.float32
    )
    causal = jnp.arange(tok_rows)[:, None] >= jnp.arange(tok_rows)[None, :]
    spread = running_total.T[:, :, None] - running_total.T[:, None, :]
    weights = jnp.where(
        causal[None], scores * jnp.exp(jnp.where(causal[None], spread, 0.0)), 0.0
    ).astype(jnp.bfloat16)
    inside = jnp.einsum(
        "hts,shd->thd", weights, per_head_values, preferred_element_type=jnp.float32
    )
    external_part = jnp.exp(running_total)[:, :, None] * jnp.einsum(
        "wjc,jco->wjo", per_head_queries, state_in, preferred_element_type=jnp.float32
    )
    retrieved = inside + external_part
    centre = jnp.mean(retrieved, axis=-1, keepdims=True)
    deviation = retrieved - centre
    variance = jnp.mean(deviation * deviation, axis=-1, keepdims=True)
    normalized = (deviation * lax.rsqrt(variance + 1e-05)).reshape(tok_rows, model_width)
    residual = hidden_in[0].astype(jnp.float32) + retention_gain * normalized
    square_mean = jnp.mean(residual * residual, axis=-1, keepdims=True)
    normed = (residual * lax.rsqrt(square_mean + 1e-06) * norm_gain).astype(jnp.bfloat16)

    expert_count = lax.axis_size(OWNERS)
    top_count = routes.shape[2]
    capacity = (tok_rows * top_count * 5 + 4 * expert_count - 1) // (4 * expert_count)
    slot_count = expert_count * capacity
    route_rows = routes[0]
    expert_hits = (
        route_rows.reshape(tok_rows * top_count)[:, None]
        == jnp.arange(expert_count, dtype=jnp.int32)[None, :]
    ).astype(jnp.int32)
    earlier = jnp.cumsum(expert_hits, axis=0) - expert_hits
    slot_rank = jnp.sum(earlier * expert_hits, axis=1).reshape(tok_rows, top_count)
    destination = route_rows * capacity + slot_rank
    slot_lanes = jnp.arange(slot_count, dtype=jnp.int32)
    placing = jnp.any(destination[None, :, :] == slot_lanes[:, None, None], axis=2).astype(
        jnp.bfloat16
    )
    outgoing = jnp.dot(placing, own_order(normed), preferred_element_type=jnp.float32).astype(jnp.bfloat16)
    lanes = 128
    packed = (expert_count, capacity * model_width // lanes, lanes)
    arrived = exchange(outgoing.reshape(packed), OWNERS).reshape(slot_count, model_width)
    gate_next = jnp.dot(arrived, gate_full, preferred_element_type=jnp.float32)
    up_next = jnp.dot(arrived, up_full, preferred_element_type=jnp.float32)
    hidden = (jax.nn.silu(gate_next) * up_next).astype(jnp.bfloat16)
    expert_out = lax.dot_general(
        hidden, down_full, (((1,), (1,)), ((), ())), preferred_element_type=jnp.float32
    ).astype(jnp.bfloat16)
    returned = exchange(expert_out.reshape(packed), OWNERS).reshape(slot_count, model_width)
    mixed = jnp.zeros((tok_rows, model_width), jnp.float32)
    for route_index in range(top_count):
        picking = (destination[:, route_index][:, None] == slot_lanes[None, :]).astype(jnp.bfloat16)
        routed = jnp.dot(picking, returned, preferred_element_type=jnp.float32)
        mixed = mixed + route_weights[0][:, route_index][:, None] * routed
    output = residual + own_order(mixed, back=True)
    return output.astype(jnp.bfloat16)[None]


def solution(mesh):
    ctx, exp, dp = mesh.shape["ctx"], mesh.shape["exp"], mesh.shape["dp"]
    split = Mesh(
        mesh.devices.reshape(ctx // 2, 2, exp // 2, 2, dp), ("z", "ylo", "x", "core", "yhi")
    )
    tokens = P("yhi", CTX + EXP, None)
    experts = P(OWNERS, EXP, None)
    in_specs = (tokens,) * 5 + (P(), P()) + (tokens,) * 2 + (experts,) * 3
    return jax.shard_map(body, mesh=split, in_specs=in_specs, out_specs=tokens, check_vma=False)
```

```python
import jax
import jax.numpy as jnp
from jax import lax
from jax.sharding import Mesh, PartitionSpec as P

CTX = ("z", "ylo")
EXP = ("x", "core")
PLANE = ("ylo", "x", "core")
OWNERS = ("z", "ylo", "yhi")


def exchange(blocks, axes):
    return lax.all_to_all(blocks, axes, split_axis=0, concat_axis=0, tiled=True)


def rotate(vectors, token_position):
    half_dim = vectors.shape[-1] // 2
    inverse = 10000.0 ** (-jnp.arange(half_dim, dtype=jnp.float32) / half_dim)
    angles = token_position.astype(jnp.float32)[:, None] * inverse[None, :]
    cosine = jnp.cos(angles)[:, None, :]
    sine_part = jnp.sin(angles)[:, None, :]
    leading = vectors[..., :half_dim]
    trailing = vectors[..., half_dim:]
    return jnp.concatenate(
        [leading * cosine - trailing * sine_part, trailing * cosine + leading * sine_part], axis=-1
    )


def split_log(value):
    high = lax.reduce_precision(value, 8, 7)
    rest = value - high
    middle = lax.reduce_precision(rest, 8, 7)
    low = rest - middle
    return jnp.stack([high, middle, low] + [jnp.zeros_like(value)] * 5).astype(jnp.bfloat16)


def join_log(rows):
    return jnp.sum(rows[:, :3].astype(jnp.float32), axis=1)


def later_sums(logs):
    place = jnp.arange(logs.shape[0])
    return jnp.sum(jnp.where(place[None, :] > place[:, None], logs[None, :], 0.0), 1)


def before_sums(logs, upto):
    place = jnp.arange(logs.shape[0])
    between = (place[None, None, :] > place[None, :, None]) & (
        place[None, None, :] < upto[:, None, None]
    )
    reach = jnp.exp(jnp.sum(jnp.where(between, logs[None, None, :], 0.0), 2))
    return jnp.where(place[None, :] < upto[:, None], reach, 0.0)


def plane_summaries(block_summary, block_log):
    plane = lax.axis_size(PLANE)
    heads, head_dim, _ = block_summary.shape
    rows = heads * head_dim // plane
    parts = plane // heads
    message = block_summary.astype(jnp.bfloat16).reshape(plane, rows, head_dim)
    logs = jnp.repeat(split_log(block_log).T, parts, axis=0)
    logs = jnp.broadcast_to(logs[:, :, None], (plane, 8, head_dim))
    arrived = exchange(jnp.concatenate([message, logs], axis=1), PLANE)
    return arrived[:, :rows], join_log(arrived[:, rows:])[:, 0]


def leading_state(summaries, logs):
    depth = lax.axis_size("z")
    rows, head_dim = summaries.shape[1:]
    after = jnp.exp(later_sums(logs))
    plane_sum = jnp.sum(after[:, None, None] * summaries.astype(jnp.float32), axis=0)
    plane_log = split_log(jnp.sum(jnp.broadcast_to(logs[:, None], (logs.shape[0], head_dim)), axis=0))
    message = jnp.concatenate([plane_sum.astype(jnp.bfloat16), plane_log], axis=0)
    arrived = exchange(jnp.broadcast_to(message[None], (depth,) + message.shape), "z")
    plane_logs = join_log(arrived[:, rows:])[:, 0]
    reach = before_sums(plane_logs, lax.axis_index("z")[None])[0]
    return jnp.sum(reach[:, None, None] * arrived[:, :rows].astype(jnp.float32), axis=0)


def entering_state(summaries, logs, leading, heads):
    plane = lax.axis_size(PLANE)
    place = jnp.arange(plane)
    head_dim = summaries.shape[2]
    to_block = jnp.exp(jnp.sum(jnp.where(place[None, :] < place[:, None], logs[None, :], 0.0), 1))
    inner = before_sums(logs, place)
    entering = to_block[:, None, None] * leading[None] + jnp.sum(
        inner[:, :, None, None] * summaries.astype(jnp.float32)[None], axis=1
    )
    return exchange(entering.astype(jnp.bfloat16), PLANE).reshape(heads, head_dim, head_dim)


def near_weights(stacked):
    size = lax.axis_size("x")
    return [stacked] + [
        lax.ppermute(stacked, "x", [(i, (i - k) % size) for i in range(size)])
        for k in range(1, size)
    ]


def all_weights(near):
    far = [lax.ppermute(piece, "core", [(0, 1), (1, 0)]) for piece in near]
    return [
        jnp.concatenate([part[index] for pair in zip(near, far) for part in pair], axis=0)
        for index in range(near[0].shape[0])
    ]


def own_order(rows, back=False):
    chips, cores = lax.axis_size("x"), lax.axis_size("core")
    count, width = rows.shape
    view = rows.reshape(count, chips, cores, width // (chips * cores))
    view = jnp.where(lax.axis_index("core") == 1, view[:, :, ::-1], view)
    own = lax.axis_index("x")
    start = (chips - own) % chips if back else own
    twice = jnp.concatenate([view, view], axis=1)
    return lax.dynamic_slice_in_dim(twice, start, chips, axis=1).reshape(count, width)


def body(
    hidden_in,
    queries,
    keys,
    values,
    log_decay,
    retention_gain,
    norm_gain,
    routes,
    route_weights,
    w_gate,
    w_up,
    w_down,
):
    tok_rows = hidden_in.shape[1]
    model_width = hidden_in.shape[2]
    head_count = log_decay.shape[2]
    head_dim = model_width // head_count
    block_index = lax.axis_index(CTX) * lax.axis_size(EXP) + lax.axis_index(EXP)
    token_position = block_index * tok_rows + jnp.arange(tok_rows, dtype=jnp.int32)
    per_head_keys = rotate(
        keys[0].astype(jnp.float32).reshape(tok_rows, head_count, head_dim), token_position
    ).astype(jnp.bfloat16)
    per_head_values = values[0].reshape(tok_rows, head_count, head_dim)
    running_total = jnp.cumsum(log_decay[0], axis=0)
    trailing_decay = jnp.exp(running_total[-1][None, :] - running_total)
    block_summary = jnp.einsum(
        "qpf,qpy->pfy",
        (per_head_keys.astype(jnp.float32) * trailing_decay[:, :, None]),
        per_head_values.astype(jnp.float32),
        precision=lax.Precision.HIGHEST,
    )
    summaries, logs = plane_summaries(block_summary, running_total[-1])
    stacked = jnp.stack([w_gate[0], w_up[0], w_down[0]])
    near = near_weights(stacked)
    leading = leading_state(summaries, logs)
    state_in = entering_state(summaries, logs, leading, head_count)

    per_head_queries = (
        rotate(
            queries[0].astype(jnp.float32).reshape(tok_rows, head_count, head_dim), token_position
        )
        * head_dim ** (-0.5)
    ).astype(jnp.bfloat16)
    scores = jnp.einsum(
        "thd,shd->hts", per_head_queries, per_head_keys, preferred_element_type=jnp.float32
    )
    causal = jnp.arange(tok_rows)[:, None] >= jnp.arange(tok_rows)[None, :]
    spread = running_total.T[:, :, None] - running_total.T[:, None, :]
    weights = jnp.where(
        causal[None], scores * jnp.exp(jnp.where(causal[None], spread, 0.0)), 0.0
    ).astype(jnp.bfloat16)
    inside = jnp.einsum(
        "hts,shd->thd", weights, per_head_values, preferred_element_type=jnp.float32
    )
    external_part = jnp.exp(running_total)[:, :, None] * jnp.einsum(
        "wjc,jco->wjo", per_head_queries, state_in, preferred_element_type=jnp.float32
    )
    retrieved = inside + external_part
    centre = jnp.mean(retrieved, axis=-1, keepdims=True)
    deviation = retrieved - centre
    variance = jnp.mean(deviation * deviation, axis=-1, keepdims=True)
    normalized = (deviation * lax.rsqrt(variance + 1e-05)).reshape(tok_rows, model_width)
    residual = hidden_in[0].astype(jnp.float32) + retention_gain * normalized
    square_mean = jnp.mean(residual * residual, axis=-1, keepdims=True)
    normed = (residual * lax.rsqrt(square_mean + 1e-06) * norm_gain).astype(jnp.bfloat16)

    expert_count = lax.axis_size(OWNERS)
    top_count = routes.shape[2]
    capacity = (tok_rows * top_count * 5 + 4 * expert_count - 1) // (4 * expert_count)
    slot_count = expert_count * capacity
    route_rows = routes[0]
    expert_hits = (
        route_rows.reshape(tok_rows * top_count)[:, None]
        == jnp.arange(expert_count, dtype=jnp.int32)[None, :]
    ).astype(jnp.int32)
    earlier = jnp.cumsum(expert_hits, axis=0) - expert_hits
    slot_rank = jnp.sum(earlier * expert_hits, axis=1).reshape(tok_rows, top_count)
    destination = route_rows * capacity + slot_rank
    slot_lanes = jnp.arange(slot_count, dtype=jnp.int32)
    placing = jnp.any(destination[None, :, :] == slot_lanes[:, None, None], axis=2).astype(
        jnp.bfloat16
    )
    outgoing = jnp.dot(placing, own_order(normed), preferred_element_type=jnp.float32).astype(jnp.bfloat16)
    gate_full, up_full, down_full = all_weights(near)
    lanes = 128
    packed = (expert_count, capacity * model_width // lanes, lanes)
    arrived = exchange(outgoing.reshape(packed), OWNERS).reshape(slot_count, model_width)
    gate_next = jnp.dot(arrived, gate_full, preferred_element_type=jnp.float32)
    up_next = jnp.dot(arrived, up_full, preferred_element_type=jnp.float32)
    hidden = (jax.nn.silu(gate_next) * up_next).astype(jnp.bfloat16)
    expert_out = lax.dot_general(
        hidden, down_full, (((1,), (1,)), ((), ())), preferred_element_type=jnp.float32
    ).astype(jnp.bfloat16)
    returned = exchange(expert_out.reshape(packed), OWNERS).reshape(slot_count, model_width)
    mixed = jnp.zeros((tok_rows, model_width), jnp.float32)
    for route_index in range(top_count):
        picking = (destination[:, route_index][:, None] == slot_lanes[None, :]).astype(jnp.bfloat16)
        routed = jnp.dot(picking, returned, preferred_element_type=jnp.float32)
        mixed = mixed + route_weights[0][:, route_index][:, None] * routed
    output = residual + own_order(mixed, back=True)
    return output.astype(jnp.bfloat16)[None]


def solution(mesh):
    ctx, exp, dp = mesh.shape["ctx"], mesh.shape["exp"], mesh.shape["dp"]
    split = Mesh(
        mesh.devices.reshape(ctx // 2, 2, exp // 2, 2, dp), ("z", "ylo", "x", "core", "yhi")
    )
    tokens = P("yhi", CTX + EXP, None)
    experts = P(OWNERS, EXP, None)
    in_specs = (tokens,) * 5 + (P(), P()) + (tokens,) * 2 + (experts,) * 3
    return jax.shard_map(body, mesh=split, in_specs=in_specs, out_specs=tokens, check_vma=False)
```

```python
import jax
import jax.numpy as jnp
from jax import lax
from jax.experimental import pallas as pl
from jax.experimental.pallas import tpu as pltpu
from jax.sharding import Mesh, PartitionSpec as P

CTX = ("z", "ylo")
EXP = ("x", "core")
PLANE = ("ylo", "x", "core")
OWNERS = ("z", "ylo", "yhi")


def exchange(blocks, axes):
    return lax.all_to_all(blocks, axes, split_axis=0, concat_axis=0, tiled=True)


def rotate(vectors, token_position):
    half_dim = vectors.shape[-1] // 2
    inverse = 10000.0 ** (-jnp.arange(half_dim, dtype=jnp.float32) / half_dim)
    angles = token_position.astype(jnp.float32)[:, None] * inverse[None, :]
    cosine = jnp.cos(angles)[:, None, :]
    sine_part = jnp.sin(angles)[:, None, :]
    leading = vectors[..., :half_dim]
    trailing = vectors[..., half_dim:]
    return jnp.concatenate(
        [leading * cosine - trailing * sine_part, trailing * cosine + leading * sine_part], axis=-1
    )


def split_log(value):
    high = lax.reduce_precision(value, 8, 7)
    rest = value - high
    middle = lax.reduce_precision(rest, 8, 7)
    low = rest - middle
    return jnp.stack([high, middle, low] + [jnp.zeros_like(value)] * 5).astype(jnp.bfloat16)


def log_row(block):
    return jnp.sum(block.astype(jnp.float32), axis=0, keepdims=True)


def plane_sum_kernel(arrived_ref, message_ref):
    plane, _, head_dim = arrived_ref.shape
    rows = arrived_ref.shape[1] - 8
    total = jnp.zeros((rows, head_dim), jnp.float32)
    log_total = jnp.zeros((1, head_dim), jnp.float32)
    for block in range(plane):
        log = log_row(arrived_ref[block, rows:])
        total = jnp.exp(log) * total + arrived_ref[block, :rows].astype(jnp.float32)
        log_total = log_total + log
    high = log_total.astype(jnp.bfloat16).astype(jnp.float32)
    middle = (log_total - high).astype(jnp.bfloat16).astype(jnp.float32)
    low = log_total - high - middle
    line = lax.broadcasted_iota(jnp.int32, (8, head_dim), 0)
    logs = jnp.where(line == 0, high, jnp.where(line == 1, middle, jnp.where(line == 2, low, 0.0)))
    total, logs = total.astype(jnp.bfloat16), logs.astype(jnp.bfloat16)
    for z in range(message_ref.shape[0]):
        message_ref[z, :rows] = total
        message_ref[z, rows:] = logs


def entering_kernel(own_ref, arrived_ref, planes_ref, entering_ref):
    rows = entering_ref.shape[1]
    own = own_ref[0]
    state = jnp.zeros(entering_ref.shape[1:], jnp.float32)
    for z in range(planes_ref.shape[0]):
        log = log_row(planes_ref[z, rows:])
        later = jnp.exp(log) * state + planes_ref[z, :rows].astype(jnp.float32)
        state = jnp.where(z < own, later, state)
    for block in range(arrived_ref.shape[0]):
        entering_ref[block] = state.astype(jnp.bfloat16)
        log = log_row(arrived_ref[block, rows:])
        state = jnp.exp(log) * state + arrived_ref[block, :rows].astype(jnp.float32)


def plane_summaries(block_summary, block_log):
    plane = lax.axis_size(PLANE)
    heads, head_dim, _ = block_summary.shape
    rows = heads * head_dim // plane
    parts = plane // heads
    message = block_summary.astype(jnp.bfloat16).reshape(plane, rows, head_dim)
    logs = jnp.repeat(split_log(block_log).T, parts, axis=0)
    logs = jnp.broadcast_to(logs[:, :, None], (plane, 8, head_dim))
    return exchange(jnp.concatenate([message, logs], axis=1), PLANE)


def plane_sums(arrived):
    depth = lax.axis_size("z")
    message = pl.pallas_call(
        plane_sum_kernel,
        out_shape=jax.ShapeDtypeStruct((depth,) + arrived.shape[1:], jnp.bfloat16),
        cost_estimate=pl.CostEstimate(flops=500000, bytes_accessed=600000, transcendentals=2048),
    )(arrived)
    return exchange(message, "z")


def entering_state(arrived, planes, heads):
    plane, rows, head_dim = arrived.shape
    entering = pl.pallas_call(
        entering_kernel,
        out_shape=jax.ShapeDtypeStruct((plane, rows - 8, head_dim), jnp.bfloat16),
        in_specs=[
            pl.BlockSpec(memory_space=pltpu.SMEM),
            pl.BlockSpec(memory_space=pltpu.VMEM),
            pl.BlockSpec(memory_space=pltpu.VMEM),
        ],
        cost_estimate=pl.CostEstimate(flops=900000, bytes_accessed=900000, transcendentals=4096),
    )(lax.axis_index("z")[None], arrived, planes)
    return exchange(entering, PLANE).reshape(heads, head_dim, head_dim)


def along_x(piece, step):
    size = lax.axis_size("x")
    return lax.ppermute(piece, "x", [(i, (i - step) % size) for i in range(size)])


def all_weights(own, after, before):
    half = own.shape[1] // 2
    far = [along_x(after[:, :half], 1), along_x(before[:, half:], -1)]

    def swapped(piece):
        return lax.ppermute(piece, "core", [(0, 1), (1, 0)])

    pieces = [[own], [after], far, [before]]
    other = [[swapped(part) for part in piece] for piece in pieces]
    parts = [part for pair in zip(pieces, other) for piece in pair for part in piece]
    return [jnp.concatenate([part[index] for part in parts], axis=0) for index in range(own.shape[0])]


def own_order(rows, back=False):
    chips, cores = lax.axis_size("x"), lax.axis_size("core")
    count, width = rows.shape
    view = rows.reshape(count, chips, cores, width // (chips * cores))
    view = jnp.where(lax.axis_index("core") == 1, view[:, :, ::-1], view)
    own = lax.axis_index("x")
    start = (chips - own) % chips if back else own
    twice = jnp.concatenate([view, view], axis=1)
    return lax.dynamic_slice_in_dim(twice, start, chips, axis=1).reshape(count, width)


def body(
    hidden_in,
    queries,
    keys,
    values,
    log_decay,
    retention_gain,
    norm_gain,
    routes,
    route_weights,
    w_gate,
    w_up,
    w_down,
):
    tok_rows = hidden_in.shape[1]
    model_width = hidden_in.shape[2]
    head_count = log_decay.shape[2]
    head_dim = model_width // head_count
    block_index = lax.axis_index(CTX) * lax.axis_size(EXP) + lax.axis_index(EXP)
    token_position = block_index * tok_rows + jnp.arange(tok_rows, dtype=jnp.int32)
    per_head_keys = rotate(
        keys[0].astype(jnp.float32).reshape(tok_rows, head_count, head_dim), token_position
    ).astype(jnp.bfloat16)
    per_head_values = values[0].reshape(tok_rows, head_count, head_dim)
    running_total = jnp.cumsum(log_decay[0], axis=0)
    trailing_decay = jnp.exp(running_total[-1][None, :] - running_total)
    block_summary = jnp.einsum(
        "qpf,qpy->pfy",
        (per_head_keys.astype(jnp.float32) * trailing_decay[:, :, None]),
        per_head_values.astype(jnp.float32),
        precision=lax.Precision.HIGHEST,
    )
    summaries = plane_summaries(block_summary, running_total[-1])
    stacked = jnp.stack([w_gate[0], w_up[0], w_down[0]])
    after, before = along_x(stacked, 1), along_x(stacked, -1)
    planes = plane_sums(summaries)
    state_in = entering_state(summaries, planes, head_count)

    per_head_queries = (
        rotate(
            queries[0].astype(jnp.float32).reshape(tok_rows, head_count, head_dim), token_position
        )
        * head_dim ** (-0.5)
    ).astype(jnp.bfloat16)
    scores = jnp.einsum(
        "thd,shd->hts", per_head_queries, per_head_keys, preferred_element_type=jnp.float32
    )
    causal = jnp.arange(tok_rows)[:, None] >= jnp.arange(tok_rows)[None, :]
    spread = running_total.T[:, :, None] - running_total.T[:, None, :]
    weights = jnp.where(
        causal[None], scores * jnp.exp(jnp.where(causal[None], spread, 0.0)), 0.0
    ).astype(jnp.bfloat16)
    inside = jnp.einsum(
        "hts,shd->thd", weights, per_head_values, preferred_element_type=jnp.float32
    )
    external_part = jnp.exp(running_total)[:, :, None] * jnp.einsum(
        "wjc,jco->wjo", per_head_queries, state_in, preferred_element_type=jnp.float32
    )
    retrieved = inside + external_part
    centre = jnp.mean(retrieved, axis=-1, keepdims=True)
    deviation = retrieved - centre
    variance = jnp.mean(deviation * deviation, axis=-1, keepdims=True)
    normalized = (deviation * lax.rsqrt(variance + 1e-05)).reshape(tok_rows, model_width)
    residual = hidden_in[0].astype(jnp.float32) + retention_gain * normalized
    square_mean = jnp.mean(residual * residual, axis=-1, keepdims=True)
    normed = (residual * lax.rsqrt(square_mean + 1e-06) * norm_gain).astype(jnp.bfloat16)

    expert_count = lax.axis_size(OWNERS)
    top_count = routes.shape[2]
    capacity = (tok_rows * top_count * 5 + 4 * expert_count - 1) // (4 * expert_count)
    slot_count = expert_count * capacity
    route_rows = routes[0]
    expert_hits = (
        route_rows.reshape(tok_rows * top_count)[:, None]
        == jnp.arange(expert_count, dtype=jnp.int32)[None, :]
    ).astype(jnp.int32)
    earlier = jnp.cumsum(expert_hits, axis=0) - expert_hits
    slot_rank = jnp.sum(earlier * expert_hits, axis=1).reshape(tok_rows, top_count)
    destination = route_rows * capacity + slot_rank
    slot_lanes = jnp.arange(slot_count, dtype=jnp.int32)
    placing = jnp.any(destination[None, :, :] == slot_lanes[:, None, None], axis=2).astype(
        jnp.bfloat16
    )
    outgoing = jnp.dot(placing, own_order(normed), preferred_element_type=jnp.float32).astype(jnp.bfloat16)
    gate_full, up_full, down_full = all_weights(stacked, after, before)
    lanes = 128
    packed = (expert_count, capacity * model_width // lanes, lanes)
    arrived = exchange(outgoing.reshape(packed), OWNERS).reshape(slot_count, model_width)
    gate_next = jnp.dot(arrived, gate_full, preferred_element_type=jnp.float32)
    up_next = jnp.dot(arrived, up_full, preferred_element_type=jnp.float32)
    hidden = (jax.nn.silu(gate_next) * up_next).astype(jnp.bfloat16)
    expert_out = lax.dot_general(
        hidden, down_full, (((1,), (1,)), ((), ())), preferred_element_type=jnp.float32
    ).astype(jnp.bfloat16)
    returned = exchange(expert_out.reshape(packed), OWNERS).reshape(slot_count, model_width)
    mixed = jnp.zeros((tok_rows, model_width), jnp.float32)
    for route_index in range(top_count):
        picking = (destination[:, route_index][:, None] == slot_lanes[None, :]).astype(jnp.bfloat16)
        routed = jnp.dot(picking, returned, preferred_element_type=jnp.float32)
        mixed = mixed + route_weights[0][:, route_index][:, None] * routed
    output = residual + own_order(mixed, back=True)
    return output.astype(jnp.bfloat16)[None]


def solution(mesh):
    ctx, exp, dp = mesh.shape["ctx"], mesh.shape["exp"], mesh.shape["dp"]
    split = Mesh(
        mesh.devices.reshape(ctx // 2, 2, exp // 2, 2, dp), ("z", "ylo", "x", "core", "yhi")
    )
    tokens = P("yhi", CTX + EXP, None)
    experts = P(OWNERS, EXP, None)
    in_specs = (tokens,) * 5 + (P(), P()) + (tokens,) * 2 + (experts,) * 3
    return jax.shard_map(body, mesh=split, in_specs=in_specs, out_specs=tokens, check_vma=False)
```

```python
import jax
import jax.numpy as jnp
import numpy as np
from jax import lax
from jax.experimental import pallas as pl
from jax.experimental.pallas import tpu as pltpu
from jax.sharding import Mesh, PartitionSpec as P

CTX = ("z", "ylo")
EXP = ("x", "core")
PLANE = ("ylo", "x", "core")
OWNERS = ("z", "ylo", "yhi")
LOG_ROWS = 8
F32, BF16 = jnp.float32, jnp.bfloat16


def exchange(blocks, axes):
    return lax.all_to_all(blocks, axes, split_axis=0, concat_axis=0, tiled=True)


def dot32(left, right):
    return jnp.dot(left, right, preferred_element_type=F32)


def cost(flops, moved):
    return pl.CostEstimate(flops=flops, bytes_accessed=moved, transcendentals=flops // 1000)


def log_rows(value):
    high = value.astype(BF16).astype(F32)
    middle = (value - high).astype(BF16).astype(F32)
    low = value - high - middle
    line = lax.broadcasted_iota(jnp.int32, (LOG_ROWS, value.shape[1]), 0)
    rows = jnp.where(line == 0, high, jnp.where(line == 1, middle, jnp.where(line == 2, low, 0.0)))
    return rows.astype(BF16)


def log_row(rows):
    return jnp.sum(rows.astype(F32), axis=0, keepdims=True)


def turned(block, cosine, sine):
    return block * cosine + pltpu.roll(block, block.shape[1] // 2, 1) * sine


def summary_kernel(keys_ref, values_ref, log_ref, cos_ref, sin_ref, message_ref, turned_ref, total_ref):
    heads, count = log_ref.shape
    head_dim = cos_ref.shape[1]
    parts = message_ref.shape[0] // heads
    rows = head_dim // parts
    earlier = lax.broadcasted_iota(jnp.int32, (count, count), 0)
    upto = lax.broadcasted_iota(jnp.int32, (count, count), 1)
    ones = jnp.where(earlier <= upto, 1.0, 0.0).astype(F32)
    total = jnp.dot(
        log_ref[...], ones, precision=lax.Precision.HIGHEST, preferred_element_type=F32
    )
    total_ref[...] = total
    last = total[:, count - 1 :]
    trailing = jnp.exp(last - total)
    wide = jnp.broadcast_to(last, (heads, head_dim))
    for head in range(heads):
        lanes = slice(head * head_dim, (head + 1) * head_dim)
        keys = turned(keys_ref[:, lanes].astype(F32), cos_ref[...], sin_ref[...]).astype(BF16)
        turned_ref[:, lanes] = keys
        faded = keys.astype(F32).T * trailing[head : head + 1]
        coarse = faded.astype(BF16)
        fine = (faded - coarse.astype(F32)).astype(BF16)
        summary = dot32(coarse, values_ref[:, lanes]) + dot32(fine, values_ref[:, lanes])
        summary = summary.astype(BF16)
        logs = log_rows(wide[head : head + 1])
        for part in range(parts):
            message_ref[head * parts + part, :rows] = summary[part * rows : (part + 1) * rows]
            message_ref[head * parts + part, rows:] = logs


def inside_kernel(
    queries_ref, keys_ref, values_ref, total_ref, cos_ref, sin_ref, turned_ref, inside_ref, fade_ref
):
    heads, count = total_ref.shape
    head_dim = cos_ref.shape[1]
    row = lax.broadcasted_iota(jnp.int32, (count, count), 0)
    column = lax.broadcasted_iota(jnp.int32, (count, count), 1)
    causal = row >= column
    for head in range(heads):
        lanes = slice(head * head_dim, (head + 1) * head_dim)
        queries = turned(queries_ref[:, lanes].astype(F32), cos_ref[...], sin_ref[...])
        queries = (queries * head_dim ** (-0.5)).astype(BF16)
        turned_ref[:, lanes] = queries
        scores = lax.dot_general(
            queries, keys_ref[:, lanes], (((1,), (1,)), ((), ())), preferred_element_type=F32
        )
        here = total_ref[head : head + 1, :]
        down = jnp.broadcast_to(here, (head_dim, count)).T
        spread = jnp.where(causal, down - here, 0.0)
        weights = jnp.where(causal, scores * jnp.exp(spread), 0.0).astype(BF16)
        inside_ref[:, lanes] = dot32(weights, values_ref[:, lanes])
        fade_ref[:, lanes] = jnp.exp(down)


def plane_sum_kernel(arrived_ref, message_ref):
    plane, rows, head_dim = arrived_ref.shape
    rows = rows - LOG_ROWS
    total = jnp.zeros((rows, head_dim), F32)
    log_total = jnp.zeros((1, head_dim), F32)
    for block in range(plane):
        log = log_row(arrived_ref[block, rows:])
        total = jnp.exp(log) * total + arrived_ref[block, :rows].astype(F32)
        log_total = log_total + log
    total, logs = total.astype(BF16), log_rows(log_total)
    for z in range(message_ref.shape[0]):
        message_ref[z, :rows] = total
        message_ref[z, rows:] = logs


def entering_kernel(own_ref, arrived_ref, planes_ref, entering_ref):
    rows = entering_ref.shape[1]
    own = own_ref[0]
    state = jnp.zeros(entering_ref.shape[1:], F32)
    for z in range(planes_ref.shape[0]):
        log = log_row(planes_ref[z, rows:])
        later = jnp.exp(log) * state + planes_ref[z, :rows].astype(F32)
        state = jnp.where(z < own, later, state)
    for block in range(arrived_ref.shape[0]):
        entering_ref[block] = state.astype(BF16)
        log = log_row(arrived_ref[block, rows:])
        state = jnp.exp(log) * state + arrived_ref[block, :rows].astype(F32)


def outgoing_kernel(
    own_ref,
    state_ref,
    queries_ref,
    inside_ref,
    fade_ref,
    hidden_ref,
    group_gain_ref,
    norm_gain_ref,
    placing_ref,
    residual_ref,
    outgoing_ref,
    normed_ref,
):
    chunks, count, head_dim = normed_ref.shape
    square = jnp.zeros((count, 1), F32)
    for head in range(chunks):
        lanes = slice(head * head_dim, (head + 1) * head_dim)
        far = dot32(queries_ref[:, lanes], state_ref[head * head_dim : (head + 1) * head_dim, :])
        retrieved = inside_ref[:, lanes] + fade_ref[:, lanes] * far
        deviation = retrieved - jnp.mean(retrieved, axis=1, keepdims=True)
        variance = jnp.mean(deviation * deviation, axis=1, keepdims=True)
        normalized = deviation * lax.rsqrt(variance + 1e-05)
        residual = hidden_ref[:, lanes].astype(F32) + group_gain_ref[:, lanes] * normalized
        residual_ref[:, lanes] = residual
        square = square + jnp.sum(residual * residual, axis=1, keepdims=True)
    scale = lax.rsqrt(square * (1.0 / (chunks * head_dim)) + 1e-06)
    for chunk in range(chunks):
        lanes = slice(chunk * head_dim, (chunk + 1) * head_dim)
        normed = residual_ref[:, lanes] * scale * norm_gain_ref[:, lanes]
        normed_ref[own_ref[chunk]] = normed.astype(BF16)
    for chunk in range(chunks):
        lanes = slice(chunk * head_dim, (chunk + 1) * head_dim)
        outgoing_ref[:, lanes] = dot32(placing_ref[...], normed_ref[chunk]).astype(BF16)


def expert_kernel(*refs):
    arrived_ref, pieces, out_ref = refs[0], refs[1:-4], refs[-4]
    weights_ref, hidden_ref, sems = refs[-3], refs[-2], refs[-1]
    width = weights_ref.shape[2]
    copies = []
    for index in range(3):
        start = 0
        for number, piece in enumerate(pieces):
            size = piece.shape[1]
            copy = pltpu.make_async_copy(
                piece.at[index],
                weights_ref.at[index, pl.ds(start, size), :],
                sems.at[index, number],
            )
            copy.start()
            copies.append(copy)
            start += size
    count = len(pieces)
    for copy in copies[: 2 * count]:
        copy.wait()
    tile = 512
    for start in range(0, width, tile):
        columns = slice(start, min(width, start + tile))
        gate = dot32(arrived_ref[...], weights_ref[0, :, columns])
        up = dot32(arrived_ref[...], weights_ref[1, :, columns])
        hidden_ref[:, columns] = (gate / (1.0 + jnp.exp(-gate)) * up).astype(BF16)
    for copy in copies[2 * count :]:
        copy.wait()
    tile = 256
    for start in range(0, out_ref.shape[1], tile):
        rows = slice(start, start + tile)
        out_ref[:, rows] = lax.dot_general(
            hidden_ref[...],
            weights_ref[2, rows, :],
            (((1,), (1,)), ((), ())),
            preferred_element_type=F32,
        ).astype(BF16)


def shape(dims, kind):
    return jax.ShapeDtypeStruct(dims, kind)


def run_experts(arrived, pieces):
    rows, model_width = arrived.shape
    width = pieces[0].shape[2]
    anywhere = pl.BlockSpec(memory_space=pl.ANY)
    return pl.pallas_call(
        expert_kernel,
        name="experts",
        out_shape=shape((rows, model_width), BF16),
        in_specs=[pl.BlockSpec(memory_space=pltpu.VMEM)] + [anywhere] * len(pieces),
        out_specs=pl.BlockSpec(memory_space=pltpu.VMEM),
        scratch_shapes=[
            pltpu.VMEM((3, model_width, width), BF16),
            pltpu.VMEM((rows, width), BF16),
            pltpu.SemaphoreType.DMA((3, len(pieces))),
        ],
        cost_estimate=cost(6 * rows * model_width * width, 6 * model_width * width),
    )(arrived, *pieces)


def along_x(piece, step):
    size = lax.axis_size("x")
    return lax.ppermute(piece, "x", [(i, (i - step) % size) for i in range(size)])


def swapped(piece):
    return lax.ppermute(piece, "core", [(0, 1), (1, 0)])


def own_places():
    chips, cores = lax.axis_size("x"), lax.axis_size("core")
    chunk = jnp.arange(chips * cores, dtype=jnp.int32)
    chip = (chunk // cores + chips - lax.axis_index("x")) % chips
    return chip * cores + (chunk + lax.axis_index("core")) % cores


def model_order(rows):
    chips, cores = lax.axis_size("x"), lax.axis_size("core")
    count, width = rows.shape
    view = rows.reshape(count, chips, cores, width // (chips * cores))
    view = jnp.where(lax.axis_index("core") == 1, view[:, :, ::-1], view)
    start = (chips - lax.axis_index("x")) % chips
    twice = jnp.concatenate([view, view], axis=1)
    return lax.dynamic_slice_in_dim(twice, start, chips, axis=1).reshape(count, width)


def body(
    hidden_in,
    queries,
    keys,
    values,
    log_decay,
    retention_gain,
    norm_gain,
    routes,
    route_weights,
    w_gate,
    w_up,
    w_down,
):
    tok_rows = hidden_in.shape[1]
    model_width = hidden_in.shape[2]
    head_count = log_decay.shape[2]
    head_dim = model_width // head_count
    wide = (tok_rows, model_width)
    plane, depth = lax.axis_size(PLANE), lax.axis_size("z")
    part_rows = head_count * head_dim // plane
    message = (plane, part_rows + LOG_ROWS, head_dim)

    half = head_dim // 2
    inverse = (10000.0 ** (-np.arange(half) / half)).astype(np.float32)
    sign = np.repeat(np.array([-1.0, 1.0], np.float32), half)
    block_index = lax.axis_index(CTX) * lax.axis_size(EXP) + lax.axis_index(EXP)
    position = block_index * tok_rows + jnp.arange(tok_rows, dtype=jnp.int32)
    angles = position.astype(F32)[:, None] * np.tile(inverse, 2)[None, :]
    cosine, sine = jnp.cos(angles), jnp.sin(angles) * sign

    out_message, turned_keys, total = pl.pallas_call(
        summary_kernel,
        name="summary",
        out_shape=(shape(message, BF16), shape(wide, BF16), shape((head_count, tok_rows), F32)),
        cost_estimate=cost(70000000, 1200000),
    )(keys[0], values[0], log_decay[0].T, cosine, sine)
    summaries = exchange(out_message, PLANE)
    stacked = jnp.stack([w_gate[0], w_up[0], w_down[0]])
    after, before = along_x(stacked, 1), along_x(stacked, -1)
    turned_queries, inside, fade = pl.pallas_call(
        inside_kernel,
        name="inside",
        out_shape=(shape(wide, BF16), shape(wide, F32), shape(wide, F32)),
        cost_estimate=cost(70000000, 2200000),
    )(queries[0], turned_keys, values[0], total, cosine, sine)
    sums = pl.pallas_call(
        plane_sum_kernel,
        name="plane_sum",
        out_shape=shape((depth,) + message[1:], BF16),
        cost_estimate=cost(500000, 600000),
    )(summaries)
    sums = exchange(sums, "z")
    own_other = swapped(stacked)
    entering = pl.pallas_call(
        entering_kernel,
        name="enter",
        out_shape=shape((plane, part_rows, head_dim), BF16),
        in_specs=[pl.BlockSpec(memory_space=pltpu.SMEM)]
        + [pl.BlockSpec(memory_space=pltpu.VMEM)] * 2,
        cost_estimate=cost(900000, 900000),
    )(lax.axis_index("z")[None], summaries, sums)
    state_in = exchange(entering, PLANE).reshape(model_width, head_dim)
    after_other, before_other = swapped(after), swapped(before)

    expert_count = lax.axis_size(OWNERS)
    top_count = routes.shape[2]
    capacity = (tok_rows * top_count * 5 + 4 * expert_count - 1) // (4 * expert_count)
    slot_count = expert_count * capacity
    route_rows = routes[0]
    expert_hits = (
        route_rows.reshape(tok_rows * top_count)[:, None]
        == jnp.arange(expert_count, dtype=jnp.int32)[None, :]
    ).astype(jnp.int32)
    earlier = jnp.cumsum(expert_hits, axis=0) - expert_hits
    slot_rank = jnp.sum(earlier * expert_hits, axis=1).reshape(tok_rows, top_count)
    destination = route_rows * capacity + slot_rank
    slot_lanes = jnp.arange(slot_count, dtype=jnp.int32)
    placing = jnp.any(destination[None, :, :] == slot_lanes[:, None, None], axis=2).astype(BF16)

    residual, outgoing = pl.pallas_call(
        outgoing_kernel,
        name="outgoing",
        out_shape=(shape(wide, F32), shape((slot_count, model_width), BF16)),
        in_specs=[pl.BlockSpec(memory_space=pltpu.SMEM)]
        + [pl.BlockSpec(memory_space=pltpu.VMEM)] * 8,
        scratch_shapes=[pltpu.VMEM((head_count, tok_rows, head_dim), BF16)],
        cost_estimate=cost(120000000, 3000000),
    )(
        own_places(),
        state_in,
        turned_queries,
        inside,
        fade,
        hidden_in[0],
        retention_gain[None],
        norm_gain[None],
        placing,
    )
    lanes = 128
    packed = (expert_count, capacity * model_width // lanes, lanes)
    arrived = exchange(outgoing.reshape(packed), OWNERS).reshape(slot_count, model_width)
    cut = stacked.shape[1] // 2
    far = [along_x(after[:, :cut], 1), along_x(before[:, cut:], -1)]
    far_other = [swapped(piece) for piece in far]
    pieces = [stacked, own_other, after, after_other, *far, *far_other, before, before_other]
    expert_out = run_experts(arrived, pieces)
    returned = exchange(expert_out.reshape(packed), OWNERS).reshape(slot_count, model_width)
    mixed = jnp.zeros(wide, F32)
    for route_index in range(top_count):
        picking = (destination[:, route_index][:, None] == slot_lanes[None, :]).astype(BF16)
        routed = dot32(picking, returned)
        mixed = mixed + route_weights[0][:, route_index][:, None] * routed
    return (residual + model_order(mixed)).astype(BF16)[None]


def solution(mesh):
    ctx, exp, dp = mesh.shape["ctx"], mesh.shape["exp"], mesh.shape["dp"]
    split = Mesh(
        mesh.devices.reshape(ctx // 2, 2, exp // 2, 2, dp), ("z", "ylo", "x", "core", "yhi")
    )
    tokens = P("yhi", CTX + EXP, None)
    experts = P(OWNERS, EXP, None)
    in_specs = (tokens,) * 5 + (P(), P()) + (tokens,) * 2 + (experts,) * 3
    return jax.shard_map(body, mesh=split, in_specs=in_specs, out_specs=tokens, check_vma=False)
```

```python
import jax
import jax.numpy as jnp
import numpy as np
from jax import lax
from jax.experimental import pallas as pl
from jax.experimental.pallas import tpu as pltpu
from jax.sharding import Mesh, PartitionSpec as P

CTX = ("z", "ylo")
EXP = ("x", "core")
PLANE = ("ylo", "x", "core")
OWNERS = ("z", "ylo", "yhi")
LOG_ROWS = 8
LANES = 128
F32, BF16 = jnp.float32, jnp.bfloat16


def exchange(blocks, axes):
    return lax.all_to_all(blocks, axes, split_axis=0, concat_axis=0, tiled=True)


def dot32(left, right):
    return jnp.dot(left, right, preferred_element_type=F32)


def cost(flops, moved):
    return pl.CostEstimate(flops=flops, bytes_accessed=moved, transcendentals=flops // 1000)


def log_rows(value):
    high = value.astype(BF16).astype(F32)
    middle = (value - high).astype(BF16).astype(F32)
    low = value - high - middle
    line = lax.broadcasted_iota(jnp.int32, (LOG_ROWS, value.shape[1]), 0)
    rows = jnp.where(line == 0, high, jnp.where(line == 1, middle, jnp.where(line == 2, low, 0.0)))
    return rows.astype(BF16)


def log_row(rows):
    return jnp.sum(rows.astype(F32), axis=0, keepdims=True)


def turned(block, cosine, sine):
    return block * cosine + pltpu.roll(block, block.shape[1] // 2, 1) * sine


def summary_kernel(keys_ref, values_ref, log_ref, cos_ref, sin_ref, message_ref, turned_ref, total_ref):
    heads, count = log_ref.shape
    head_dim = cos_ref.shape[1]
    parts = message_ref.shape[0] // heads
    rows = head_dim // parts
    earlier = lax.broadcasted_iota(jnp.int32, (count, count), 0)
    upto = lax.broadcasted_iota(jnp.int32, (count, count), 1)
    ones = jnp.where(earlier <= upto, 1.0, 0.0).astype(F32)
    total = jnp.dot(
        log_ref[...], ones, precision=lax.Precision.HIGHEST, preferred_element_type=F32
    )
    total_ref[...] = total
    last = total[:, count - 1 :]
    trailing = jnp.exp(last - total)
    wide = jnp.broadcast_to(last, (heads, head_dim))
    for head in range(heads):
        lanes = slice(head * head_dim, (head + 1) * head_dim)
        keys = turned(keys_ref[:, lanes].astype(F32), cos_ref[...], sin_ref[...]).astype(BF16)
        turned_ref[:, lanes] = keys
        faded = keys.astype(F32).T * trailing[head : head + 1]
        coarse = faded.astype(BF16)
        fine = (faded - coarse.astype(F32)).astype(BF16)
        summary = dot32(coarse, values_ref[:, lanes]) + dot32(fine, values_ref[:, lanes])
        summary = summary.astype(BF16)
        logs = log_rows(wide[head : head + 1])
        for part in range(parts):
            message_ref[head * parts + part, :rows] = summary[part * rows : (part + 1) * rows]
            message_ref[head * parts + part, rows:] = logs


def inside_kernel(
    queries_ref, keys_ref, values_ref, total_ref, cos_ref, sin_ref, turned_ref, inside_ref, fade_ref
):
    heads, count = total_ref.shape
    head_dim = cos_ref.shape[1]
    row = lax.broadcasted_iota(jnp.int32, (count, count), 0)
    column = lax.broadcasted_iota(jnp.int32, (count, count), 1)
    causal = row >= column
    for head in range(heads):
        lanes = slice(head * head_dim, (head + 1) * head_dim)
        queries = turned(queries_ref[:, lanes].astype(F32), cos_ref[...], sin_ref[...])
        queries = (queries * head_dim ** (-0.5)).astype(BF16)
        turned_ref[:, lanes] = queries
        scores = lax.dot_general(
            queries, keys_ref[:, lanes], (((1,), (1,)), ((), ())), preferred_element_type=F32
        )
        here = total_ref[head : head + 1, :]
        down = jnp.broadcast_to(here, (head_dim, count)).T
        spread = jnp.where(causal, down - here, 0.0)
        weights = jnp.where(causal, scores * jnp.exp(spread), 0.0).astype(BF16)
        inside_ref[:, lanes] = dot32(weights, values_ref[:, lanes])
        fade_ref[:, lanes] = jnp.exp(down)


def plane_sum_kernel(arrived_ref, message_ref):
    plane, rows, head_dim = arrived_ref.shape
    rows = rows - LOG_ROWS
    total = jnp.zeros((rows, head_dim), F32)
    log_total = jnp.zeros((1, head_dim), F32)
    for block in range(plane):
        log = log_row(arrived_ref[block, rows:])
        total = jnp.exp(log) * total + arrived_ref[block, :rows].astype(F32)
        log_total = log_total + log
    total, logs = total.astype(BF16), log_rows(log_total)
    for z in range(message_ref.shape[0]):
        message_ref[z, :rows] = total
        message_ref[z, rows:] = logs


def entering_kernel(own_ref, arrived_ref, planes_ref, entering_ref):
    rows = entering_ref.shape[1]
    own = own_ref[0]
    state = jnp.zeros(entering_ref.shape[1:], F32)
    for z in range(planes_ref.shape[0]):
        log = log_row(planes_ref[z, rows:])
        later = jnp.exp(log) * state + planes_ref[z, :rows].astype(F32)
        state = jnp.where(z < own, later, state)
    for block in range(arrived_ref.shape[0]):
        entering_ref[block] = state.astype(BF16)
        log = log_row(arrived_ref[block, rows:])
        state = jnp.exp(log) * state + arrived_ref[block, :rows].astype(F32)


def outgoing_kernel(
    own_ref,
    state_ref,
    queries_ref,
    inside_ref,
    fade_ref,
    hidden_ref,
    group_gain_ref,
    norm_gain_ref,
    placing_ref,
    residual_ref,
    outgoing_ref,
    normed_ref,
    packed_ref,
):
    chunks, count, head_dim = normed_ref.shape
    square = jnp.zeros((count, 1), F32)
    for head in range(chunks):
        lanes = slice(head * head_dim, (head + 1) * head_dim)
        far = dot32(queries_ref[:, lanes], state_ref[head * head_dim : (head + 1) * head_dim, :])
        retrieved = inside_ref[:, lanes] + fade_ref[:, lanes] * far
        deviation = retrieved - jnp.mean(retrieved, axis=1, keepdims=True)
        variance = jnp.mean(deviation * deviation, axis=1, keepdims=True)
        normalized = deviation * lax.rsqrt(variance + 1e-05)
        residual = hidden_ref[:, lanes].astype(F32) + group_gain_ref[:, lanes] * normalized
        residual_ref[:, lanes] = residual
        square = square + jnp.sum(residual * residual, axis=1, keepdims=True)
    scale = lax.rsqrt(square * (1.0 / (chunks * head_dim)) + 1e-06)
    for chunk in range(chunks):
        lanes = slice(chunk * head_dim, (chunk + 1) * head_dim)
        normed = residual_ref[:, lanes] * scale * norm_gain_ref[:, lanes]
        normed_ref[own_ref[chunk]] = normed.astype(BF16)
    slots = placing_ref.shape[0]
    for chunk in range(chunks):
        packed_ref[pl.ds(chunk, slots, stride=chunks), :] = dot32(
            placing_ref[...], normed_ref[chunk]
        )
    outgoing_ref[...] = packed_ref[...].astype(BF16)


def combine_kernel(
    own_ref, returned_ref, first_ref, second_ref, weights_ref, residual_ref, out_ref, mixed_ref
):
    chunks, _, lanes_count = mixed_ref.shape
    for chunk in range(chunks):
        lanes = slice(chunk * lanes_count, (chunk + 1) * lanes_count)
        rows = returned_ref[:, lanes]
        mixed_ref[chunk] = weights_ref[:, :1] * dot32(first_ref[...], rows) + weights_ref[
            :, 1:
        ] * dot32(second_ref[...], rows)
    for chunk in range(chunks):
        lanes = slice(chunk * lanes_count, (chunk + 1) * lanes_count)
        out_ref[:, lanes] = (residual_ref[:, lanes] + mixed_ref[own_ref[chunk]]).astype(BF16)


def expert_kernel(*refs):
    arrived_ref, pieces, out_ref = refs[0], refs[1:-5], refs[-5]
    weights_ref, hidden_ref, packed_ref, sems = refs[-4:]
    width = weights_ref.shape[2]
    copies = []
    for index in range(3):
        start = 0
        for number, piece in enumerate(pieces):
            size = piece.shape[1]
            copy = pltpu.make_async_copy(
                piece.at[index],
                weights_ref.at[index, pl.ds(start, size), :],
                sems.at[index, number],
            )
            copy.start()
            copies.append(copy)
            start += size
    count = len(pieces)
    for copy in copies[: 2 * count]:
        copy.wait()
    tile = 512
    for start in range(0, width, tile):
        columns = slice(start, min(width, start + tile))
        gate = dot32(arrived_ref[...], weights_ref[0, :, columns])
        up = dot32(arrived_ref[...], weights_ref[1, :, columns])
        hidden_ref[:, columns] = (gate / (1.0 + jnp.exp(-gate)) * up).astype(BF16)
    for copy in copies[2 * count :]:
        copy.wait()
    rows, lanes = arrived_ref.shape[0], packed_ref.shape[1]
    chunks = packed_ref.shape[0] // rows
    for chunk in range(0, chunks, 2):
        pair = lax.dot_general(
            hidden_ref[...],
            weights_ref[2, chunk * lanes : (chunk + 2) * lanes, :],
            (((1,), (1,)), ((), ())),
            preferred_element_type=F32,
        )
        for side in range(2):
            packed_ref[pl.ds(chunk + side, rows, stride=chunks), :] = pair[
                :, side * lanes : (side + 1) * lanes
            ]
    out_ref[...] = packed_ref[...].astype(BF16)


def shape(dims, kind):
    return jax.ShapeDtypeStruct(dims, kind)


def vmem(mebibytes):
    return pltpu.CompilerParams(vmem_limit_bytes=mebibytes << 20)


def run_experts(arrived, pieces):
    rows, model_width = arrived.shape
    width = pieces[0].shape[2]
    anywhere = pl.BlockSpec(memory_space=pl.ANY)
    return pl.pallas_call(
        expert_kernel,
        name="experts",
        out_shape=shape((rows * model_width // LANES, LANES), BF16),
        in_specs=[pl.BlockSpec(memory_space=pltpu.VMEM)] + [anywhere] * len(pieces),
        out_specs=pl.BlockSpec(memory_space=pltpu.VMEM),
        scratch_shapes=[
            pltpu.VMEM((3, model_width, width), BF16),
            pltpu.VMEM((rows, width), BF16),
            pltpu.VMEM((rows * model_width // LANES, LANES), F32),
            pltpu.SemaphoreType.DMA((3, len(pieces))),
        ],
        cost_estimate=cost(6 * rows * model_width * width, 6 * model_width * width),
        compiler_params=vmem(20),
    )(arrived, *pieces)


def along_x(piece, step):
    size = lax.axis_size("x")
    return lax.ppermute(piece, "x", [(i, (i - step) % size) for i in range(size)])


def swapped(piece):
    return lax.ppermute(piece, "core", [(0, 1), (1, 0)])


def own_places():
    chips, cores = lax.axis_size("x"), lax.axis_size("core")
    chunk = jnp.arange(chips * cores, dtype=jnp.int32)
    chip = (chunk // cores + chips - lax.axis_index("x")) % chips
    return chip * cores + (chunk + lax.axis_index("core")) % cores


def body(
    hidden_in,
    queries,
    keys,
    values,
    log_decay,
    retention_gain,
    norm_gain,
    routes,
    route_weights,
    w_gate,
    w_up,
    w_down,
):
    tok_rows = hidden_in.shape[1]
    model_width = hidden_in.shape[2]
    head_count = log_decay.shape[2]
    head_dim = model_width // head_count
    wide = (tok_rows, model_width)
    plane, depth = lax.axis_size(PLANE), lax.axis_size("z")
    part_rows = head_count * head_dim // plane
    message = (plane, part_rows + LOG_ROWS, head_dim)

    half = head_dim // 2
    inverse = (10000.0 ** (-np.arange(half) / half)).astype(np.float32)
    sign = np.repeat(np.array([-1.0, 1.0], np.float32), half)
    block_index = lax.axis_index(CTX) * lax.axis_size(EXP) + lax.axis_index(EXP)
    position = block_index * tok_rows + jnp.arange(tok_rows, dtype=jnp.int32)
    angles = position.astype(F32)[:, None] * np.tile(inverse, 2)[None, :]
    cosine, sine = jnp.cos(angles), jnp.sin(angles) * sign

    out_message, turned_keys, total = pl.pallas_call(
        summary_kernel,
        name="summary",
        out_shape=(shape(message, BF16), shape(wide, BF16), shape((head_count, tok_rows), F32)),
        cost_estimate=cost(70000000, 1200000),
        compiler_params=vmem(6),
    )(keys[0], values[0], log_decay[0].T, cosine, sine)
    summaries = exchange(out_message, PLANE)
    stacked = jnp.stack([w_gate[0], w_up[0], w_down[0]])
    after, before = along_x(stacked, 1), along_x(stacked, -1)
    turned_queries, inside, fade = pl.pallas_call(
        inside_kernel,
        name="inside",
        out_shape=(shape(wide, BF16), shape(wide, F32), shape(wide, F32)),
        cost_estimate=cost(70000000, 2200000),
        compiler_params=vmem(8),
    )(queries[0], turned_keys, values[0], total, cosine, sine)
    sums = pl.pallas_call(
        plane_sum_kernel,
        name="plane_sum",
        out_shape=shape((depth,) + message[1:], BF16),
        cost_estimate=cost(500000, 600000),
        compiler_params=vmem(4),
    )(summaries)
    sums = exchange(sums, "z")
    own_other = swapped(stacked)
    entering = pl.pallas_call(
        entering_kernel,
        name="enter",
        out_shape=shape((plane, part_rows, head_dim), BF16),
        in_specs=[pl.BlockSpec(memory_space=pltpu.SMEM)]
        + [pl.BlockSpec(memory_space=pltpu.VMEM)] * 2,
        cost_estimate=cost(900000, 900000),
        compiler_params=vmem(4),
    )(lax.axis_index("z")[None], summaries, sums)
    state_in = exchange(entering, PLANE).reshape(model_width, head_dim)
    after_other, before_other = swapped(after), swapped(before)

    expert_count = lax.axis_size(OWNERS)
    top_count = routes.shape[2]
    capacity = (tok_rows * top_count * 5 + 4 * expert_count - 1) // (4 * expert_count)
    slot_count = expert_count * capacity
    route_rows = routes[0]
    expert_hits = (
        route_rows.reshape(tok_rows * top_count)[:, None]
        == jnp.arange(expert_count, dtype=jnp.int32)[None, :]
    ).astype(jnp.int32)
    earlier = jnp.cumsum(expert_hits, axis=0) - expert_hits
    slot_rank = jnp.sum(earlier * expert_hits, axis=1).reshape(tok_rows, top_count)
    destination = route_rows * capacity + slot_rank
    slot_lanes = jnp.arange(slot_count, dtype=jnp.int32)
    placing = jnp.any(destination[None, :, :] == slot_lanes[:, None, None], axis=2).astype(BF16)

    flat = (slot_count * model_width // LANES, LANES)
    places = own_places()
    residual, outgoing = pl.pallas_call(
        outgoing_kernel,
        name="outgoing",
        out_shape=(shape(wide, F32), shape(flat, BF16)),
        in_specs=[pl.BlockSpec(memory_space=pltpu.SMEM)]
        + [pl.BlockSpec(memory_space=pltpu.VMEM)] * 8,
        scratch_shapes=[
            pltpu.VMEM((head_count, tok_rows, head_dim), BF16),
            pltpu.VMEM(flat, F32),
        ],
        cost_estimate=cost(120000000, 3000000),
        compiler_params=vmem(10),
    )(
        places,
        state_in,
        turned_queries,
        inside,
        fade,
        hidden_in[0],
        retention_gain[None],
        norm_gain[None],
        placing,
    )
    packed = (expert_count, capacity * model_width // LANES, LANES)
    arrived = exchange(outgoing.reshape(packed), OWNERS).reshape(slot_count, model_width)
    cut = stacked.shape[1] // 2
    far = [along_x(after[:, :cut], 1), along_x(before[:, cut:], -1)]
    far_other = [swapped(piece) for piece in far]
    pieces = [stacked, own_other, after, after_other, *far, *far_other, before, before_other]
    expert_out = run_experts(arrived, pieces)
    returned = exchange(expert_out.reshape(packed), OWNERS).reshape(slot_count, model_width)
    picks = [
        (destination[:, index][:, None] == slot_lanes[None, :]).astype(BF16)
        for index in range(top_count)
    ]
    output = pl.pallas_call(
        combine_kernel,
        name="combine",
        out_shape=shape(wide, BF16),
        in_specs=[pl.BlockSpec(memory_space=pltpu.SMEM)]
        + [pl.BlockSpec(memory_space=pltpu.VMEM)] * 5,
        scratch_shapes=[pltpu.VMEM((head_count, tok_rows, head_dim), F32)],
        cost_estimate=cost(180000000, 2000000),
        compiler_params=vmem(8),
    )(places, returned, *picks, route_weights[0], residual)
    return output[None]


def solution(mesh):
    ctx, exp, dp = mesh.shape["ctx"], mesh.shape["exp"], mesh.shape["dp"]
    split = Mesh(
        mesh.devices.reshape(ctx // 2, 2, exp // 2, 2, dp), ("z", "ylo", "x", "core", "yhi")
    )
    tokens = P("yhi", CTX + EXP, None)
    experts = P(OWNERS, EXP, None)
    in_specs = (tokens,) * 5 + (P(), P()) + (tokens,) * 2 + (experts,) * 3
    return jax.shard_map(body, mesh=split, in_specs=in_specs, out_specs=tokens, check_vma=False)
```

```python
import jax
import jax.numpy as jnp
import numpy as np
from jax import lax
from jax.experimental import pallas as pl
from jax.experimental.pallas import tpu as pltpu
from jax.sharding import Mesh, PartitionSpec as P

CTX = ("z", "ylo")
EXP = ("x", "core")
PLANE = ("ylo", "x", "core")
OWNERS = ("z", "ylo", "yhi")
LOG_ROWS = 8
LANES = 128
TILE = 512
F32, BF16 = jnp.float32, jnp.bfloat16


def exchange(blocks, axes):
    return lax.all_to_all(blocks, axes, split_axis=0, concat_axis=0, tiled=True)


def dot32(left, right):
    return jnp.dot(left, right, preferred_element_type=F32)


def cost(flops, moved):
    return pl.CostEstimate(flops=flops, bytes_accessed=moved, transcendentals=flops // 1000)


def log_rows(value):
    high = value.astype(BF16).astype(F32)
    middle = (value - high).astype(BF16).astype(F32)
    low = value - high - middle
    line = lax.broadcasted_iota(jnp.int32, (LOG_ROWS, value.shape[1]), 0)
    rows = jnp.where(line == 0, high, jnp.where(line == 1, middle, jnp.where(line == 2, low, 0.0)))
    return rows.astype(BF16)


def log_row(rows):
    return jnp.sum(rows.astype(F32), axis=0, keepdims=True)


def turned(block, cosine, sine):
    return block * cosine + pltpu.roll(block, block.shape[1] // 2, 1) * sine


def summary_kernel(keys_ref, values_ref, log_ref, cos_ref, sin_ref, message_ref, total_ref):
    heads, count = log_ref.shape
    head_dim = cos_ref.shape[1]
    parts = message_ref.shape[0] // heads
    rows = head_dim // parts
    earlier = lax.broadcasted_iota(jnp.int32, (count, count), 0)
    upto = lax.broadcasted_iota(jnp.int32, (count, count), 1)
    ones = jnp.where(earlier <= upto, 1.0, 0.0).astype(F32)
    total = jnp.dot(
        log_ref[...], ones, precision=lax.Precision.HIGHEST, preferred_element_type=F32
    )
    total_ref[...] = total
    last = total[:, count - 1 :]
    trailing = jnp.exp(last - total)
    wide = jnp.broadcast_to(last, (heads, head_dim))
    for head in range(heads):
        lanes = slice(head * head_dim, (head + 1) * head_dim)
        keys = turned(keys_ref[:, lanes].astype(F32), cos_ref[...], sin_ref[...]).astype(BF16)
        faded = keys.astype(F32).T * trailing[head : head + 1]
        coarse = faded.astype(BF16)
        fine = (faded - coarse.astype(F32)).astype(BF16)
        summary = dot32(coarse, values_ref[:, lanes]) + dot32(fine, values_ref[:, lanes])
        summary = summary.astype(BF16)
        logs = log_rows(wide[head : head + 1])
        for part in range(parts):
            message_ref[head * parts + part, :rows] = summary[part * rows : (part + 1) * rows]
            message_ref[head * parts + part, rows:] = logs


def inside_kernel(
    queries_ref, keys_ref, values_ref, total_ref, cos_ref, sin_ref, turned_ref, inside_ref, fade_ref
):
    heads, count = total_ref.shape
    head_dim = cos_ref.shape[1]
    row = lax.broadcasted_iota(jnp.int32, (count, count), 0)
    column = lax.broadcasted_iota(jnp.int32, (count, count), 1)
    causal = row >= column
    for head in range(heads):
        lanes = slice(head * head_dim, (head + 1) * head_dim)
        queries = turned(queries_ref[:, lanes].astype(F32), cos_ref[...], sin_ref[...])
        queries = (queries * head_dim ** (-0.5)).astype(BF16)
        turned_ref[:, lanes] = queries
        keys = turned(keys_ref[:, lanes].astype(F32), cos_ref[...], sin_ref[...]).astype(BF16)
        scores = lax.dot_general(
            queries, keys, (((1,), (1,)), ((), ())), preferred_element_type=F32
        )
        here = total_ref[head : head + 1, :]
        down = jnp.broadcast_to(here, (head_dim, count)).T
        spread = jnp.where(causal, down - here, 0.0)
        weights = jnp.where(causal, scores * jnp.exp(spread), 0.0).astype(BF16)
        inside_ref[:, lanes] = dot32(weights, values_ref[:, lanes])
        fade_ref[:, lanes] = jnp.exp(down)


def plane_sum_kernel(arrived_ref, message_ref):
    plane, rows, head_dim = arrived_ref.shape
    rows = rows - LOG_ROWS
    total = jnp.zeros((rows, head_dim), F32)
    log_total = jnp.zeros((1, head_dim), F32)
    for block in range(plane):
        log = log_row(arrived_ref[block, rows:])
        total = jnp.exp(log) * total + arrived_ref[block, :rows].astype(F32)
        log_total = log_total + log
    total, logs = total.astype(BF16), log_rows(log_total)
    for z in range(message_ref.shape[0]):
        message_ref[z, :rows] = total
        message_ref[z, rows:] = logs


def entering_kernel(own_ref, arrived_ref, planes_ref, entering_ref):
    rows = entering_ref.shape[1]
    own = own_ref[0]
    state = jnp.zeros(entering_ref.shape[1:], F32)
    for z in range(planes_ref.shape[0]):
        log = log_row(planes_ref[z, rows:])
        later = jnp.exp(log) * state + planes_ref[z, :rows].astype(F32)
        state = jnp.where(z < own, later, state)
    for block in range(arrived_ref.shape[0]):
        entering_ref[block] = state.astype(BF16)
        log = log_row(arrived_ref[block, rows:])
        state = jnp.exp(log) * state + arrived_ref[block, :rows].astype(F32)


def outgoing_kernel(
    own_ref,
    state_ref,
    queries_ref,
    inside_ref,
    fade_ref,
    hidden_ref,
    group_gain_ref,
    norm_gain_ref,
    placing_ref,
    residual_ref,
    outgoing_ref,
    normed_ref,
    packed_ref,
):
    chunks, count, head_dim = normed_ref.shape
    square = jnp.zeros((count, 1), F32)
    for head in range(chunks):
        lanes = slice(head * head_dim, (head + 1) * head_dim)
        far = dot32(queries_ref[:, lanes], state_ref[head * head_dim : (head + 1) * head_dim, :])
        retrieved = inside_ref[:, lanes] + fade_ref[:, lanes] * far
        deviation = retrieved - jnp.mean(retrieved, axis=1, keepdims=True)
        variance = jnp.mean(deviation * deviation, axis=1, keepdims=True)
        normalized = deviation * lax.rsqrt(variance + 1e-05)
        residual = hidden_ref[:, lanes].astype(F32) + group_gain_ref[:, lanes] * normalized
        residual_ref[:, lanes] = residual
        square = square + jnp.sum(residual * residual, axis=1, keepdims=True)
    scale = lax.rsqrt(square * (1.0 / (chunks * head_dim)) + 1e-06)
    for chunk in range(chunks):
        lanes = slice(chunk * head_dim, (chunk + 1) * head_dim)
        normed = residual_ref[:, lanes] * scale * norm_gain_ref[:, lanes]
        normed_ref[own_ref[chunk]] = normed.astype(BF16)
    slots = placing_ref.shape[0]
    for chunk in range(chunks):
        packed_ref[pl.ds(chunk, slots, stride=chunks), :] = dot32(
            placing_ref[...], normed_ref[chunk]
        )
    outgoing_ref[...] = packed_ref[...].astype(BF16)


def combine_kernel(
    own_ref, returned_ref, first_ref, second_ref, weights_ref, residual_ref, out_ref, mixed_ref
):
    chunks, _, lanes_count = mixed_ref.shape
    for chunk in range(chunks):
        lanes = slice(chunk * lanes_count, (chunk + 1) * lanes_count)
        rows = returned_ref[:, lanes]
        mixed_ref[chunk] = weights_ref[:, :1] * dot32(first_ref[...], rows) + weights_ref[
            :, 1:
        ] * dot32(second_ref[...], rows)
    for chunk in range(chunks):
        lanes = slice(chunk * lanes_count, (chunk + 1) * lanes_count)
        out_ref[:, lanes] = (residual_ref[:, lanes] + mixed_ref[own_ref[chunk]]).astype(BF16)


def expert_kernel(*refs):
    arrived_ref, pieces, out_ref = refs[0], refs[1:-5], refs[-5]
    weights_ref, hidden_ref, packed_ref, sems = refs[-4:]
    width = weights_ref.shape[2]
    tiles = [slice(start, min(width, start + TILE)) for start in range(0, width, TILE)]
    groups = [[(index, tile) for index in range(2)] for tile in tiles] + [[(2, slice(0, width))]]
    copies = [[] for _ in groups]
    for group, (members, started) in enumerate(zip(groups, copies)):
        for index, columns in members:
            start = 0
            for number, piece in enumerate(pieces):
                size = piece.shape[1]
                copy = pltpu.make_async_copy(
                    piece.at[index, :, columns],
                    weights_ref.at[index, start : start + size, columns],
                    sems.at[group, index, number],
                )
                copy.start()
                started.append(copy)
                start += size
    for columns, started in zip(tiles, copies):
        for copy in started:
            copy.wait()
        gate = dot32(arrived_ref[...], weights_ref[0, :, columns])
        up = dot32(arrived_ref[...], weights_ref[1, :, columns])
        hidden_ref[:, columns] = (gate / (1.0 + jnp.exp(-gate)) * up).astype(BF16)
    for copy in copies[-1]:
        copy.wait()
    rows, lanes = arrived_ref.shape[0], packed_ref.shape[1]
    chunks = packed_ref.shape[0] // rows
    for chunk in range(0, chunks, 2):
        pair = lax.dot_general(
            hidden_ref[...],
            weights_ref[2, chunk * lanes : (chunk + 2) * lanes, :],
            (((1,), (1,)), ((), ())),
            preferred_element_type=F32,
        )
        for side in range(2):
            packed_ref[pl.ds(chunk + side, rows, stride=chunks), :] = pair[
                :, side * lanes : (side + 1) * lanes
            ]
    out_ref[...] = packed_ref[...].astype(BF16)


def shape(dims, kind):
    return jax.ShapeDtypeStruct(dims, kind)


def vmem(mebibytes):
    return pltpu.CompilerParams(vmem_limit_bytes=mebibytes << 20)


def run_experts(arrived, pieces):
    rows, model_width = arrived.shape
    width = pieces[0].shape[2]
    anywhere = pl.BlockSpec(memory_space=pl.ANY)
    return pl.pallas_call(
        expert_kernel,
        name="experts",
        out_shape=shape((rows * model_width // LANES, LANES), BF16),
        in_specs=[pl.BlockSpec(memory_space=pltpu.VMEM)] + [anywhere] * len(pieces),
        out_specs=pl.BlockSpec(memory_space=pltpu.VMEM),
        scratch_shapes=[
            pltpu.VMEM((3, model_width, width), BF16),
            pltpu.VMEM((rows, width), BF16),
            pltpu.VMEM((rows * model_width // LANES, LANES), F32),
            pltpu.SemaphoreType.DMA((-(-width // TILE) + 1, 3, len(pieces))),
        ],
        cost_estimate=cost(6 * rows * model_width * width, 6 * model_width * width),
        compiler_params=vmem(20),
    )(arrived, *pieces)


def along_x(piece, step):
    size = lax.axis_size("x")
    return lax.ppermute(piece, "x", [(i, (i - step) % size) for i in range(size)])


def swapped(piece):
    return lax.ppermute(piece, "core", [(0, 1), (1, 0)])


def own_places():
    chips, cores = lax.axis_size("x"), lax.axis_size("core")
    chunk = jnp.arange(chips * cores, dtype=jnp.int32)
    chip = (chunk // cores + chips - lax.axis_index("x")) % chips
    return chip * cores + (chunk + lax.axis_index("core")) % cores


def body(
    hidden_in,
    queries,
    keys,
    values,
    log_decay,
    retention_gain,
    norm_gain,
    routes,
    route_weights,
    w_gate,
    w_up,
    w_down,
):
    tok_rows = hidden_in.shape[1]
    model_width = hidden_in.shape[2]
    head_count = log_decay.shape[2]
    head_dim = model_width // head_count
    wide = (tok_rows, model_width)
    plane, depth = lax.axis_size(PLANE), lax.axis_size("z")
    part_rows = head_count * head_dim // plane
    message = (plane, part_rows + LOG_ROWS, head_dim)

    half = head_dim // 2
    inverse = (10000.0 ** (-np.arange(half) / half)).astype(np.float32)
    sign = np.repeat(np.array([-1.0, 1.0], np.float32), half)
    block_index = lax.axis_index(CTX) * lax.axis_size(EXP) + lax.axis_index(EXP)
    position = block_index * tok_rows + jnp.arange(tok_rows, dtype=jnp.int32)
    angles = position.astype(F32)[:, None] * np.tile(inverse, 2)[None, :]
    cosine, sine = jnp.cos(angles), jnp.sin(angles) * sign

    out_message, total = pl.pallas_call(
        summary_kernel,
        name="summary",
        out_shape=(shape(message, BF16), shape((head_count, tok_rows), F32)),
        cost_estimate=cost(70000000, 1200000),
    )(keys[0], values[0], log_decay[0].T, cosine, sine)
    summaries = exchange(out_message, PLANE)
    stacked = jnp.stack([w_gate[0], w_up[0], w_down[0]])
    after = along_x(stacked, 1)
    before = along_x(stacked, -1)
    turned_queries, inside, fade = pl.pallas_call(
        inside_kernel,
        name="inside",
        out_shape=(shape(wide, BF16), shape(wide, F32), shape(wide, F32)),
        cost_estimate=cost(70000000, 2200000),
        compiler_params=vmem(8),
    )(queries[0], keys[0], values[0], total, cosine, sine)
    sums = pl.pallas_call(
        plane_sum_kernel,
        name="plane_sum",
        out_shape=shape((depth,) + message[1:], BF16),
        cost_estimate=cost(500000, 600000),
        compiler_params=vmem(4),
    )(summaries)
    sums = exchange(sums, "z")
    own_other = swapped(stacked)
    entering = pl.pallas_call(
        entering_kernel,
        name="enter",
        out_shape=shape((plane, part_rows, head_dim), BF16),
        in_specs=[pl.BlockSpec(memory_space=pltpu.SMEM)]
        + [pl.BlockSpec(memory_space=pltpu.VMEM)] * 2,
        cost_estimate=cost(900000, 900000),
        compiler_params=vmem(4),
    )(lax.axis_index("z")[None], summaries, sums)
    state_in = exchange(entering, PLANE).reshape(model_width, head_dim)
    after_other, before_other = swapped(after), swapped(before)

    expert_count = lax.axis_size(OWNERS)
    top_count = routes.shape[2]
    capacity = (tok_rows * top_count * 5 + 4 * expert_count - 1) // (4 * expert_count)
    slot_count = expert_count * capacity
    route_rows = routes[0]
    expert_hits = (
        route_rows.reshape(tok_rows * top_count)[:, None]
        == jnp.arange(expert_count, dtype=jnp.int32)[None, :]
    ).astype(jnp.int32)
    earlier = jnp.cumsum(expert_hits, axis=0) - expert_hits
    slot_rank = jnp.sum(earlier * expert_hits, axis=1).reshape(tok_rows, top_count)
    destination = route_rows * capacity + slot_rank
    slot_lanes = jnp.arange(slot_count, dtype=jnp.int32)
    placing = jnp.any(destination[None, :, :] == slot_lanes[:, None, None], axis=2).astype(BF16)

    flat = (slot_count * model_width // LANES, LANES)
    places = own_places()
    residual, outgoing = pl.pallas_call(
        outgoing_kernel,
        name="outgoing",
        out_shape=(shape(wide, F32), shape(flat, BF16)),
        in_specs=[pl.BlockSpec(memory_space=pltpu.SMEM)]
        + [pl.BlockSpec(memory_space=pltpu.VMEM)] * 8,
        scratch_shapes=[
            pltpu.VMEM((head_count, tok_rows, head_dim), BF16),
            pltpu.VMEM(flat, F32),
        ],
        cost_estimate=cost(120000000, 3000000),
        compiler_params=vmem(10),
    )(
        places,
        state_in,
        turned_queries,
        inside,
        fade,
        hidden_in[0],
        retention_gain[None],
        norm_gain[None],
        placing,
    )
    packed = (expert_count, capacity * model_width // LANES, LANES)
    arrived = exchange(outgoing.reshape(packed), OWNERS).reshape(slot_count, model_width)
    cut = stacked.shape[1] // 2
    far = [along_x(after[:, :cut], 1), along_x(before[:, cut:], -1)]
    far_other = [swapped(piece) for piece in far]
    pieces = [stacked, own_other, after, after_other, *far, *far_other, before, before_other]
    expert_out = run_experts(arrived, pieces)
    returned = exchange(expert_out.reshape(packed), OWNERS).reshape(slot_count, model_width)
    picks = [
        (destination[:, index][:, None] == slot_lanes[None, :]).astype(BF16)
        for index in range(top_count)
    ]
    output = pl.pallas_call(
        combine_kernel,
        name="combine",
        out_shape=shape(wide, BF16),
        in_specs=[pl.BlockSpec(memory_space=pltpu.SMEM)]
        + [pl.BlockSpec(memory_space=pltpu.VMEM)] * 5,
        scratch_shapes=[pltpu.VMEM((head_count, tok_rows, head_dim), F32)],
        cost_estimate=cost(180000000, 2000000),
        compiler_params=vmem(8),
    )(places, returned, *picks, route_weights[0], residual)
    return output[None]


def solution(mesh):
    ctx, exp, dp = mesh.shape["ctx"], mesh.shape["exp"], mesh.shape["dp"]
    split = Mesh(
        mesh.devices.reshape(ctx // 2, 2, exp // 2, 2, dp), ("z", "ylo", "x", "core", "yhi")
    )
    tokens = P("yhi", CTX + EXP, None)
    experts = P(OWNERS, EXP, None)
    in_specs = (tokens,) * 5 + (P(), P()) + (tokens,) * 2 + (experts,) * 3
    return jax.shard_map(body, mesh=split, in_specs=in_specs, out_specs=tokens, check_vma=False)
```

```python
import jax
import jax.numpy as jnp
import numpy as np
from jax import lax
from jax.experimental import pallas as pl
from jax.experimental.pallas import tpu as pltpu
from jax.sharding import Mesh, PartitionSpec as P

CTX = ("z", "ylo")
EXP = ("x", "core")
PLANE = ("ylo", "x", "core")
OWNERS = ("z", "ylo", "yhi")
LOG_ROWS = 8
LANES = 128
TILE = 512
F32, BF16 = jnp.float32, jnp.bfloat16


def exchange(blocks, axes):
    return lax.all_to_all(blocks, axes, split_axis=0, concat_axis=0, tiled=True)


def dot32(left, right):
    return jnp.dot(left, right, preferred_element_type=F32)


def cost(flops, moved):
    return pl.CostEstimate(flops=flops, bytes_accessed=moved, transcendentals=flops // 1000)


def log_rows(value):
    high = value.astype(BF16).astype(F32)
    middle = (value - high).astype(BF16).astype(F32)
    low = value - high - middle
    line = lax.broadcasted_iota(jnp.int32, (LOG_ROWS, value.shape[1]), 0)
    rows = jnp.where(line == 0, high, jnp.where(line == 1, middle, jnp.where(line == 2, low, 0.0)))
    return rows.astype(BF16)


def log_row(rows):
    return jnp.sum(rows.astype(F32), axis=0, keepdims=True)


def turned(block, cosine, sine):
    return block * cosine + pltpu.roll(block, block.shape[1] // 2, 1) * sine


def summary_kernel(
    keys_ref,
    values_ref,
    log_ref,
    cos_ref,
    sin_ref,
    gate_hbm,
    up_hbm,
    down_hbm,
    message_ref,
    total_ref,
    stacked_hbm,
    shard_ref,
    in_sems,
    out_sems,
):
    shards = (gate_hbm, up_hbm, down_hbm)
    loads = [
        pltpu.make_async_copy(shard, shard_ref.at[index], in_sems.at[index])
        for index, shard in enumerate(shards)
    ]
    stores = [
        pltpu.make_async_copy(shard_ref.at[index], stacked_hbm.at[index], out_sems.at[index])
        for index in range(len(shards))
    ]
    for load in loads:
        load.start()
    heads, count = log_ref.shape
    head_dim = cos_ref.shape[1]
    parts = message_ref.shape[0] // heads
    rows = head_dim // parts
    earlier = lax.broadcasted_iota(jnp.int32, (count, count), 0)
    upto = lax.broadcasted_iota(jnp.int32, (count, count), 1)
    ones = jnp.where(earlier <= upto, 1.0, 0.0).astype(F32)
    total = jnp.dot(
        log_ref[...], ones, precision=lax.Precision.HIGHEST, preferred_element_type=F32
    )
    total_ref[...] = total
    last = total[:, count - 1 :]
    trailing = jnp.exp(last - total)
    wide = jnp.broadcast_to(last, (heads, head_dim))
    for head in range(heads):
        if head == heads // 2:
            for load, store in zip(loads, stores):
                load.wait()
                store.start()
        lanes = slice(head * head_dim, (head + 1) * head_dim)
        keys = turned(keys_ref[:, lanes].astype(F32), cos_ref[...], sin_ref[...]).astype(BF16)
        faded = keys.astype(F32).T * trailing[head : head + 1]
        coarse = faded.astype(BF16)
        fine = (faded - coarse.astype(F32)).astype(BF16)
        summary = dot32(coarse, values_ref[:, lanes]) + dot32(fine, values_ref[:, lanes])
        summary = summary.astype(BF16)
        logs = log_rows(wide[head : head + 1])
        for part in range(parts):
            message_ref[head * parts + part, :rows] = summary[part * rows : (part + 1) * rows]
            message_ref[head * parts + part, rows:] = logs
    for store in stores:
        store.wait()


def inside_kernel(
    queries_ref, keys_ref, values_ref, total_ref, cos_ref, sin_ref, turned_ref, inside_ref, fade_ref
):
    heads, count = total_ref.shape
    head_dim = cos_ref.shape[1]
    row = lax.broadcasted_iota(jnp.int32, (count, count), 0)
    column = lax.broadcasted_iota(jnp.int32, (count, count), 1)
    causal = row >= column
    fade = jnp.zeros((count, count), F32)
    for head in range(heads):
        lanes = slice(head * head_dim, (head + 1) * head_dim)
        queries = turned(queries_ref[:, lanes].astype(F32), cos_ref[...], sin_ref[...])
        queries = (queries * head_dim ** (-0.5)).astype(BF16)
        turned_ref[:, lanes] = queries
        keys = turned(keys_ref[:, lanes].astype(F32), cos_ref[...], sin_ref[...]).astype(BF16)
        scores = lax.dot_general(
            queries, keys, (((1,), (1,)), ((), ())), preferred_element_type=F32
        )
        here = total_ref[head : head + 1, :]
        down = jnp.broadcast_to(here, (head_dim, count)).T
        spread = jnp.where(causal, down - here, 0.0)
        weights = jnp.where(causal, scores * jnp.exp(spread), 0.0).astype(BF16)
        inside_ref[:, lanes] = dot32(weights, values_ref[:, lanes])
        fade = jnp.where(column == head, jnp.exp(down), fade)
    fade_ref[...] = fade


def plane_sum_kernel(arrived_ref, message_ref):
    plane, rows, head_dim = arrived_ref.shape
    rows = rows - LOG_ROWS
    total = jnp.zeros((rows, head_dim), F32)
    log_total = jnp.zeros((1, head_dim), F32)
    for block in range(plane):
        log = log_row(arrived_ref[block, rows:])
        total = jnp.exp(log) * total + arrived_ref[block, :rows].astype(F32)
        log_total = log_total + log
    total, logs = total.astype(BF16), log_rows(log_total)
    for z in range(message_ref.shape[0]):
        message_ref[z, :rows] = total
        message_ref[z, rows:] = logs


def entering_kernel(own_ref, arrived_ref, planes_ref, entering_ref):
    rows = entering_ref.shape[1]
    own = own_ref[0]
    state = jnp.zeros(entering_ref.shape[1:], F32)
    for z in range(planes_ref.shape[0]):
        log = log_row(planes_ref[z, rows:])
        later = jnp.exp(log) * state + planes_ref[z, :rows].astype(F32)
        state = jnp.where(z < own, later, state)
    for block in range(arrived_ref.shape[0]):
        entering_ref[block] = state.astype(BF16)
        log = log_row(arrived_ref[block, rows:])
        state = jnp.exp(log) * state + arrived_ref[block, :rows].astype(F32)


def outgoing_kernel(
    own_ref,
    state_ref,
    queries_ref,
    inside_ref,
    fade_ref,
    hidden_ref,
    group_gain_ref,
    norm_gain_ref,
    placing_ref,
    residual_ref,
    outgoing_ref,
    normed_ref,
    packed_ref,
):
    chunks, count, head_dim = normed_ref.shape
    square = jnp.zeros((count, 1), F32)
    for head in range(chunks):
        lanes = slice(head * head_dim, (head + 1) * head_dim)
        far = dot32(queries_ref[:, lanes], state_ref[head * head_dim : (head + 1) * head_dim, :])
        retrieved = inside_ref[:, lanes] + fade_ref[:, head : head + 1] * far
        deviation = retrieved - jnp.mean(retrieved, axis=1, keepdims=True)
        variance = jnp.mean(deviation * deviation, axis=1, keepdims=True)
        normalized = deviation * lax.rsqrt(variance + 1e-05)
        residual = hidden_ref[:, lanes].astype(F32) + group_gain_ref[:, lanes] * normalized
        residual_ref[:, lanes] = residual
        square = square + jnp.sum(residual * residual, axis=1, keepdims=True)
    scale = lax.rsqrt(square * (1.0 / (chunks * head_dim)) + 1e-06)
    for chunk in range(chunks):
        lanes = slice(chunk * head_dim, (chunk + 1) * head_dim)
        normed = residual_ref[:, lanes] * scale * norm_gain_ref[:, lanes]
        normed_ref[own_ref[chunk]] = normed.astype(BF16)
    slots = placing_ref.shape[0]
    for chunk in range(chunks):
        packed_ref[pl.ds(chunk, slots, stride=chunks), :] = dot32(
            placing_ref[...], normed_ref[chunk]
        )
    outgoing_ref[...] = packed_ref[...].astype(BF16)


def combine_kernel(
    own_ref, returned_ref, first_ref, second_ref, weights_ref, residual_ref, out_ref, mixed_ref
):
    chunks, _, lanes_count = mixed_ref.shape
    for chunk in range(chunks):
        lanes = slice(chunk * lanes_count, (chunk + 1) * lanes_count)
        rows = returned_ref[:, lanes]
        mixed_ref[chunk] = weights_ref[:, :1] * dot32(first_ref[...], rows) + weights_ref[
            :, 1:
        ] * dot32(second_ref[...], rows)
    for chunk in range(chunks):
        lanes = slice(chunk * lanes_count, (chunk + 1) * lanes_count)
        out_ref[:, lanes] = (residual_ref[:, lanes] + mixed_ref[own_ref[chunk]]).astype(BF16)


def expert_kernel(*refs):
    arrived_ref, pieces, out_ref = refs[0], refs[1:-5], refs[-5]
    weights_ref, hidden_ref, packed_ref, sems = refs[-4:]
    width = weights_ref.shape[2]
    copies = [[] for _ in range(3)]
    for index in range(3):
        start = 0
        for number, piece in enumerate(pieces):
            size = piece.shape[1]
            copy = pltpu.make_async_copy(
                piece.at[index],
                weights_ref.at[index, start : start + size, :],
                sems.at[index, number],
            )
            copy.start()
            copies[index].append(copy)
            start += size
    for copy in copies[0]:
        copy.wait()
    for start in range(0, width, TILE):
        columns = slice(start, min(width, start + TILE))
        gate = dot32(arrived_ref[...], weights_ref[0, :, columns])
        if start == 0:
            for copy in copies[1]:
                copy.wait()
        up = dot32(arrived_ref[...], weights_ref[1, :, columns])
        hidden_ref[:, columns] = (gate / (1.0 + jnp.exp(-gate)) * up).astype(BF16)
    for copy in copies[2]:
        copy.wait()
    rows, lanes = arrived_ref.shape[0], packed_ref.shape[1]
    chunks = packed_ref.shape[0] // rows
    for chunk in range(0, chunks, 2):
        pair = lax.dot_general(
            hidden_ref[...],
            weights_ref[2, chunk * lanes : (chunk + 2) * lanes, :],
            (((1,), (1,)), ((), ())),
            preferred_element_type=F32,
        )
        for side in range(2):
            packed_ref[pl.ds(chunk + side, rows, stride=chunks), :] = pair[
                :, side * lanes : (side + 1) * lanes
            ]
    out_ref[...] = packed_ref[...].astype(BF16)


def shape(dims, kind):
    return jax.ShapeDtypeStruct(dims, kind)


def vmem(mebibytes):
    return pltpu.CompilerParams(vmem_limit_bytes=mebibytes << 20)


def run_experts(arrived, pieces):
    rows, model_width = arrived.shape
    width = pieces[0].shape[2]
    anywhere = pl.BlockSpec(memory_space=pl.ANY)
    return pl.pallas_call(
        expert_kernel,
        name="experts",
        out_shape=shape((rows * model_width // LANES, LANES), BF16),
        in_specs=[pl.BlockSpec(memory_space=pltpu.VMEM)] + [anywhere] * len(pieces),
        out_specs=pl.BlockSpec(memory_space=pltpu.VMEM),
        scratch_shapes=[
            pltpu.VMEM((3, model_width, width), BF16),
            pltpu.VMEM((rows, width), BF16),
            pltpu.VMEM((rows * model_width // LANES, LANES), F32),
            pltpu.SemaphoreType.DMA((3, len(pieces))),
        ],
        cost_estimate=cost(6 * rows * model_width * width, 6 * model_width * width),
        compiler_params=vmem(20),
    )(arrived, *pieces)


def along_x(piece, step):
    size = lax.axis_size("x")
    return lax.ppermute(piece, "x", [(i, (i - step) % size) for i in range(size)])


def swapped(piece):
    return lax.ppermute(piece, "core", [(0, 1), (1, 0)])


def own_places():
    chips, cores = lax.axis_size("x"), lax.axis_size("core")
    chunk = jnp.arange(chips * cores, dtype=jnp.int32)
    chip = (chunk // cores + chips - lax.axis_index("x")) % chips
    return chip * cores + (chunk + lax.axis_index("core")) % cores


def body(
    hidden_in,
    queries,
    keys,
    values,
    log_decay,
    retention_gain,
    norm_gain,
    routes,
    route_weights,
    w_gate,
    w_up,
    w_down,
):
    tok_rows = hidden_in.shape[1]
    model_width = hidden_in.shape[2]
    head_count = log_decay.shape[2]
    head_dim = model_width // head_count
    wide = (tok_rows, model_width)
    plane, depth = lax.axis_size(PLANE), lax.axis_size("z")
    part_rows = head_count * head_dim // plane
    message = (plane, part_rows + LOG_ROWS, head_dim)

    half = head_dim // 2
    inverse = (10000.0 ** (-np.arange(half) / half)).astype(np.float32)
    sign = np.repeat(np.array([-1.0, 1.0], np.float32), half)
    block_index = lax.axis_index(CTX) * lax.axis_size(EXP) + lax.axis_index(EXP)
    position = block_index * tok_rows + jnp.arange(tok_rows, dtype=jnp.int32)
    angles = position.astype(F32)[:, None] * np.tile(inverse, 2)[None, :]
    cosine, sine = jnp.cos(angles), jnp.sin(angles) * sign

    shards = (3,) + w_gate.shape[1:]
    any_space, in_vmem = pl.BlockSpec(memory_space=pl.ANY), pl.BlockSpec(memory_space=pltpu.VMEM)
    out_message, total, stacked = pl.pallas_call(
        summary_kernel,
        name="summary",
        out_shape=(
            shape(message, BF16),
            shape((head_count, tok_rows), F32),
            shape(shards, BF16),
        ),
        in_specs=[in_vmem] * 5 + [any_space] * 3,
        out_specs=(in_vmem, in_vmem, any_space),
        scratch_shapes=[
            pltpu.VMEM(shards, BF16),
            pltpu.SemaphoreType.DMA((3,)),
            pltpu.SemaphoreType.DMA((3,)),
        ],
        cost_estimate=cost(70000000, 3200000),
    )(keys[0], values[0], log_decay[0].T, cosine, sine, w_gate[0], w_up[0], w_down[0])
    summaries = exchange(out_message, PLANE)
    after, before = along_x(stacked, 1), along_x(stacked, -1)
    turned_queries, inside, fade = pl.pallas_call(
        inside_kernel,
        name="inside",
        out_shape=(shape(wide, BF16), shape(wide, F32), shape((tok_rows, tok_rows), F32)),
        cost_estimate=cost(70000000, 2200000),
        compiler_params=vmem(8),
    )(queries[0], keys[0], values[0], total, cosine, sine)
    sums = pl.pallas_call(
        plane_sum_kernel,
        name="plane_sum",
        out_shape=shape((depth,) + message[1:], BF16),
        cost_estimate=cost(500000, 600000),
        compiler_params=vmem(4),
    )(summaries)
    sums = exchange(sums, "z")
    own_other = swapped(stacked)
    entering = pl.pallas_call(
        entering_kernel,
        name="enter",
        out_shape=shape((plane, part_rows, head_dim), BF16),
        in_specs=[pl.BlockSpec(memory_space=pltpu.SMEM)]
        + [pl.BlockSpec(memory_space=pltpu.VMEM)] * 2,
        cost_estimate=cost(900000, 900000),
        compiler_params=vmem(4),
    )(lax.axis_index("z")[None], summaries, sums)
    state_in = exchange(entering, PLANE).reshape(model_width, head_dim)
    after_other, before_other = swapped(after), swapped(before)

    expert_count = lax.axis_size(OWNERS)
    top_count = routes.shape[2]
    capacity = (tok_rows * top_count * 5 + 4 * expert_count - 1) // (4 * expert_count)
    slot_count = expert_count * capacity
    route_rows = routes[0]
    expert_hits = (
        route_rows.reshape(tok_rows * top_count)[:, None]
        == jnp.arange(expert_count, dtype=jnp.int32)[None, :]
    ).astype(jnp.int32)
    earlier = jnp.cumsum(expert_hits, axis=0) - expert_hits
    slot_rank = jnp.sum(earlier * expert_hits, axis=1).reshape(tok_rows, top_count)
    destination = route_rows * capacity + slot_rank
    slot_lanes = jnp.arange(slot_count, dtype=jnp.int32)
    placing = jnp.any(destination[None, :, :] == slot_lanes[:, None, None], axis=2).astype(BF16)

    flat = (slot_count * model_width // LANES, LANES)
    places = own_places()
    residual, outgoing = pl.pallas_call(
        outgoing_kernel,
        name="outgoing",
        out_shape=(shape(wide, F32), shape(flat, BF16)),
        in_specs=[pl.BlockSpec(memory_space=pltpu.SMEM)]
        + [pl.BlockSpec(memory_space=pltpu.VMEM)] * 8,
        scratch_shapes=[
            pltpu.VMEM((head_count, tok_rows, head_dim), BF16),
            pltpu.VMEM(flat, F32),
        ],
        cost_estimate=cost(120000000, 3000000),
        compiler_params=vmem(10),
    )(
        places,
        state_in,
        turned_queries,
        inside,
        fade,
        hidden_in[0],
        retention_gain[None],
        norm_gain[None],
        placing,
    )
    packed = (expert_count, capacity * model_width // LANES, LANES)
    arrived = exchange(outgoing.reshape(packed), OWNERS).reshape(slot_count, model_width)
    cut = stacked.shape[1] // 2
    far = [along_x(after[:, :cut], 1), along_x(before[:, cut:], -1)]
    far_other = [swapped(piece) for piece in far]
    pieces = [stacked, own_other, after, after_other, *far, *far_other, before, before_other]
    expert_out = run_experts(arrived, pieces)
    returned = exchange(expert_out.reshape(packed), OWNERS).reshape(slot_count, model_width)
    picks = [
        (destination[:, index][:, None] == slot_lanes[None, :]).astype(BF16)
        for index in range(top_count)
    ]
    output = pl.pallas_call(
        combine_kernel,
        name="combine",
        out_shape=shape(wide, BF16),
        in_specs=[pl.BlockSpec(memory_space=pltpu.SMEM)]
        + [pl.BlockSpec(memory_space=pltpu.VMEM)] * 5,
        scratch_shapes=[pltpu.VMEM((head_count, tok_rows, head_dim), F32)],
        cost_estimate=cost(180000000, 2000000),
        compiler_params=vmem(8),
    )(places, returned, *picks, route_weights[0], residual)
    return output[None]


def solution(mesh):
    ctx, exp, dp = mesh.shape["ctx"], mesh.shape["exp"], mesh.shape["dp"]
    split = Mesh(
        mesh.devices.reshape(ctx // 2, 2, exp // 2, 2, dp), ("z", "ylo", "x", "core", "yhi")
    )
    tokens = P("yhi", CTX + EXP, None)
    experts = P(OWNERS, EXP, None)
    in_specs = (tokens,) * 5 + (P(), P()) + (tokens,) * 2 + (experts,) * 3
    return jax.shard_map(body, mesh=split, in_specs=in_specs, out_specs=tokens, check_vma=False)
```

```python
import jax
import jax.numpy as jnp
import numpy as np
from jax import lax
from jax.experimental import pallas as pl
from jax.experimental.pallas import tpu as pltpu
from jax.sharding import Mesh, PartitionSpec as P

CTX = ("zhi", "zlo", "ylo")
EXP = ("x", "core")
PLANE = ("ylo", "x", "core")
OWNERS = ("zhi", "zlo", "ylo", "yhi")
LOG_ROWS = 8
LANES = 128
TILE = 512
F32, BF16 = jnp.float32, jnp.bfloat16


def exchange(blocks, axes):
    return lax.all_to_all(blocks, axes, split_axis=0, concat_axis=0, tiled=True)


def dot32(left, right):
    return jnp.dot(left, right, preferred_element_type=F32)


def cost(flops, moved):
    return pl.CostEstimate(flops=flops, bytes_accessed=moved, transcendentals=flops // 1000)


def log_rows(value):
    high = value.astype(BF16).astype(F32)
    middle = (value - high).astype(BF16).astype(F32)
    low = value - high - middle
    line = lax.broadcasted_iota(jnp.int32, (LOG_ROWS, value.shape[1]), 0)
    rows = jnp.where(line == 0, high, jnp.where(line == 1, middle, jnp.where(line == 2, low, 0.0)))
    return rows.astype(BF16)


def log_row(rows):
    return jnp.sum(rows.astype(F32), axis=0, keepdims=True)


def turned(block, cosine, sine):
    return block * cosine + pltpu.roll(block, block.shape[1] // 2, 1) * sine


def summary_kernel(
    keys_hbm,
    values_hbm,
    log_ref,
    cos_ref,
    sin_ref,
    gate_hbm,
    up_hbm,
    down_hbm,
    message_ref,
    total_ref,
    stacked_hbm,
    keys_ref,
    values_ref,
    shard_ref,
    own_sems,
    in_sems,
    out_sems,
):
    shards = (gate_hbm, up_hbm, down_hbm)
    loads = [
        pltpu.make_async_copy(shard, shard_ref.at[index], in_sems.at[index])
        for index, shard in enumerate(shards)
    ]
    stores = [
        pltpu.make_async_copy(shard_ref.at[index], stacked_hbm.at[index], out_sems.at[index])
        for index in range(len(shards))
    ]
    own = [
        pltpu.make_async_copy(keys_hbm, keys_ref, own_sems.at[0]),
        pltpu.make_async_copy(values_hbm, values_ref, own_sems.at[1]),
    ]
    for load in own + loads:
        load.start()
    heads, count = log_ref.shape
    head_dim = cos_ref.shape[1]
    parts = message_ref.shape[0] // heads
    rows = head_dim // parts
    earlier = lax.broadcasted_iota(jnp.int32, (count, count), 0)
    upto = lax.broadcasted_iota(jnp.int32, (count, count), 1)
    ones = jnp.where(earlier <= upto, 1.0, 0.0).astype(F32)
    total = jnp.dot(
        log_ref[...], ones, precision=lax.Precision.HIGHEST, preferred_element_type=F32
    )
    total_ref[...] = total
    last = total[:, count - 1 :]
    trailing = jnp.exp(last - total)
    wide = jnp.broadcast_to(last, (heads, head_dim))
    for load in own:
        load.wait()
    for head in range(heads):
        if head == 2:
            for load, store in zip(loads, stores):
                load.wait()
                store.start()
        lanes = slice(head * head_dim, (head + 1) * head_dim)
        keys = turned(keys_ref[:, lanes].astype(F32), cos_ref[...], sin_ref[...]).astype(BF16)
        faded = keys.astype(F32).T * trailing[head : head + 1]
        coarse = faded.astype(BF16)
        fine = (faded - coarse.astype(F32)).astype(BF16)
        summary = dot32(coarse, values_ref[:, lanes]) + dot32(fine, values_ref[:, lanes])
        summary = summary.astype(BF16)
        logs = log_rows(wide[head : head + 1])
        for part in range(parts):
            message_ref[head * parts + part, :rows] = summary[part * rows : (part + 1) * rows]
            message_ref[head * parts + part, rows:] = logs
    for store in stores:
        store.wait()


def inside_kernel(
    queries_ref, keys_ref, values_ref, total_ref, cos_ref, sin_ref, turned_ref, inside_ref, fade_ref
):
    heads, count = total_ref.shape
    head_dim = cos_ref.shape[1]
    row = lax.broadcasted_iota(jnp.int32, (count, count), 0)
    column = lax.broadcasted_iota(jnp.int32, (count, count), 1)
    causal = row >= column
    fade = jnp.zeros((count, count), F32)
    for head in range(heads):
        lanes = slice(head * head_dim, (head + 1) * head_dim)
        queries = turned(queries_ref[:, lanes].astype(F32), cos_ref[...], sin_ref[...])
        queries = (queries * head_dim ** (-0.5)).astype(BF16)
        turned_ref[:, lanes] = queries
        keys = turned(keys_ref[:, lanes].astype(F32), cos_ref[...], sin_ref[...]).astype(BF16)
        scores = lax.dot_general(
            queries, keys, (((1,), (1,)), ((), ())), preferred_element_type=F32
        )
        here = total_ref[head : head + 1, :]
        down = jnp.broadcast_to(here, (head_dim, count)).T
        spread = jnp.where(causal, down - here, 0.0)
        weights = jnp.where(causal, scores * jnp.exp(spread), 0.0).astype(BF16)
        inside_ref[:, lanes] = dot32(weights, values_ref[:, lanes])
        fade = jnp.where(column == head, jnp.exp(down), fade)
    fade_ref[...] = fade


def sum_kernel(arrived_ref, message_ref):
    plane, rows, head_dim = arrived_ref.shape
    rows = rows - LOG_ROWS
    total = jnp.zeros((rows, head_dim), F32)
    log_total = jnp.zeros((1, head_dim), F32)
    for block in range(plane):
        log = log_row(arrived_ref[block, rows:])
        total = jnp.exp(log) * total + arrived_ref[block, :rows].astype(F32)
        log_total = log_total + log
    total, logs = total.astype(BF16), log_rows(log_total)
    for member in range(message_ref.shape[0]):
        message_ref[member, :rows] = total
        message_ref[member, rows:] = logs


def entering_kernel(own_ref, arrived_ref, near_ref, far_ref, entering_ref):
    rows = entering_ref.shape[1]
    state = jnp.zeros(entering_ref.shape[1:], F32)
    for level, sums_ref in enumerate((far_ref, near_ref)):
        own = own_ref[level]
        for member in range(sums_ref.shape[0]):
            log = log_row(sums_ref[member, rows:])
            later = jnp.exp(log) * state + sums_ref[member, :rows].astype(F32)
            state = jnp.where(member < own, later, state)
    for block in range(arrived_ref.shape[0]):
        entering_ref[block] = state.astype(BF16)
        log = log_row(arrived_ref[block, rows:])
        state = jnp.exp(log) * state + arrived_ref[block, :rows].astype(F32)


def outgoing_kernel(
    own_ref,
    state_ref,
    queries_ref,
    inside_ref,
    fade_ref,
    hidden_ref,
    group_gain_ref,
    norm_gain_ref,
    placing_ref,
    residual_ref,
    outgoing_ref,
    normed_ref,
    packed_ref,
):
    chunks, count, head_dim = normed_ref.shape
    square = jnp.zeros((count, 1), F32)
    for head in range(chunks):
        lanes = slice(head * head_dim, (head + 1) * head_dim)
        far = dot32(queries_ref[:, lanes], state_ref[head * head_dim : (head + 1) * head_dim, :])
        retrieved = inside_ref[:, lanes] + fade_ref[:, head : head + 1] * far
        deviation = retrieved - jnp.mean(retrieved, axis=1, keepdims=True)
        variance = jnp.mean(deviation * deviation, axis=1, keepdims=True)
        normalized = deviation * lax.rsqrt(variance + 1e-05)
        residual = hidden_ref[:, lanes].astype(F32) + group_gain_ref[:, lanes] * normalized
        residual_ref[:, lanes] = residual
        square = square + jnp.sum(residual * residual, axis=1, keepdims=True)
    scale = lax.rsqrt(square * (1.0 / (chunks * head_dim)) + 1e-06)
    for chunk in range(chunks):
        lanes = slice(chunk * head_dim, (chunk + 1) * head_dim)
        normed = residual_ref[:, lanes] * scale * norm_gain_ref[:, lanes]
        normed_ref[own_ref[chunk]] = normed.astype(BF16)
    slots = placing_ref.shape[0]
    for chunk in range(chunks):
        packed_ref[pl.ds(chunk, slots, stride=chunks), :] = dot32(
            placing_ref[...], normed_ref[chunk]
        )
    outgoing_ref[...] = packed_ref[...].astype(BF16)


def combine_kernel(
    own_ref, returned_ref, first_ref, second_ref, weights_ref, residual_ref, out_ref, mixed_ref
):
    chunks, _, lanes_count = mixed_ref.shape
    for chunk in range(chunks):
        lanes = slice(chunk * lanes_count, (chunk + 1) * lanes_count)
        rows = returned_ref[:, lanes]
        mixed_ref[chunk] = weights_ref[:, :1] * dot32(first_ref[...], rows) + weights_ref[
            :, 1:
        ] * dot32(second_ref[...], rows)
    for chunk in range(chunks):
        lanes = slice(chunk * lanes_count, (chunk + 1) * lanes_count)
        out_ref[:, lanes] = (residual_ref[:, lanes] + mixed_ref[own_ref[chunk]]).astype(BF16)


def expert_kernel(*refs):
    arrived_ref, pieces, out_ref = refs[0], refs[1:-5], refs[-5]
    weights_ref, hidden_ref, packed_ref, sems = refs[-4:]
    width = weights_ref.shape[2]
    copies = [[] for _ in range(3)]
    for index in range(3):
        start = 0
        for number, piece in enumerate(pieces):
            size = piece.shape[1]
            copy = pltpu.make_async_copy(
                piece.at[index],
                weights_ref.at[index, start : start + size, :],
                sems.at[index, number],
            )
            copy.start()
            copies[index].append(copy)
            start += size
    for copy in copies[0]:
        copy.wait()
    for start in range(0, width, TILE):
        columns = slice(start, min(width, start + TILE))
        gate = dot32(arrived_ref[...], weights_ref[0, :, columns])
        if start == 0:
            for copy in copies[1]:
                copy.wait()
        up = dot32(arrived_ref[...], weights_ref[1, :, columns])
        hidden_ref[:, columns] = (gate / (1.0 + jnp.exp(-gate)) * up).astype(BF16)
    for copy in copies[2]:
        copy.wait()
    rows, lanes = arrived_ref.shape[0], packed_ref.shape[1]
    chunks = packed_ref.shape[0] // rows
    for chunk in range(0, chunks, 2):
        pair = lax.dot_general(
            hidden_ref[...],
            weights_ref[2, chunk * lanes : (chunk + 2) * lanes, :],
            (((1,), (1,)), ((), ())),
            preferred_element_type=F32,
        )
        for side in range(2):
            packed_ref[pl.ds(chunk + side, rows, stride=chunks), :] = pair[
                :, side * lanes : (side + 1) * lanes
            ]
    out_ref[...] = packed_ref[...].astype(BF16)


def shape(dims, kind):
    return jax.ShapeDtypeStruct(dims, kind)


def vmem(mebibytes):
    return pltpu.CompilerParams(vmem_limit_bytes=mebibytes << 20)


def run_experts(arrived, pieces):
    rows, model_width = arrived.shape
    width = pieces[0].shape[2]
    anywhere = pl.BlockSpec(memory_space=pl.ANY)
    return pl.pallas_call(
        expert_kernel,
        name="experts",
        out_shape=shape((rows * model_width // LANES, LANES), BF16),
        in_specs=[pl.BlockSpec(memory_space=pltpu.VMEM)] + [anywhere] * len(pieces),
        out_specs=pl.BlockSpec(memory_space=pltpu.VMEM),
        scratch_shapes=[
            pltpu.VMEM((3, model_width, width), BF16),
            pltpu.VMEM((rows, width), BF16),
            pltpu.VMEM((rows * model_width // LANES, LANES), F32),
            pltpu.SemaphoreType.DMA((3, len(pieces))),
        ],
        cost_estimate=cost(6 * rows * model_width * width, 6 * model_width * width),
        compiler_params=vmem(20),
    )(arrived, *pieces)


def summed(parts, members):
    return pl.pallas_call(
        sum_kernel,
        name="sums",
        out_shape=shape((members,) + parts.shape[1:], BF16),
        cost_estimate=cost(500000, 600000),
        compiler_params=vmem(4),
    )(parts)


def along_x(piece, step):
    size = lax.axis_size("x")
    return lax.ppermute(piece, "x", [(i, (i - step) % size) for i in range(size)])


def swapped(piece):
    return lax.ppermute(piece, "core", [(0, 1), (1, 0)])


def own_places():
    chips, cores = lax.axis_size("x"), lax.axis_size("core")
    chunk = jnp.arange(chips * cores, dtype=jnp.int32)
    chip = (chunk // cores + chips - lax.axis_index("x")) % chips
    return chip * cores + (chunk + lax.axis_index("core")) % cores


def body(
    hidden_in,
    queries,
    keys,
    values,
    log_decay,
    retention_gain,
    norm_gain,
    routes,
    route_weights,
    w_gate,
    w_up,
    w_down,
):
    tok_rows = hidden_in.shape[1]
    model_width = hidden_in.shape[2]
    head_count = log_decay.shape[2]
    head_dim = model_width // head_count
    wide = (tok_rows, model_width)
    plane = lax.axis_size(PLANE)
    part_rows = head_count * head_dim // plane
    message = (plane, part_rows + LOG_ROWS, head_dim)

    half = head_dim // 2
    inverse = (10000.0 ** (-np.arange(half) / half)).astype(np.float32)
    sign = np.repeat(np.array([-1.0, 1.0], np.float32), half)
    block_index = lax.axis_index(CTX) * lax.axis_size(EXP) + lax.axis_index(EXP)
    position = block_index * tok_rows + jnp.arange(tok_rows, dtype=jnp.int32)
    angles = position.astype(F32)[:, None] * np.tile(inverse, 2)[None, :]
    cosine, sine = jnp.cos(angles), jnp.sin(angles) * sign

    shards = (3,) + w_gate.shape[1:]
    any_space, in_vmem = pl.BlockSpec(memory_space=pl.ANY), pl.BlockSpec(memory_space=pltpu.VMEM)
    out_message, total, stacked = pl.pallas_call(
        summary_kernel,
        name="summary",
        out_shape=(
            shape(message, BF16),
            shape((head_count, tok_rows), F32),
            shape(shards, BF16),
        ),
        in_specs=[any_space] * 2 + [in_vmem] * 3 + [any_space] * 3,
        out_specs=(in_vmem, in_vmem, any_space),
        scratch_shapes=[
            pltpu.VMEM(wide, BF16),
            pltpu.VMEM(wide, BF16),
            pltpu.VMEM(shards, BF16),
            pltpu.SemaphoreType.DMA((2,)),
            pltpu.SemaphoreType.DMA((3,)),
            pltpu.SemaphoreType.DMA((3,)),
        ],
        cost_estimate=cost(70000000, 3200000),
    )(keys[0], values[0], log_decay[0].T, cosine, sine, w_gate[0], w_up[0], w_down[0])
    summaries = exchange(out_message, PLANE)
    after, before = along_x(stacked, 1), along_x(stacked, -1)
    turned_queries, inside, fade = pl.pallas_call(
        inside_kernel,
        name="inside",
        out_shape=(shape(wide, BF16), shape(wide, F32), shape((tok_rows, tok_rows), F32)),
        cost_estimate=cost(70000000, 2200000),
        compiler_params=vmem(8),
    )(queries[0], keys[0], values[0], total, cosine, sine)
    near = exchange(summed(summaries, lax.axis_size("zlo")), "zlo")
    far = exchange(summed(near, lax.axis_size("zhi")), "zhi")
    own_other = swapped(stacked)
    entering = pl.pallas_call(
        entering_kernel,
        name="enter",
        out_shape=shape((plane, part_rows, head_dim), BF16),
        in_specs=[pl.BlockSpec(memory_space=pltpu.SMEM)]
        + [pl.BlockSpec(memory_space=pltpu.VMEM)] * 3,
        cost_estimate=cost(900000, 900000),
        compiler_params=vmem(4),
    )(jnp.stack([lax.axis_index("zhi"), lax.axis_index("zlo")]), summaries, near, far)
    state_in = exchange(entering, PLANE).reshape(model_width, head_dim)
    after_other, before_other = swapped(after), swapped(before)

    expert_count = lax.axis_size(OWNERS)
    top_count = routes.shape[2]
    capacity = (tok_rows * top_count * 5 + 4 * expert_count - 1) // (4 * expert_count)
    slot_count = expert_count * capacity
    route_rows = routes[0]
    expert_hits = (
        route_rows.reshape(tok_rows * top_count)[:, None]
        == jnp.arange(expert_count, dtype=jnp.int32)[None, :]
    ).astype(jnp.int32)
    earlier = jnp.cumsum(expert_hits, axis=0) - expert_hits
    slot_rank = jnp.sum(earlier * expert_hits, axis=1).reshape(tok_rows, top_count)
    destination = route_rows * capacity + slot_rank
    slot_lanes = jnp.arange(slot_count, dtype=jnp.int32)
    placing = jnp.any(destination[None, :, :] == slot_lanes[:, None, None], axis=2).astype(BF16)

    flat = (slot_count * model_width // LANES, LANES)
    places = own_places()
    residual, outgoing = pl.pallas_call(
        outgoing_kernel,
        name="outgoing",
        out_shape=(shape(wide, F32), shape(flat, BF16)),
        in_specs=[pl.BlockSpec(memory_space=pltpu.SMEM)]
        + [pl.BlockSpec(memory_space=pltpu.VMEM)] * 8,
        scratch_shapes=[
            pltpu.VMEM((head_count, tok_rows, head_dim), BF16),
            pltpu.VMEM(flat, F32),
        ],
        cost_estimate=cost(120000000, 3000000),
        compiler_params=vmem(10),
    )(
        places,
        state_in,
        turned_queries,
        inside,
        fade,
        hidden_in[0],
        retention_gain[None],
        norm_gain[None],
        placing,
    )
    packed = (expert_count, capacity * model_width // LANES, LANES)
    arrived = exchange(outgoing.reshape(packed), OWNERS).reshape(slot_count, model_width)
    cut = stacked.shape[1] // 2
    relayed = [along_x(after[:, :cut], 1), along_x(before[:, cut:], -1)]
    relayed_other = [swapped(piece) for piece in relayed]
    pieces = [stacked, own_other, after, after_other]
    pieces += [*relayed, *relayed_other, before, before_other]
    expert_out = run_experts(arrived, pieces)
    returned = exchange(expert_out.reshape(packed), OWNERS).reshape(slot_count, model_width)
    picks = [
        (destination[:, index][:, None] == slot_lanes[None, :]).astype(BF16)
        for index in range(top_count)
    ]
    output = pl.pallas_call(
        combine_kernel,
        name="combine",
        out_shape=shape(wide, BF16),
        in_specs=[pl.BlockSpec(memory_space=pltpu.SMEM)]
        + [pl.BlockSpec(memory_space=pltpu.VMEM)] * 5,
        scratch_shapes=[pltpu.VMEM((head_count, tok_rows, head_dim), F32)],
        cost_estimate=cost(180000000, 2000000),
        compiler_params=vmem(8),
    )(places, returned, *picks, route_weights[0], residual)
    return output[None]


def solution(mesh):
    ctx, exp, dp = mesh.shape["ctx"], mesh.shape["exp"], mesh.shape["dp"]
    split = Mesh(
        mesh.devices.reshape(ctx // 8, 4, 2, exp // 2, 2, dp),
        ("zhi", "zlo", "ylo", "x", "core", "yhi"),
    )
    tokens = P("yhi", CTX + EXP, None)
    experts = P(OWNERS, EXP, None)
    in_specs = (tokens,) * 5 + (P(), P()) + (tokens,) * 2 + (experts,) * 3
    return jax.shard_map(body, mesh=split, in_specs=in_specs, out_specs=tokens, check_vma=False)
```

```python
import jax
import jax.numpy as jnp
import numpy as np
from jax import lax
from jax.experimental import pallas as pl
from jax.experimental.pallas import tpu as pltpu
from jax.sharding import Mesh, PartitionSpec as P

CTX = ("z", "ylo")
EXP = ("x", "core")
PLANE = ("ylo", "x", "core")
OWNERS = ("z", "ylo", "yhi")
LOG_ROWS = 8
LANES = 128
TILE = 512
F32, BF16 = jnp.float32, jnp.bfloat16


def exchange(blocks, axes):
    return lax.all_to_all(blocks, axes, split_axis=0, concat_axis=0, tiled=True)


def dot32(left, right):
    return jnp.dot(left, right, preferred_element_type=F32)


def cost(flops, moved):
    return pl.CostEstimate(flops=flops, bytes_accessed=moved, transcendentals=flops // 1000)


def log_rows(value):
    high = value.astype(BF16).astype(F32)
    middle = (value - high).astype(BF16).astype(F32)
    low = value - high - middle
    line = lax.broadcasted_iota(jnp.int32, (LOG_ROWS, value.shape[1]), 0)
    rows = jnp.where(line == 0, high, jnp.where(line == 1, middle, jnp.where(line == 2, low, 0.0)))
    return rows.astype(BF16)


def log_row(rows):
    return jnp.sum(rows.astype(F32), axis=0, keepdims=True)


def turned(block, cosine, sine):
    return block * cosine + pltpu.roll(block, block.shape[1] // 2, 1) * sine


def tables(start_ref, cos_ref, sin_ref):
    cosine = start_ref[0:1] * cos_ref[...] - start_ref[1:2] * sin_ref[...]
    sine = start_ref[1:2] * cos_ref[...] + start_ref[0:1] * sin_ref[...]
    return cosine, sine * start_ref[2:3]


def summary_kernel(
    keys_ref,
    values_ref,
    log_ref,
    start_ref,
    cos_ref,
    sin_ref,
    message_ref,
    total_ref,
):
    cosine, sine = tables(start_ref, cos_ref, sin_ref)
    heads, count = log_ref.shape
    head_dim = cos_ref.shape[1]
    parts = message_ref.shape[0] // heads
    rows = head_dim // parts
    earlier = lax.broadcasted_iota(jnp.int32, (count, count), 0)
    upto = lax.broadcasted_iota(jnp.int32, (count, count), 1)
    ones = jnp.where(earlier <= upto, 1.0, 0.0).astype(F32)
    total = jnp.dot(
        log_ref[...], ones, precision=lax.Precision.HIGHEST, preferred_element_type=F32
    )
    total_ref[...] = total
    last = total[:, count - 1 :]
    trailing = jnp.exp(last - total)
    wide = jnp.broadcast_to(last, (heads, head_dim))
    for head in range(heads):
        lanes = slice(head * head_dim, (head + 1) * head_dim)
        keys = turned(keys_ref[:, lanes].astype(F32), cosine, sine).astype(BF16)
        faded = keys.astype(F32).T * trailing[head : head + 1]
        coarse = faded.astype(BF16)
        fine = (faded - coarse.astype(F32)).astype(BF16)
        summary = dot32(coarse, values_ref[:, lanes]) + dot32(fine, values_ref[:, lanes])
        summary = summary.astype(BF16)
        logs = log_rows(wide[head : head + 1])
        for part in range(parts):
            message_ref[head * parts + part, :rows] = summary[part * rows : (part + 1) * rows]
            message_ref[head * parts + part, rows:] = logs


def stack_kernel(gate_hbm, up_hbm, down_hbm, stacked_hbm, shard_ref, in_sems, out_sems):
    shards = (gate_hbm, up_hbm, down_hbm)
    loads = [
        pltpu.make_async_copy(shard, shard_ref.at[index], in_sems.at[index])
        for index, shard in enumerate(shards)
    ]
    stores = [
        pltpu.make_async_copy(shard_ref.at[index], stacked_hbm.at[index], out_sems.at[index])
        for index in range(len(shards))
    ]
    for load in loads:
        load.start()
    for load, store in zip(loads, stores):
        load.wait()
        store.start()
    for store in stores:
        store.wait()


def inside_kernel(
    queries_ref,
    keys_ref,
    values_ref,
    total_ref,
    start_ref,
    cos_ref,
    sin_ref,
    turned_ref,
    inside_ref,
    fade_ref,
):
    cosine, sine = tables(start_ref, cos_ref, sin_ref)
    heads, count = total_ref.shape
    head_dim = cos_ref.shape[1]
    row = lax.broadcasted_iota(jnp.int32, (count, count), 0)
    column = lax.broadcasted_iota(jnp.int32, (count, count), 1)
    causal = row >= column
    fade = jnp.zeros((count, count), F32)
    for head in range(heads):
        lanes = slice(head * head_dim, (head + 1) * head_dim)
        queries = turned(queries_ref[:, lanes].astype(F32), cosine, sine)
        queries = (queries * head_dim ** (-0.5)).astype(BF16)
        turned_ref[:, lanes] = queries
        keys = turned(keys_ref[:, lanes].astype(F32), cosine, sine).astype(BF16)
        scores = lax.dot_general(
            queries, keys, (((1,), (1,)), ((), ())), preferred_element_type=F32
        )
        here = total_ref[head : head + 1, :]
        down = jnp.broadcast_to(here, (head_dim, count)).T
        spread = jnp.where(causal, down - here, 0.0)
        weights = jnp.where(causal, scores * jnp.exp(spread), 0.0).astype(BF16)
        inside_ref[:, lanes] = dot32(weights, values_ref[:, lanes])
        fade = jnp.where(column == head, jnp.exp(down), fade)
    fade_ref[...] = fade


def plane_sum_kernel(arrived_ref, message_ref):
    plane, rows, head_dim = arrived_ref.shape
    rows = rows - LOG_ROWS
    total = jnp.zeros((rows, head_dim), F32)
    log_total = jnp.zeros((1, head_dim), F32)
    for block in range(plane):
        log = log_row(arrived_ref[block, rows:])
        total = jnp.exp(log) * total + arrived_ref[block, :rows].astype(F32)
        log_total = log_total + log
    total, logs = total.astype(BF16), log_rows(log_total)
    for z in range(message_ref.shape[0]):
        message_ref[z, :rows] = total
        message_ref[z, rows:] = logs


def entering_kernel(own_ref, arrived_ref, planes_ref, entering_ref):
    rows = entering_ref.shape[1]
    own = own_ref[0]
    state = jnp.zeros(entering_ref.shape[1:], F32)
    for z in range(planes_ref.shape[0]):
        log = log_row(planes_ref[z, rows:])
        later = jnp.exp(log) * state + planes_ref[z, :rows].astype(F32)
        state = jnp.where(z < own, later, state)
    for block in range(arrived_ref.shape[0]):
        entering_ref[block] = state.astype(BF16)
        log = log_row(arrived_ref[block, rows:])
        state = jnp.exp(log) * state + arrived_ref[block, :rows].astype(F32)


def outgoing_kernel(
    own_ref,
    state_ref,
    queries_ref,
    inside_ref,
    fade_ref,
    hidden_ref,
    group_gain_ref,
    norm_gain_ref,
    placing_ref,
    residual_ref,
    outgoing_ref,
    normed_ref,
    packed_ref,
):
    chunks, count, head_dim = normed_ref.shape
    square = jnp.zeros((count, 1), F32)
    for head in range(chunks):
        lanes = slice(head * head_dim, (head + 1) * head_dim)
        far = dot32(queries_ref[:, lanes], state_ref[head * head_dim : (head + 1) * head_dim, :])
        retrieved = inside_ref[:, lanes] + fade_ref[:, head : head + 1] * far
        deviation = retrieved - jnp.mean(retrieved, axis=1, keepdims=True)
        variance = jnp.mean(deviation * deviation, axis=1, keepdims=True)
        normalized = deviation * lax.rsqrt(variance + 1e-05)
        residual = hidden_ref[:, lanes].astype(F32) + group_gain_ref[:, lanes] * normalized
        residual_ref[:, lanes] = residual
        square = square + jnp.sum(residual * residual, axis=1, keepdims=True)
    scale = lax.rsqrt(square * (1.0 / (chunks * head_dim)) + 1e-06)
    for chunk in range(chunks):
        lanes = slice(chunk * head_dim, (chunk + 1) * head_dim)
        normed = residual_ref[:, lanes] * scale * norm_gain_ref[:, lanes]
        normed_ref[own_ref[chunk]] = normed.astype(BF16)
    slots = placing_ref.shape[0]
    for chunk in range(chunks):
        packed_ref[pl.ds(chunk, slots, stride=chunks), :] = dot32(
            placing_ref[...], normed_ref[chunk]
        )
    outgoing_ref[...] = packed_ref[...].astype(BF16)


def combine_kernel(
    own_ref, returned_ref, first_ref, second_ref, weights_ref, residual_ref, out_ref, mixed_ref
):
    chunks, _, lanes_count = mixed_ref.shape
    for chunk in range(chunks):
        lanes = slice(chunk * lanes_count, (chunk + 1) * lanes_count)
        rows = returned_ref[:, lanes]
        mixed_ref[chunk] = weights_ref[:, :1] * dot32(first_ref[...], rows) + weights_ref[
            :, 1:
        ] * dot32(second_ref[...], rows)
    for chunk in range(chunks):
        lanes = slice(chunk * lanes_count, (chunk + 1) * lanes_count)
        out_ref[:, lanes] = (residual_ref[:, lanes] + mixed_ref[own_ref[chunk]]).astype(BF16)


def expert_kernel(*refs):
    incoming_hbm, pieces, out_ref = refs[0], refs[1:-8], refs[-8]
    weights_ref, hidden_ref, packed_ref, incoming_ref, arrived_ref, sems, sem = refs[-7:]
    incoming = pltpu.make_async_copy(incoming_hbm, incoming_ref, sem)
    incoming.start()
    width = weights_ref.shape[2]
    copies = [[] for _ in range(3)]
    for index in range(3):
        start = 0
        for number, piece in enumerate(pieces):
            size = piece.shape[1]
            copy = pltpu.make_async_copy(
                piece.at[index],
                weights_ref.at[index, start : start + size, :],
                sems.at[index, number],
            )
            copy.start()
            copies[index].append(copy)
            start += size
    rows, lanes = arrived_ref.shape[0], packed_ref.shape[1]
    chunks = packed_ref.shape[0] // rows
    incoming.wait()
    packed_ref[...] = incoming_ref[...].astype(F32)
    for chunk in range(chunks):
        arrived_ref[:, chunk * lanes : (chunk + 1) * lanes] = packed_ref[
            pl.ds(chunk, rows, stride=chunks), :
        ].astype(BF16)
    for copy in copies[0]:
        copy.wait()
    for start in range(0, width, TILE):
        columns = slice(start, min(width, start + TILE))
        gate = dot32(arrived_ref[...], weights_ref[0, :, columns])
        if start == 0:
            for copy in copies[1]:
                copy.wait()
        up = dot32(arrived_ref[...], weights_ref[1, :, columns])
        hidden_ref[:, columns] = (gate / (1.0 + jnp.exp(-gate)) * up).astype(BF16)
    for copy in copies[2]:
        copy.wait()
    for chunk in range(0, chunks, 2):
        pair = lax.dot_general(
            hidden_ref[...],
            weights_ref[2, chunk * lanes : (chunk + 2) * lanes, :],
            (((1,), (1,)), ((), ())),
            preferred_element_type=F32,
        )
        for side in range(2):
            packed_ref[pl.ds(chunk + side, rows, stride=chunks), :] = pair[
                :, side * lanes : (side + 1) * lanes
            ]
    out_ref[...] = packed_ref[...].astype(BF16)


def shape(dims, kind):
    return jax.ShapeDtypeStruct(dims, kind)


def vmem(mebibytes):
    return pltpu.CompilerParams(vmem_limit_bytes=mebibytes << 20)


def run_experts(arrived, pieces):
    model_width = sum(piece.shape[1] for piece in pieces)
    rows = arrived.size // model_width
    width = pieces[0].shape[2]
    anywhere = pl.BlockSpec(memory_space=pl.ANY)
    return pl.pallas_call(
        expert_kernel,
        name="experts",
        out_shape=shape((rows * model_width // LANES, LANES), BF16),
        in_specs=[anywhere] * (1 + len(pieces)),
        out_specs=pl.BlockSpec(memory_space=pltpu.VMEM),
        scratch_shapes=[
            pltpu.VMEM((3, model_width, width), BF16),
            pltpu.VMEM((rows, width), BF16),
            pltpu.VMEM((rows * model_width // LANES, LANES), F32),
            pltpu.VMEM((rows * model_width // LANES, LANES), BF16),
            pltpu.VMEM((rows, model_width), BF16),
            pltpu.SemaphoreType.DMA((3, len(pieces))),
            pltpu.SemaphoreType.DMA,
        ],
        cost_estimate=cost(6 * rows * model_width * width, 6 * model_width * width),
    )(arrived, *pieces)


def along_x(piece, step):
    size = lax.axis_size("x")
    return lax.ppermute(piece, "x", [(i, (i - step) % size) for i in range(size)])


def swapped(piece):
    return lax.ppermute(piece, "core", [(0, 1), (1, 0)])


def own_places():
    chips, cores = lax.axis_size("x"), lax.axis_size("core")
    chunk = jnp.arange(chips * cores, dtype=jnp.int32)
    chip = (chunk // cores + chips - lax.axis_index("x")) % chips
    return chip * cores + (chunk + lax.axis_index("core")) % cores


def body(
    hidden_in,
    queries,
    keys,
    values,
    log_decay,
    retention_gain,
    norm_gain,
    routes,
    route_weights,
    w_gate,
    w_up,
    w_down,
):
    tok_rows = hidden_in.shape[1]
    model_width = hidden_in.shape[2]
    head_count = log_decay.shape[2]
    head_dim = model_width // head_count
    wide = (tok_rows, model_width)
    plane, depth = lax.axis_size(PLANE), lax.axis_size("z")
    part_rows = head_count * head_dim // plane
    message = (plane, part_rows + LOG_ROWS, head_dim)

    half = head_dim // 2
    inverse = np.tile(10000.0 ** (-np.arange(half) / half), 2)
    sign = np.repeat(np.array([-1.0, 1.0], np.float32), half)
    within = np.arange(tok_rows)[:, None] * inverse[None, :]
    block_index = lax.axis_index(CTX) * lax.axis_size(EXP) + lax.axis_index(EXP)
    start = (block_index * tok_rows).astype(F32) * inverse.astype(np.float32)[None, :]
    start = jnp.concatenate([jnp.cos(start), jnp.sin(start), sign[None, :]])
    turn = (start, np.cos(within).astype(np.float32), np.sin(within).astype(np.float32))

    out_message, total = pl.pallas_call(
        summary_kernel,
        name="summary",
        out_shape=(shape(message, BF16), shape((head_count, tok_rows), F32)),
        cost_estimate=cost(70000000, 1200000),
    )(keys[0], values[0], log_decay[0].T, *turn)
    summaries = exchange(out_message, PLANE)
    shards = (3,) + w_gate.shape[1:]
    stacked = pl.pallas_call(
        stack_kernel,
        name="stack",
        out_shape=shape(shards, BF16),
        in_specs=[pl.BlockSpec(memory_space=pl.ANY)] * 3,
        out_specs=pl.BlockSpec(memory_space=pl.ANY),
        scratch_shapes=[
            pltpu.VMEM(shards, BF16),
            pltpu.SemaphoreType.DMA((3,)),
            pltpu.SemaphoreType.DMA((3,)),
        ],
        cost_estimate=cost(0, 2200000),
    )(w_gate[0], w_up[0], w_down[0])
    after, before = along_x(stacked, 1), along_x(stacked, -1)
    turned_queries, inside, fade = pl.pallas_call(
        inside_kernel,
        name="inside",
        out_shape=(shape(wide, BF16), shape(wide, F32), shape((tok_rows, tok_rows), F32)),
        cost_estimate=cost(70000000, 2200000),
        compiler_params=vmem(8),
    )(queries[0], keys[0], values[0], total, *turn)
    sums = pl.pallas_call(
        plane_sum_kernel,
        name="plane_sum",
        out_shape=shape((depth,) + message[1:], BF16),
        cost_estimate=cost(500000, 600000),
        compiler_params=vmem(4),
    )(summaries)
    sums = exchange(sums, "z")
    own_other = swapped(stacked)
    entering = pl.pallas_call(
        entering_kernel,
        name="enter",
        out_shape=shape((plane, part_rows, head_dim), BF16),
        in_specs=[pl.BlockSpec(memory_space=pltpu.SMEM)]
        + [pl.BlockSpec(memory_space=pltpu.VMEM)] * 2,
        cost_estimate=cost(900000, 900000),
        compiler_params=vmem(4),
    )(lax.axis_index("z")[None], summaries, sums)
    state_in = exchange(entering, PLANE).reshape(model_width, head_dim)
    after_other, before_other = swapped(after), swapped(before)

    expert_count = lax.axis_size(OWNERS)
    top_count = routes.shape[2]
    capacity = (tok_rows * top_count * 5 + 4 * expert_count - 1) // (4 * expert_count)
    slot_count = expert_count * capacity
    route_rows = routes[0]
    expert_hits = (
        route_rows.reshape(tok_rows * top_count)[:, None]
        == jnp.arange(expert_count, dtype=jnp.int32)[None, :]
    ).astype(jnp.int32)
    earlier = jnp.cumsum(expert_hits, axis=0) - expert_hits
    slot_rank = jnp.sum(earlier * expert_hits, axis=1).reshape(tok_rows, top_count)
    destination = route_rows * capacity + slot_rank
    slot_lanes = jnp.arange(slot_count, dtype=jnp.int32)
    placing = jnp.any(destination[None, :, :] == slot_lanes[:, None, None], axis=2).astype(BF16)

    flat = (slot_count * model_width // LANES, LANES)
    places = own_places()
    residual, outgoing = pl.pallas_call(
        outgoing_kernel,
        name="outgoing",
        out_shape=(shape(wide, F32), shape(flat, BF16)),
        in_specs=[pl.BlockSpec(memory_space=pltpu.SMEM)]
        + [pl.BlockSpec(memory_space=pltpu.VMEM)] * 8,
        scratch_shapes=[
            pltpu.VMEM((head_count, tok_rows, head_dim), BF16),
            pltpu.VMEM(flat, F32),
        ],
        cost_estimate=cost(120000000, 3000000),
        compiler_params=vmem(10),
    )(
        places,
        state_in,
        turned_queries,
        inside,
        fade,
        hidden_in[0],
        retention_gain[None],
        norm_gain[None],
        placing,
    )
    packed = (expert_count, capacity * model_width // LANES, LANES)
    arrived = exchange(outgoing.reshape(packed), OWNERS).reshape(flat)
    cut = stacked.shape[1] // 2
    far = [along_x(after[:, :cut], 1), along_x(before[:, cut:], -1)]
    far_other = [swapped(piece) for piece in far]
    pieces = [stacked, own_other, after, after_other, *far, *far_other, before, before_other]
    expert_out = run_experts(arrived, pieces)
    returned = exchange(expert_out.reshape(packed), OWNERS).reshape(slot_count, model_width)
    picks = [
        (destination[:, index][:, None] == slot_lanes[None, :]).astype(BF16)
        for index in range(top_count)
    ]
    output = pl.pallas_call(
        combine_kernel,
        name="combine",
        out_shape=shape(wide, BF16),
        in_specs=[pl.BlockSpec(memory_space=pltpu.SMEM)]
        + [pl.BlockSpec(memory_space=pltpu.VMEM)] * 5,
        scratch_shapes=[pltpu.VMEM((head_count, tok_rows, head_dim), F32)],
        cost_estimate=cost(180000000, 2000000),
        compiler_params=vmem(8),
    )(places, returned, *picks, route_weights[0], residual)
    return output[None]


def solution(mesh):
    ctx, exp, dp = mesh.shape["ctx"], mesh.shape["exp"], mesh.shape["dp"]
    split = Mesh(
        mesh.devices.reshape(ctx // 2, 2, exp // 2, 2, dp), ("z", "ylo", "x", "core", "yhi")
    )
    tokens = P("yhi", CTX + EXP, None)
    experts = P(OWNERS, EXP, None)
    in_specs = (tokens,) * 5 + (P(), P()) + (tokens,) * 2 + (experts,) * 3
    return jax.shard_map(body, mesh=split, in_specs=in_specs, out_specs=tokens, check_vma=False)
```

```python
import jax
import jax.numpy as jnp
import numpy as np
from jax import lax
from jax.experimental import pallas as pl
from jax.experimental.pallas import tpu as pltpu
from jax.sharding import Mesh, PartitionSpec as P

CTX = ("z", "ylo")
EXP = ("x", "core")
PLANE = ("ylo", "x", "core")
OWNERS = ("z", "ylo", "yhi")
LOG_ROWS = 8
LANES = 128
TILE = 512
F32, BF16 = jnp.float32, jnp.bfloat16


def exchange(blocks, axes):
    return lax.all_to_all(blocks, axes, split_axis=0, concat_axis=0, tiled=True)


def dot32(left, right):
    return jnp.dot(left, right, preferred_element_type=F32)


def cost(flops, moved):
    return pl.CostEstimate(flops=flops, bytes_accessed=moved, transcendentals=flops // 1000)


def log_rows(value):
    high = value.astype(BF16).astype(F32)
    middle = (value - high).astype(BF16).astype(F32)
    low = value - high - middle
    line = lax.broadcasted_iota(jnp.int32, (LOG_ROWS, value.shape[1]), 0)
    rows = jnp.where(line == 0, high, jnp.where(line == 1, middle, jnp.where(line == 2, low, 0.0)))
    return rows.astype(BF16)


def log_row(rows):
    return jnp.sum(rows.astype(F32), axis=0, keepdims=True)


def turned(block, cosine, sine):
    return block * cosine + pltpu.roll(block, block.shape[1] // 2, 1) * sine


def tables(cos_start_ref, sin_start_ref, cos_ref, sin_ref):
    cosine = cos_start_ref[...] * cos_ref[...] - sin_start_ref[...] * sin_ref[...]
    sine = sin_start_ref[...] * cos_ref[...] + cos_start_ref[...] * sin_ref[...]
    lane = lax.broadcasted_iota(jnp.int32, sine.shape, 1)
    return cosine, jnp.where(lane < sine.shape[1] // 2, -sine, sine)


def summary_kernel(
    keys_ref,
    values_ref,
    log_ref,
    cos_start_ref,
    sin_start_ref,
    cos_ref,
    sin_ref,
    gate_hbm,
    up_hbm,
    down_hbm,
    message_ref,
    total_ref,
    stacked_hbm,
    shard_ref,
    in_sems,
    out_sems,
):
    shards = (gate_hbm, up_hbm, down_hbm)
    loads = [
        pltpu.make_async_copy(shard, shard_ref.at[index], in_sems.at[index])
        for index, shard in enumerate(shards)
    ]
    stores = [
        pltpu.make_async_copy(shard_ref.at[index], stacked_hbm.at[index], out_sems.at[index])
        for index in range(len(shards))
    ]
    for load in loads:
        load.start()
    cosine, sine = tables(cos_start_ref, sin_start_ref, cos_ref, sin_ref)
    heads, count = log_ref.shape
    head_dim = cos_ref.shape[1]
    parts = message_ref.shape[0] // heads
    rows = head_dim // parts
    earlier = lax.broadcasted_iota(jnp.int32, (count, count), 0)
    upto = lax.broadcasted_iota(jnp.int32, (count, count), 1)
    ones = jnp.where(earlier <= upto, 1.0, 0.0).astype(F32)
    total = jnp.dot(
        log_ref[...], ones, precision=lax.Precision.HIGHEST, preferred_element_type=F32
    )
    total_ref[...] = total
    last = total[:, count - 1 :]
    trailing = jnp.exp(last - total)
    wide = jnp.broadcast_to(last, (heads, head_dim))
    for head in range(heads):
        if head == heads // 2:
            for load, store in zip(loads, stores):
                load.wait()
                store.start()
        lanes = slice(head * head_dim, (head + 1) * head_dim)
        keys = turned(keys_ref[:, lanes].astype(F32), cosine, sine).astype(BF16)
        faded = keys.astype(F32).T * trailing[head : head + 1]
        coarse = faded.astype(BF16)
        fine = (faded - coarse.astype(F32)).astype(BF16)
        summary = dot32(coarse, values_ref[:, lanes]) + dot32(fine, values_ref[:, lanes])
        summary = summary.astype(BF16)
        logs = log_rows(wide[head : head + 1])
        for part in range(parts):
            message_ref[head * parts + part, :rows] = summary[part * rows : (part + 1) * rows]
            message_ref[head * parts + part, rows:] = logs
    for store in stores:
        store.wait()


def inside_kernel(
    queries_ref,
    keys_ref,
    values_ref,
    total_ref,
    cos_start_ref,
    sin_start_ref,
    cos_ref,
    sin_ref,
    turned_ref,
    inside_ref,
    fade_ref,
):
    cosine, sine = tables(cos_start_ref, sin_start_ref, cos_ref, sin_ref)
    heads, count = total_ref.shape
    head_dim = cos_ref.shape[1]
    row = lax.broadcasted_iota(jnp.int32, (count, count), 0)
    column = lax.broadcasted_iota(jnp.int32, (count, count), 1)
    causal = row >= column
    fade = jnp.zeros((count, count), F32)
    for head in range(heads):
        lanes = slice(head * head_dim, (head + 1) * head_dim)
        queries = turned(queries_ref[:, lanes].astype(F32), cosine, sine)
        queries = (queries * head_dim ** (-0.5)).astype(BF16)
        turned_ref[:, lanes] = queries
        keys = turned(keys_ref[:, lanes].astype(F32), cosine, sine).astype(BF16)
        scores = lax.dot_general(
            queries, keys, (((1,), (1,)), ((), ())), preferred_element_type=F32
        )
        here = total_ref[head : head + 1, :]
        down = jnp.broadcast_to(here, (head_dim, count)).T
        spread = jnp.where(causal, down - here, 0.0)
        weights = jnp.where(causal, scores * jnp.exp(spread), 0.0).astype(BF16)
        inside_ref[:, lanes] = dot32(weights, values_ref[:, lanes])
        fade = jnp.where(column == head, jnp.exp(down), fade)
    fade_ref[...] = fade


def plane_sum_kernel(arrived_ref, message_ref):
    plane, rows, head_dim = arrived_ref.shape
    rows = rows - LOG_ROWS
    total = jnp.zeros((rows, head_dim), F32)
    log_total = jnp.zeros((1, head_dim), F32)
    for block in range(plane):
        log = log_row(arrived_ref[block, rows:])
        total = jnp.exp(log) * total + arrived_ref[block, :rows].astype(F32)
        log_total = log_total + log
    total, logs = total.astype(BF16), log_rows(log_total)
    for z in range(message_ref.shape[0]):
        message_ref[z, :rows] = total
        message_ref[z, rows:] = logs


def entering_kernel(own_ref, arrived_ref, planes_ref, entering_ref):
    rows = entering_ref.shape[1]
    own = own_ref[0]
    state = jnp.zeros(entering_ref.shape[1:], F32)
    for z in range(planes_ref.shape[0]):
        log = log_row(planes_ref[z, rows:])
        later = jnp.exp(log) * state + planes_ref[z, :rows].astype(F32)
        state = jnp.where(z < own, later, state)
    for block in range(arrived_ref.shape[0]):
        entering_ref[block] = state.astype(BF16)
        log = log_row(arrived_ref[block, rows:])
        state = jnp.exp(log) * state + arrived_ref[block, :rows].astype(F32)


def outgoing_kernel(
    own_ref,
    state_ref,
    queries_ref,
    inside_ref,
    fade_ref,
    hidden_ref,
    group_gain_ref,
    norm_gain_ref,
    placing_ref,
    residual_ref,
    outgoing_ref,
    normed_ref,
    packed_ref,
):
    chunks, count, head_dim = normed_ref.shape
    square = jnp.zeros((count, 1), F32)
    for head in range(chunks):
        lanes = slice(head * head_dim, (head + 1) * head_dim)
        far = dot32(queries_ref[:, lanes], state_ref[head * head_dim : (head + 1) * head_dim, :])
        retrieved = inside_ref[:, lanes] + fade_ref[:, head : head + 1] * far
        deviation = retrieved - jnp.mean(retrieved, axis=1, keepdims=True)
        variance = jnp.mean(deviation * deviation, axis=1, keepdims=True)
        normalized = deviation * lax.rsqrt(variance + 1e-05)
        residual = hidden_ref[:, lanes].astype(F32) + group_gain_ref[:, lanes] * normalized
        residual_ref[:, lanes] = residual
        square = square + jnp.sum(residual * residual, axis=1, keepdims=True)
    scale = lax.rsqrt(square * (1.0 / (chunks * head_dim)) + 1e-06)
    for chunk in range(chunks):
        lanes = slice(chunk * head_dim, (chunk + 1) * head_dim)
        normed = residual_ref[:, lanes] * scale * norm_gain_ref[:, lanes]
        normed_ref[own_ref[chunk]] = normed.astype(BF16)
    slots = placing_ref.shape[0]
    for chunk in range(chunks):
        packed_ref[pl.ds(chunk, slots, stride=chunks), :] = dot32(
            placing_ref[...], normed_ref[chunk]
        )
    outgoing_ref[...] = packed_ref[...].astype(BF16)


def combine_kernel(
    own_ref, returned_ref, first_ref, second_ref, weights_ref, residual_ref, out_ref, mixed_ref
):
    chunks, _, lanes_count = mixed_ref.shape
    for chunk in range(chunks):
        lanes = slice(chunk * lanes_count, (chunk + 1) * lanes_count)
        rows = returned_ref[:, lanes]
        mixed_ref[chunk] = weights_ref[:, :1] * dot32(first_ref[...], rows) + weights_ref[
            :, 1:
        ] * dot32(second_ref[...], rows)
    for chunk in range(chunks):
        lanes = slice(chunk * lanes_count, (chunk + 1) * lanes_count)
        out_ref[:, lanes] = (residual_ref[:, lanes] + mixed_ref[own_ref[chunk]]).astype(BF16)


def expert_kernel(*refs):
    arrived_ref, pieces, out_ref = refs[0], refs[1:-5], refs[-5]
    weights_ref, hidden_ref, packed_ref, sems = refs[-4:]
    width = weights_ref.shape[2]
    copies = [[] for _ in range(3)]
    for index in range(3):
        start = 0
        for number, piece in enumerate(pieces):
            size = piece.shape[1]
            copy = pltpu.make_async_copy(
                piece.at[index],
                weights_ref.at[index, start : start + size, :],
                sems.at[index, number],
            )
            copy.start()
            copies[index].append(copy)
            start += size
    for copy in copies[0]:
        copy.wait()
    for start in range(0, width, TILE):
        columns = slice(start, min(width, start + TILE))
        gate = dot32(arrived_ref[...], weights_ref[0, :, columns])
        if start == 0:
            for copy in copies[1]:
                copy.wait()
        up = dot32(arrived_ref[...], weights_ref[1, :, columns])
        hidden_ref[:, columns] = (gate / (1.0 + jnp.exp(-gate)) * up).astype(BF16)
    for copy in copies[2]:
        copy.wait()
    rows, lanes = arrived_ref.shape[0], packed_ref.shape[1]
    chunks = packed_ref.shape[0] // rows
    for chunk in range(0, chunks, 2):
        pair = lax.dot_general(
            hidden_ref[...],
            weights_ref[2, chunk * lanes : (chunk + 2) * lanes, :],
            (((1,), (1,)), ((), ())),
            preferred_element_type=F32,
        )
        for side in range(2):
            packed_ref[pl.ds(chunk + side, rows, stride=chunks), :] = pair[
                :, side * lanes : (side + 1) * lanes
            ]
    out_ref[...] = packed_ref[...].astype(BF16)


def shape(dims, kind):
    return jax.ShapeDtypeStruct(dims, kind)


def vmem(mebibytes):
    return pltpu.CompilerParams(vmem_limit_bytes=mebibytes << 20)


def run_experts(arrived, pieces):
    rows, model_width = arrived.shape
    width = pieces[0].shape[2]
    anywhere = pl.BlockSpec(memory_space=pl.ANY)
    return pl.pallas_call(
        expert_kernel,
        name="experts",
        out_shape=shape((rows * model_width // LANES, LANES), BF16),
        in_specs=[pl.BlockSpec(memory_space=pltpu.VMEM)] + [anywhere] * len(pieces),
        out_specs=pl.BlockSpec(memory_space=pltpu.VMEM),
        scratch_shapes=[
            pltpu.VMEM((3, model_width, width), BF16),
            pltpu.VMEM((rows, width), BF16),
            pltpu.VMEM((rows * model_width // LANES, LANES), F32),
            pltpu.SemaphoreType.DMA((3, len(pieces))),
        ],
        cost_estimate=cost(6 * rows * model_width * width, 6 * model_width * width),
        compiler_params=vmem(20),
    )(arrived, *pieces)


def along_x(piece, step):
    size = lax.axis_size("x")
    return lax.ppermute(piece, "x", [(i, (i - step) % size) for i in range(size)])


def swapped(piece):
    return lax.ppermute(piece, "core", [(0, 1), (1, 0)])


def own_places():
    chips, cores = lax.axis_size("x"), lax.axis_size("core")
    chunk = jnp.arange(chips * cores, dtype=jnp.int32)
    chip = (chunk // cores + chips - lax.axis_index("x")) % chips
    return chip * cores + (chunk + lax.axis_index("core")) % cores


def body(
    hidden_in,
    queries,
    keys,
    values,
    log_decay,
    retention_gain,
    norm_gain,
    routes,
    route_weights,
    w_gate,
    w_up,
    w_down,
):
    tok_rows = hidden_in.shape[1]
    model_width = hidden_in.shape[2]
    head_count = log_decay.shape[2]
    head_dim = model_width // head_count
    wide = (tok_rows, model_width)
    plane, depth = lax.axis_size(PLANE), lax.axis_size("z")
    part_rows = head_count * head_dim // plane
    message = (plane, part_rows + LOG_ROWS, head_dim)

    half = head_dim // 2
    inverse = np.tile(10000.0 ** (-np.arange(half) / half), 2)
    within = np.arange(tok_rows)[:, None] * inverse[None, :]
    block_index = lax.axis_index(CTX) * lax.axis_size(EXP) + lax.axis_index(EXP)
    start = (block_index * tok_rows).astype(F32) * inverse.astype(np.float32)[None, :]
    turn = (
        jnp.cos(start),
        jnp.sin(start),
        np.cos(within).astype(np.float32),
        np.sin(within).astype(np.float32),
    )

    shards = (3,) + w_gate.shape[1:]
    any_space, in_vmem = pl.BlockSpec(memory_space=pl.ANY), pl.BlockSpec(memory_space=pltpu.VMEM)
    out_message, total, stacked = pl.pallas_call(
        summary_kernel,
        name="summary",
        out_shape=(
            shape(message, BF16),
            shape((head_count, tok_rows), F32),
            shape(shards, BF16),
        ),
        in_specs=[in_vmem] * 7 + [any_space] * 3,
        out_specs=(in_vmem, in_vmem, any_space),
        scratch_shapes=[
            pltpu.VMEM(shards, BF16),
            pltpu.SemaphoreType.DMA((3,)),
            pltpu.SemaphoreType.DMA((3,)),
        ],
        cost_estimate=cost(70000000, 3200000),
    )(keys[0], values[0], log_decay[0].T, *turn, w_gate[0], w_up[0], w_down[0])
    summaries = exchange(out_message, PLANE)
    after, before = along_x(stacked, 1), along_x(stacked, -1)
    turned_queries, inside, fade = pl.pallas_call(
        inside_kernel,
        name="inside",
        out_shape=(shape(wide, BF16), shape(wide, F32), shape((tok_rows, tok_rows), F32)),
        cost_estimate=cost(70000000, 2200000),
        compiler_params=vmem(8),
    )(queries[0], keys[0], values[0], total, *turn)
    sums = pl.pallas_call(
        plane_sum_kernel,
        name="plane_sum",
        out_shape=shape((depth,) + message[1:], BF16),
        cost_estimate=cost(500000, 600000),
        compiler_params=vmem(4),
    )(summaries)
    sums = exchange(sums, "z")
    own_other = swapped(stacked)
    entering = pl.pallas_call(
        entering_kernel,
        name="enter",
        out_shape=shape((plane, part_rows, head_dim), BF16),
        in_specs=[pl.BlockSpec(memory_space=pltpu.SMEM)]
        + [pl.BlockSpec(memory_space=pltpu.VMEM)] * 2,
        cost_estimate=cost(900000, 900000),
        compiler_params=vmem(4),
    )(lax.axis_index("z")[None], summaries, sums)
    state_in = exchange(entering, PLANE).reshape(model_width, head_dim)
    after_other, before_other = swapped(after), swapped(before)

    expert_count = lax.axis_size(OWNERS)
    top_count = routes.shape[2]
    capacity = (tok_rows * top_count * 5 + 4 * expert_count - 1) // (4 * expert_count)
    slot_count = expert_count * capacity
    route_rows = routes[0]
    expert_hits = (
        route_rows.reshape(tok_rows * top_count)[:, None]
        == jnp.arange(expert_count, dtype=jnp.int32)[None, :]
    ).astype(jnp.int32)
    earlier = jnp.cumsum(expert_hits, axis=0) - expert_hits
    slot_rank = jnp.sum(earlier * expert_hits, axis=1).reshape(tok_rows, top_count)
    destination = route_rows * capacity + slot_rank
    slot_lanes = jnp.arange(slot_count, dtype=jnp.int32)
    placing = jnp.any(destination[None, :, :] == slot_lanes[:, None, None], axis=2).astype(BF16)

    flat = (slot_count * model_width // LANES, LANES)
    places = own_places()
    residual, outgoing = pl.pallas_call(
        outgoing_kernel,
        name="outgoing",
        out_shape=(shape(wide, F32), shape(flat, BF16)),
        in_specs=[pl.BlockSpec(memory_space=pltpu.SMEM)]
        + [pl.BlockSpec(memory_space=pltpu.VMEM)] * 8,
        scratch_shapes=[
            pltpu.VMEM((head_count, tok_rows, head_dim), BF16),
            pltpu.VMEM(flat, F32),
        ],
        cost_estimate=cost(120000000, 3000000),
        compiler_params=vmem(10),
    )(
        places,
        state_in,
        turned_queries,
        inside,
        fade,
        hidden_in[0],
        retention_gain[None],
        norm_gain[None],
        placing,
    )
    packed = (expert_count, capacity * model_width // LANES, LANES)
    arrived = exchange(outgoing.reshape(packed), OWNERS).reshape(slot_count, model_width)
    cut = stacked.shape[1] // 2
    far = [along_x(after[:, :cut], 1), along_x(before[:, cut:], -1)]
    far_other = [swapped(piece) for piece in far]
    pieces = [stacked, own_other, after, after_other, *far, *far_other, before, before_other]
    expert_out = run_experts(arrived, pieces)
    returned = exchange(expert_out.reshape(packed), OWNERS).reshape(slot_count, model_width)
    picks = [
        (destination[:, index][:, None] == slot_lanes[None, :]).astype(BF16)
        for index in range(top_count)
    ]
    output = pl.pallas_call(
        combine_kernel,
        name="combine",
        out_shape=shape(wide, BF16),
        in_specs=[pl.BlockSpec(memory_space=pltpu.SMEM)]
        + [pl.BlockSpec(memory_space=pltpu.VMEM)] * 5,
        scratch_shapes=[pltpu.VMEM((head_count, tok_rows, head_dim), F32)],
        cost_estimate=cost(180000000, 2000000),
        compiler_params=vmem(8),
    )(places, returned, *picks, route_weights[0], residual)
    return output[None]


def solution(mesh):
    ctx, exp, dp = mesh.shape["ctx"], mesh.shape["exp"], mesh.shape["dp"]
    split = Mesh(
        mesh.devices.reshape(ctx // 2, 2, exp // 2, 2, dp), ("z", "ylo", "x", "core", "yhi")
    )
    tokens = P("yhi", CTX + EXP, None)
    experts = P(OWNERS, EXP, None)
    in_specs = (tokens,) * 5 + (P(), P()) + (tokens,) * 2 + (experts,) * 3
    return jax.shard_map(body, mesh=split, in_specs=in_specs, out_specs=tokens, check_vma=False)
```

```python
import jax
import jax.numpy as jnp
import numpy as np
from jax import lax
from jax.experimental import pallas as pl
from jax.experimental.pallas import tpu as pltpu
from jax.sharding import Mesh, PartitionSpec as P

CTX = ("z", "ylo")
EXP = ("x", "core")
PLANE = ("ylo", "x", "core")
OWNERS = ("z", "ylo", "yhi")
LOG_ROWS = 8
LANES = 128
TILE = 512
F32, BF16 = jnp.float32, jnp.bfloat16


def exchange(blocks, axes):
    return lax.all_to_all(blocks, axes, split_axis=0, concat_axis=0, tiled=True)


def dot32(left, right):
    return jnp.dot(left, right, preferred_element_type=F32)


def cost(flops, moved):
    return pl.CostEstimate(flops=flops, bytes_accessed=moved, transcendentals=flops // 1000)


def log_rows(value):
    high = value.astype(BF16).astype(F32)
    middle = (value - high).astype(BF16).astype(F32)
    low = value - high - middle
    line = lax.broadcasted_iota(jnp.int32, (LOG_ROWS, value.shape[1]), 0)
    rows = jnp.where(line == 0, high, jnp.where(line == 1, middle, jnp.where(line == 2, low, 0.0)))
    return rows.astype(BF16)


def log_row(rows):
    return jnp.sum(rows.astype(F32), axis=0, keepdims=True)


def turned(block, cosine, sine):
    return block * cosine + pltpu.roll(block, block.shape[1] // 2, 1) * sine


def turn_by(cosine, sine, row, table):
    cos_row, sin_row = table[0, pl.ds(row, 1), :], table[1, pl.ds(row, 1), :]
    return cosine * cos_row - sine * sin_row, sine * cos_row + cosine * sin_row


def tables(plane_ref, block_ref, plane_table, block_table, within_table):
    cosine, sine = within_table[0], within_table[1]
    cosine, sine = turn_by(cosine, sine, plane_ref[0], plane_table)
    cosine, sine = turn_by(cosine, sine, block_ref[0], block_table)
    lane = lax.broadcasted_iota(jnp.int32, sine.shape, 1)
    return cosine, jnp.where(lane < sine.shape[1] // 2, -sine, sine)


def summary_kernel(
    keys_ref,
    values_ref,
    log_ref,
    plane_ref,
    block_ref,
    plane_table,
    block_table,
    within_table,
    gate_hbm,
    up_hbm,
    down_hbm,
    message_ref,
    total_ref,
    stacked_hbm,
    shard_ref,
    in_sems,
    out_sems,
):
    shards = (gate_hbm, up_hbm, down_hbm)
    loads = [
        pltpu.make_async_copy(shard, shard_ref.at[index], in_sems.at[index])
        for index, shard in enumerate(shards)
    ]
    stores = [
        pltpu.make_async_copy(shard_ref.at[index], stacked_hbm.at[index], out_sems.at[index])
        for index in range(len(shards))
    ]
    for load in loads:
        load.start()
    cosine, sine = tables(plane_ref, block_ref, plane_table, block_table, within_table)
    heads, count = log_ref.shape
    head_dim = within_table.shape[2]
    parts = message_ref.shape[0] // heads
    rows = head_dim // parts
    earlier = lax.broadcasted_iota(jnp.int32, (count, count), 0)
    upto = lax.broadcasted_iota(jnp.int32, (count, count), 1)
    ones = jnp.where(earlier <= upto, 1.0, 0.0).astype(F32)
    total = jnp.dot(
        log_ref[...], ones, precision=lax.Precision.HIGHEST, preferred_element_type=F32
    )
    total_ref[...] = total
    last = total[:, count - 1 :]
    trailing = jnp.exp(last - total)
    wide = jnp.broadcast_to(last, (heads, head_dim))
    for head in range(heads):
        if head == heads // 2:
            for load, store in zip(loads, stores):
                load.wait()
                store.start()
        lanes = slice(head * head_dim, (head + 1) * head_dim)
        keys = turned(keys_ref[:, lanes].astype(F32), cosine, sine).astype(BF16)
        faded = keys.astype(F32).T * trailing[head : head + 1]
        coarse = faded.astype(BF16)
        fine = (faded - coarse.astype(F32)).astype(BF16)
        summary = dot32(coarse, values_ref[:, lanes]) + dot32(fine, values_ref[:, lanes])
        summary = summary.astype(BF16)
        logs = log_rows(wide[head : head + 1])
        for part in range(parts):
            message_ref[head * parts + part, :rows] = summary[part * rows : (part + 1) * rows]
            message_ref[head * parts + part, rows:] = logs
    for store in stores:
        store.wait()


def inside_kernel(
    queries_ref,
    keys_ref,
    values_ref,
    total_ref,
    plane_ref,
    block_ref,
    plane_table,
    block_table,
    within_table,
    turned_ref,
    inside_ref,
    fade_ref,
):
    cosine, sine = tables(plane_ref, block_ref, plane_table, block_table, within_table)
    heads, count = total_ref.shape
    head_dim = within_table.shape[2]
    row = lax.broadcasted_iota(jnp.int32, (count, count), 0)
    column = lax.broadcasted_iota(jnp.int32, (count, count), 1)
    causal = row >= column
    fade = jnp.zeros((count, count), F32)
    for head in range(heads):
        lanes = slice(head * head_dim, (head + 1) * head_dim)
        queries = turned(queries_ref[:, lanes].astype(F32), cosine, sine)
        queries = (queries * head_dim ** (-0.5)).astype(BF16)
        turned_ref[:, lanes] = queries
        keys = turned(keys_ref[:, lanes].astype(F32), cosine, sine).astype(BF16)
        scores = lax.dot_general(
            queries, keys, (((1,), (1,)), ((), ())), preferred_element_type=F32
        )
        here = total_ref[head : head + 1, :]
        down = jnp.broadcast_to(here, (head_dim, count)).T
        spread = jnp.where(causal, down - here, 0.0)
        weights = jnp.where(causal, scores * jnp.exp(spread), 0.0).astype(BF16)
        inside_ref[:, lanes] = dot32(weights, values_ref[:, lanes])
        fade = jnp.where(column == head, jnp.exp(down), fade)
    fade_ref[...] = fade


def plane_sum_kernel(arrived_ref, message_ref):
    plane, rows, head_dim = arrived_ref.shape
    rows = rows - LOG_ROWS
    total = jnp.zeros((rows, head_dim), F32)
    log_total = jnp.zeros((1, head_dim), F32)
    for block in range(plane):
        log = log_row(arrived_ref[block, rows:])
        total = jnp.exp(log) * total + arrived_ref[block, :rows].astype(F32)
        log_total = log_total + log
    total, logs = total.astype(BF16), log_rows(log_total)
    for z in range(message_ref.shape[0]):
        message_ref[z, :rows] = total
        message_ref[z, rows:] = logs


def entering_kernel(own_ref, arrived_ref, planes_ref, entering_ref):
    rows = entering_ref.shape[1]
    own = own_ref[0]
    state = jnp.zeros(entering_ref.shape[1:], F32)
    for z in range(planes_ref.shape[0]):
        log = log_row(planes_ref[z, rows:])
        later = jnp.exp(log) * state + planes_ref[z, :rows].astype(F32)
        state = jnp.where(z < own, later, state)
    for block in range(arrived_ref.shape[0]):
        entering_ref[block] = state.astype(BF16)
        log = log_row(arrived_ref[block, rows:])
        state = jnp.exp(log) * state + arrived_ref[block, :rows].astype(F32)


def outgoing_kernel(
    own_ref,
    state_ref,
    queries_ref,
    inside_ref,
    fade_ref,
    hidden_ref,
    group_gain_ref,
    norm_gain_ref,
    placing_ref,
    residual_ref,
    outgoing_ref,
    normed_ref,
    packed_ref,
):
    chunks, count, head_dim = normed_ref.shape
    square = jnp.zeros((count, 1), F32)
    for head in range(chunks):
        lanes = slice(head * head_dim, (head + 1) * head_dim)
        far = dot32(queries_ref[:, lanes], state_ref[head * head_dim : (head + 1) * head_dim, :])
        retrieved = inside_ref[:, lanes] + fade_ref[:, head : head + 1] * far
        deviation = retrieved - jnp.mean(retrieved, axis=1, keepdims=True)
        variance = jnp.mean(deviation * deviation, axis=1, keepdims=True)
        normalized = deviation * lax.rsqrt(variance + 1e-05)
        residual = hidden_ref[:, lanes].astype(F32) + group_gain_ref[:, lanes] * normalized
        residual_ref[:, lanes] = residual
        square = square + jnp.sum(residual * residual, axis=1, keepdims=True)
    scale = lax.rsqrt(square * (1.0 / (chunks * head_dim)) + 1e-06)
    for chunk in range(chunks):
        lanes = slice(chunk * head_dim, (chunk + 1) * head_dim)
        normed = residual_ref[:, lanes] * scale * norm_gain_ref[:, lanes]
        normed_ref[own_ref[chunk]] = normed.astype(BF16)
    slots = placing_ref.shape[0]
    for chunk in range(chunks):
        packed_ref[pl.ds(chunk, slots, stride=chunks), :] = dot32(
            placing_ref[...], normed_ref[chunk]
        )
    outgoing_ref[...] = packed_ref[...].astype(BF16)


def combine_kernel(
    own_ref, returned_ref, first_ref, second_ref, weights_ref, residual_ref, out_ref, mixed_ref
):
    chunks, _, lanes_count = mixed_ref.shape
    for chunk in range(chunks):
        lanes = slice(chunk * lanes_count, (chunk + 1) * lanes_count)
        rows = returned_ref[:, lanes]
        mixed_ref[chunk] = weights_ref[:, :1] * dot32(first_ref[...], rows) + weights_ref[
            :, 1:
        ] * dot32(second_ref[...], rows)
    for chunk in range(chunks):
        lanes = slice(chunk * lanes_count, (chunk + 1) * lanes_count)
        out_ref[:, lanes] = (residual_ref[:, lanes] + mixed_ref[own_ref[chunk]]).astype(BF16)


def expert_kernel(*refs):
    arrived_ref, pieces, out_ref = refs[0], refs[1:-5], refs[-5]
    weights_ref, hidden_ref, packed_ref, sems = refs[-4:]
    width = weights_ref.shape[2]
    copies = [[] for _ in range(3)]
    for index in range(3):
        start = 0
        for number, piece in enumerate(pieces):
            size = piece.shape[1]
            copy = pltpu.make_async_copy(
                piece.at[index],
                weights_ref.at[index, start : start + size, :],
                sems.at[index, number],
            )
            copy.start()
            copies[index].append(copy)
            start += size
    for copy in copies[0]:
        copy.wait()
    for start in range(0, width, TILE):
        columns = slice(start, min(width, start + TILE))
        gate = dot32(arrived_ref[...], weights_ref[0, :, columns])
        if start == 0:
            for copy in copies[1]:
                copy.wait()
        up = dot32(arrived_ref[...], weights_ref[1, :, columns])
        hidden_ref[:, columns] = (gate / (1.0 + jnp.exp(-gate)) * up).astype(BF16)
    for copy in copies[2]:
        copy.wait()
    rows, lanes = arrived_ref.shape[0], packed_ref.shape[1]
    chunks = packed_ref.shape[0] // rows
    for chunk in range(0, chunks, 2):
        pair = lax.dot_general(
            hidden_ref[...],
            weights_ref[2, chunk * lanes : (chunk + 2) * lanes, :],
            (((1,), (1,)), ((), ())),
            preferred_element_type=F32,
        )
        for side in range(2):
            packed_ref[pl.ds(chunk + side, rows, stride=chunks), :] = pair[
                :, side * lanes : (side + 1) * lanes
            ]
    out_ref[...] = packed_ref[...].astype(BF16)


def shape(dims, kind):
    return jax.ShapeDtypeStruct(dims, kind)


def vmem(mebibytes):
    return pltpu.CompilerParams(vmem_limit_bytes=mebibytes << 20)


def run_experts(arrived, pieces):
    rows, model_width = arrived.shape
    width = pieces[0].shape[2]
    anywhere = pl.BlockSpec(memory_space=pl.ANY)
    return pl.pallas_call(
        expert_kernel,
        name="experts",
        out_shape=shape((rows * model_width // LANES, LANES), BF16),
        in_specs=[pl.BlockSpec(memory_space=pltpu.VMEM)] + [anywhere] * len(pieces),
        out_specs=pl.BlockSpec(memory_space=pltpu.VMEM),
        scratch_shapes=[
            pltpu.VMEM((3, model_width, width), BF16),
            pltpu.VMEM((rows, width), BF16),
            pltpu.VMEM((rows * model_width // LANES, LANES), F32),
            pltpu.SemaphoreType.DMA((3, len(pieces))),
        ],
        cost_estimate=cost(6 * rows * model_width * width, 6 * model_width * width),
        compiler_params=vmem(20),
    )(arrived, *pieces)


def along_x(piece, step):
    size = lax.axis_size("x")
    return lax.ppermute(piece, "x", [(i, (i - step) % size) for i in range(size)])


def swapped(piece):
    return lax.ppermute(piece, "core", [(0, 1), (1, 0)])


def own_places():
    chips, cores = lax.axis_size("x"), lax.axis_size("core")
    chunk = jnp.arange(chips * cores, dtype=jnp.int32)
    chip = (chunk // cores + chips - lax.axis_index("x")) % chips
    return chip * cores + (chunk + lax.axis_index("core")) % cores


def body(
    hidden_in,
    queries,
    keys,
    values,
    log_decay,
    retention_gain,
    norm_gain,
    routes,
    route_weights,
    w_gate,
    w_up,
    w_down,
):
    tok_rows = hidden_in.shape[1]
    model_width = hidden_in.shape[2]
    head_count = log_decay.shape[2]
    head_dim = model_width // head_count
    wide = (tok_rows, model_width)
    plane, depth = lax.axis_size(PLANE), lax.axis_size("z")
    part_rows = head_count * head_dim // plane
    message = (plane, part_rows + LOG_ROWS, head_dim)

    half = head_dim // 2
    inverse = np.tile(10000.0 ** (-np.arange(half) / half), 2)


    def angle_table(rows, step):
        angles = np.arange(0, rows * step, step)[:, None] * inverse[None, :]
        return np.stack([np.cos(angles), np.sin(angles)]).astype(np.float32)

    turn = (
        lax.axis_index("z")[None],
        lax.axis_index(PLANE)[None],
        angle_table(lax.axis_size("z"), plane * tok_rows),
        angle_table(plane, tok_rows),
        angle_table(tok_rows, 1),
    )
    in_smem = pl.BlockSpec(memory_space=pltpu.SMEM)

    shards = (3,) + w_gate.shape[1:]
    any_space, in_vmem = pl.BlockSpec(memory_space=pl.ANY), pl.BlockSpec(memory_space=pltpu.VMEM)
    out_message, total, stacked = pl.pallas_call(
        summary_kernel,
        name="summary",
        out_shape=(
            shape(message, BF16),
            shape((head_count, tok_rows), F32),
            shape(shards, BF16),
        ),
        in_specs=[in_vmem] * 3 + [in_smem] * 2 + [in_vmem] * 3 + [any_space] * 3,
        out_specs=(in_vmem, in_vmem, any_space),
        scratch_shapes=[
            pltpu.VMEM(shards, BF16),
            pltpu.SemaphoreType.DMA((3,)),
            pltpu.SemaphoreType.DMA((3,)),
        ],
        cost_estimate=cost(70000000, 3200000),
    )(keys[0], values[0], log_decay[0].T, *turn, w_gate[0], w_up[0], w_down[0])
    summaries = exchange(out_message, PLANE)
    after, before = along_x(stacked, 1), along_x(stacked, -1)
    turned_queries, inside, fade = pl.pallas_call(
        inside_kernel,
        name="inside",
        out_shape=(shape(wide, BF16), shape(wide, F32), shape((tok_rows, tok_rows), F32)),
        in_specs=[in_vmem] * 4 + [in_smem] * 2 + [in_vmem] * 3,
        cost_estimate=cost(70000000, 2200000),
        compiler_params=vmem(8),
    )(queries[0], keys[0], values[0], total, *turn)
    sums = pl.pallas_call(
        plane_sum_kernel,
        name="plane_sum",
        out_shape=shape((depth,) + message[1:], BF16),
        cost_estimate=cost(500000, 600000),
        compiler_params=vmem(4),
    )(summaries)
    sums = exchange(sums, "z")
    own_other = swapped(stacked)
    entering = pl.pallas_call(
        entering_kernel,
        name="enter",
        out_shape=shape((plane, part_rows, head_dim), BF16),
        in_specs=[pl.BlockSpec(memory_space=pltpu.SMEM)]
        + [pl.BlockSpec(memory_space=pltpu.VMEM)] * 2,
        cost_estimate=cost(900000, 900000),
        compiler_params=vmem(4),
    )(lax.axis_index("z")[None], summaries, sums)
    state_in = exchange(entering, PLANE).reshape(model_width, head_dim)
    after_other, before_other = swapped(after), swapped(before)

    expert_count = lax.axis_size(OWNERS)
    top_count = routes.shape[2]
    capacity = (tok_rows * top_count * 5 + 4 * expert_count - 1) // (4 * expert_count)
    slot_count = expert_count * capacity
    route_rows = routes[0]
    expert_hits = (
        route_rows.reshape(tok_rows * top_count)[:, None]
        == jnp.arange(expert_count, dtype=jnp.int32)[None, :]
    ).astype(jnp.int32)
    earlier = jnp.cumsum(expert_hits, axis=0) - expert_hits
    slot_rank = jnp.sum(earlier * expert_hits, axis=1).reshape(tok_rows, top_count)
    destination = route_rows * capacity + slot_rank
    slot_lanes = jnp.arange(slot_count, dtype=jnp.int32)
    placing = jnp.any(destination[None, :, :] == slot_lanes[:, None, None], axis=2).astype(BF16)

    flat = (slot_count * model_width // LANES, LANES)
    places = own_places()
    residual, outgoing = pl.pallas_call(
        outgoing_kernel,
        name="outgoing",
        out_shape=(shape(wide, F32), shape(flat, BF16)),
        in_specs=[pl.BlockSpec(memory_space=pltpu.SMEM)]
        + [pl.BlockSpec(memory_space=pltpu.VMEM)] * 8,
        scratch_shapes=[
            pltpu.VMEM((head_count, tok_rows, head_dim), BF16),
            pltpu.VMEM(flat, F32),
        ],
        cost_estimate=cost(120000000, 3000000),
        compiler_params=vmem(10),
    )(
        places,
        state_in,
        turned_queries,
        inside,
        fade,
        hidden_in[0],
        retention_gain[None],
        norm_gain[None],
        placing,
    )
    packed = (expert_count, capacity * model_width // LANES, LANES)
    arrived = exchange(outgoing.reshape(packed), OWNERS).reshape(slot_count, model_width)
    cut = stacked.shape[1] // 2
    far = [along_x(after[:, :cut], 1), along_x(before[:, cut:], -1)]
    far_other = [swapped(piece) for piece in far]
    pieces = [stacked, own_other, after, after_other, *far, *far_other, before, before_other]
    expert_out = run_experts(arrived, pieces)
    returned = exchange(expert_out.reshape(packed), OWNERS).reshape(slot_count, model_width)
    picks = [
        (destination[:, index][:, None] == slot_lanes[None, :]).astype(BF16)
        for index in range(top_count)
    ]
    output = pl.pallas_call(
        combine_kernel,
        name="combine",
        out_shape=shape(wide, BF16),
        in_specs=[pl.BlockSpec(memory_space=pltpu.SMEM)]
        + [pl.BlockSpec(memory_space=pltpu.VMEM)] * 5,
        scratch_shapes=[pltpu.VMEM((head_count, tok_rows, head_dim), F32)],
        cost_estimate=cost(180000000, 2000000),
        compiler_params=vmem(8),
    )(places, returned, *picks, route_weights[0], residual)
    return output[None]


def solution(mesh):
    ctx, exp, dp = mesh.shape["ctx"], mesh.shape["exp"], mesh.shape["dp"]
    split = Mesh(
        mesh.devices.reshape(ctx // 2, 2, exp // 2, 2, dp), ("z", "ylo", "x", "core", "yhi")
    )
    tokens = P("yhi", CTX + EXP, None)
    experts = P(OWNERS, EXP, None)
    in_specs = (tokens,) * 5 + (P(), P()) + (tokens,) * 2 + (experts,) * 3
    return jax.shard_map(body, mesh=split, in_specs=in_specs, out_specs=tokens, check_vma=False)
```
